512 devices in a mesh: row: 32 (over y, z_hi, core), col: 16 (over x, z_lo).
Axes of the slice: x: 4, y: 8, z: 8 (z_hi: 2, z_lo: 4; z = z_hi * 4 + z_lo), core: 2. Of those that a mesh axis runs over, the one named last changes fastest.
Arguments:
- features: bfloat16 [32, 16, 128, 128], P('row', 'col'), may hold values from -6 to 6
- tiles: bfloat16 [32, 16, 128, 128, 128], P('row', 'col'), may hold values from -0.3984375 to 0.3984375
- tile_coords: int32 [32, 16, 128, 2], P('row', 'col'), may hold values from 0 to 31, as said below
- tile_count: int32 [32, 16], P('row', 'col'), may hold values from 1 to 128, as said below
- batch_mask: int32 [32, 16, 128], P('row', 'col'), may hold values 0 or 1
- history: bfloat16 [32, 16, 128, 256], P('row', 'col'), may hold values from 0 to 1.5
- weight_one: bfloat16 [128, 256], replicated, may hold values from -0.5 to 0.5
- bias_one: float32 [256], replicated, may hold values from -3 to 3
- weight_two: bfloat16 [256, 172], replicated, may hold values from -0.375 to 0.375
- bias_two: float32 [172], replicated, may hold values from -3 to 3
Outputs:
- new_history: bfloat16 [32, 16, 128, 256], P('row', 'col')
- logits: float32 [32, 16, 128, 172], P('row', 'col')
The draws below stay inside these ranges and needn't reach their ends.
Inputs may be any that keep to these rules, and one draw needn't show every extreme that they name: `tile_coords`: column 0 is below 16 and column 1 below 32; coordinates may repeat. `tile_count`: some device has all 128 slots live.
All inputs are finite; a program needn't handle non-finite values. No bound on the sum of `batch_mask` on one device may be relied on, other than what follows from the above.
Results may differ from the reference program's by a relative error of at most 0.024.
Values may be sent and summed in bfloat16 or wider, within the bound.
A program may use at most 64 MiB of HBM per device.

```python
import jax
import jax.numpy as jnp
from jax import lax

BLOCK = 128
F_IN = 128
HID = 256
CLASSES = 172
TILES_DEV = 128
N_ROW = 32
N_COL = 16


def draw_tile_coords(key, part):
    first_key, second_key = jax.random.split(jax.random.fold_in(key, 11))
    block_rows = jax.random.randint(first_key, (N_ROW, N_COL, TILES_DEV, 1), 0, N_COL)
    block_cols = jax.random.randint(second_key, (N_ROW, N_COL, TILES_DEV, 1), 0, N_ROW)
    return jnp.concatenate([block_rows, block_cols], axis=-1).astype(jnp.int32)


def draw_tile_count(key, part):
    first_key, second_key, third_key = jax.random.split(jax.random.fold_in(key, 23), 3)
    first_draw = jax.random.randint(first_key, (N_ROW * N_COL,), 1, TILES_DEV + 1)
    second_draw = jax.random.randint(second_key, (N_ROW * N_COL,), 1, TILES_DEV + 1)
    fullest = jax.random.randint(third_key, (), 0, N_ROW * N_COL)
    counts = jnp.minimum(first_draw, second_draw).at[fullest].set(TILES_DEV)
    return counts.reshape(N_ROW, N_COL).astype(jnp.int32)


def with_ends(entries, rng, least, largest):
    index_at = [jax.random.randint(jax.random.fold_in(rng, axis), (), 0, length) for axis, length in enumerate(entries.shape)]
    main_axis = entries.shape.index(max(entries.shape))
    next_to = index_at[:main_axis] + [(index_at[main_axis] + 1) % entries.shape[main_axis]] + index_at[main_axis + 1:]
    return entries.at[tuple(index_at)].set(least).at[tuple(next_to)].set(largest)


def level_of(rng, shape, cuts, least, high):
    factor_of, own = 1.0, jax.random.fold_in(rng, 6)
    for dim, parts in cuts:
        heights = jnp.exp(jax.random.uniform(jax.random.fold_in(own, dim), (parts,), jnp.float32, least / len(cuts), high / len(cuts)))
        factor_of = factor_of * jnp.repeat(heights, shape[dim] // parts).reshape([-1 if axis == dim else 1 for axis in range(len(shape))])
    return factor_of


def gaussian(stream_key, extent, width, limit, cuts=(), kind=jnp.bfloat16):
    loudness = level_of(stream_key, extent, cuts, -0.22, 0.18) if cuts else 1.0
    array = jax.random.normal(stream_key, extent, jnp.float32) * width * loudness
    return jnp.minimum(jnp.maximum(array, -limit), limit).astype(kind)


def setup_inputs(seed: int = 0) -> dict:
    splits = jax.random.split(jax.random.key(seed), 11)
    return {
        "features": gaussian(splits[0], (N_ROW, N_COL, BLOCK, F_IN), 1.0, 6.0, ((0, 32), (1, 16))),
        "tiles": gaussian(splits[1], (N_ROW, N_COL, TILES_DEV, BLOCK, BLOCK), 0.05, 0.3984375, ((0, 32), (1, 16))),
        "tile_coords": draw_tile_coords(jax.random.fold_in(splits[10], 71), 0),
        "tile_count": draw_tile_count(jax.random.fold_in(splits[10], 71), 0),
        "batch_mask": with_ends((jax.random.randint(splits[4], (N_ROW, N_COL, BLOCK), 0, 2) < 1).astype(jnp.int32), jax.random.fold_in(splits[4], 1), 0, 1),
        "history": jnp.clip(1.5 * jax.random.uniform(splits[5], (N_ROW, N_COL, BLOCK, HID), jnp.float32) ** level_of(splits[5], (N_ROW, N_COL, BLOCK, HID), ((0, 32), (1, 16)), -0.2, 0.2), 0.0, 1.5).astype(jnp.bfloat16),
        "weight_one": gaussian(splits[6], (F_IN, HID), F_IN ** -0.5, 0.5),
        "bias_one": gaussian(splits[7], (HID,), 0.5, 3.0, (), jnp.float32),
        "weight_two": gaussian(splits[8], (HID, CLASSES), HID ** -0.5, 0.375),
        "bias_two": gaussian(splits[9], (CLASSES,), 0.5, 3.0, (), jnp.float32),
    }


def partial_sums(node_data, tiles, tile_coords, tile_count):
    row_blocks = node_data.shape[1]
    slots = tiles.shape[2]
    col_ids = jnp.arange(row_blocks, dtype=jnp.int32)

    def one_device(tile_set, coord_set, live_total, col_index):
        sources = node_data[coord_set[:, 1], col_index].astype(jnp.float32)
        products = jnp.einsum("tij,tjf->tif", tile_set.astype(jnp.float32), sources, precision=lax.Precision.HIGHEST)
        alive = (jnp.arange(slots, dtype=jnp.int32) < live_total).astype(jnp.float32)
        placing = (coord_set[:, 0][None, :] == col_ids[:, None]).astype(jnp.float32) * alive[None, :]
        summed = jnp.einsum("rt,tif->rif", placing, products, precision=lax.Precision.HIGHEST)
        rounded = lax.optimization_barrier(summed.astype(jnp.bfloat16))
        return rounded.astype(jnp.float32)

    def one_row(packed):
        tile_row, coord_row, count_row = packed
        pieces = jax.vmap(one_device)(tile_row, coord_row, count_row, col_ids)
        return jnp.sum(pieces, axis=0)

    return lax.map(one_row, (tiles, tile_coords, tile_count))


def reference(features, tiles, tile_coords, tile_count, batch_mask, history, weight_one, bias_one, weight_two, bias_two):
    agg_one = (features.astype(jnp.float32) + partial_sums(features, tiles, tile_coords, tile_count)).astype(jnp.bfloat16)
    pre_one = jnp.einsum("rcif,fh->rcih", agg_one.astype(jnp.float32), weight_one.astype(jnp.float32), precision=lax.Precision.HIGHEST)
    hidden = jax.nn.relu(pre_one + bias_one).astype(jnp.bfloat16)
    new_history = jnp.where(batch_mask[..., None] == 1, hidden, history)
    pre_two = jnp.einsum("rcih,hk->rcik", new_history.astype(jnp.float32), weight_two.astype(jnp.float32), precision=lax.Precision.HIGHEST)
    projected = lax.optimization_barrier(pre_two.astype(jnp.bfloat16))
    logits = projected.astype(jnp.float32) + partial_sums(projected, tiles, tile_coords, tile_count) + bias_two
    return new_history, logits
```

```python
import jax
import jax.numpy as jnp
from jax import lax
from jax.sharding import PartitionSpec as P


def joined_along(tiles, dim):
    tiles = jnp.moveaxis(tiles, 0, dim)
    lengths = tiles.shape
    return tiles.reshape(*lengths[:dim], lengths[dim] * lengths[dim + 1], *lengths[dim + 2 :])


def copy_for_each(shard, axis):
    copies = jnp.broadcast_to(shard, (lax.axis_size(axis), *shard.shape))
    return lax.all_to_all(copies, axis, split_axis=0, concat_axis=0, tiled=True)


def collect(shard, axis, dim):
    return joined_along(copy_for_each(shard, axis), dim)


def in_blocks(shard, dim, size):
    lengths = shard.shape
    tiles = shard.reshape(*lengths[:dim], size, lengths[dim] // size, *lengths[dim + 1 :])
    return jnp.moveaxis(tiles, dim, 0)


def sent_and_summed(shard, axis, dim):
    tiles = in_blocks(shard, dim, lax.axis_size(axis))
    arrived = lax.all_to_all(tiles, axis, split_axis=0, concat_axis=0, tiled=True)
    return arrived.astype(jnp.float32).sum(axis=0)


def tile_products(gathered, tiles, coords, live_total, group_size, group_count):
    row_blocks = lax.axis_size("col")
    block_ids = jnp.arange(row_blocks, dtype=jnp.int32)

    def one_group(step, running):
        first = step * group_size
        tile_group = lax.dynamic_slice_in_dim(tiles, first, group_size, 0)
        coord_group = lax.dynamic_slice_in_dim(coords, first, group_size, 0)
        sources = jnp.take(gathered, coord_group[:, 1], axis=0)
        products = jnp.einsum(
            "gij,gjf->gif", tile_group, sources, preferred_element_type=jnp.float32
        )
        slot_ids = first + jnp.arange(group_size, dtype=jnp.int32)
        alive = (slot_ids < live_total).astype(jnp.float32)
        placing = (coord_group[:, 0][None, :] == block_ids[:, None]).astype(jnp.float32) * alive[
            None, :
        ]
        return running + jnp.einsum(
            "rg,gif->rif", placing, products, precision=lax.Precision.HIGHEST
        )

    start_total = jnp.zeros((row_blocks, gathered.shape[1], gathered.shape[2]), jnp.float32)
    return lax.fori_loop(0, group_count, one_group, start_total)


def on_device(
    features,
    tiles,
    tile_coords,
    tile_count,
    batch_mask,
    history,
    weight_one,
    bias_one,
    weight_two,
    bias_two,
):
    tile_set = tiles[0, 0]
    coord_set = tile_coords[0, 0]
    live_total = tile_count[0, 0]
    slots = tile_set.shape[0]
    group_size = 16
    group_count = (live_total + group_size - 1) // group_size
    gathered_input = lax.all_gather(features[0, 0], "row", axis=0)
    summed_one = tile_products(
        gathered_input, tile_set, coord_set, live_total, group_size, group_count
    )
    owned_one = lax.psum_scatter(
        summed_one.astype(jnp.bfloat16).astype(jnp.float32), "col", scatter_dimension=0
    )
    agg_one = (features[0, 0].astype(jnp.float32) + owned_one).astype(jnp.bfloat16)
    pre_one = jnp.dot(agg_one, weight_one, preferred_element_type=jnp.float32) + bias_one
    hidden = jax.nn.relu(pre_one).astype(jnp.bfloat16)
    pushed = jnp.where(batch_mask[0, 0][:, None] == 1, hidden, history[0, 0])
    projected = jnp.dot(pushed, weight_two, preferred_element_type=jnp.float32).astype(jnp.bfloat16)
    gathered_proj = lax.all_gather(projected, "row", axis=0)
    summed_two = tile_products(
        gathered_proj, tile_set, coord_set, live_total, group_size, group_count
    )
    owned_two = lax.psum_scatter(
        summed_two.astype(jnp.bfloat16).astype(jnp.float32), "col", scatter_dimension=0
    )
    scores = projected.astype(jnp.float32) + owned_two + bias_two
    return (pushed[None, None], scores[None, None])


def solution(mesh):
    return jax.shard_map(
        on_device,
        mesh=mesh,
        in_specs=(
            P("row", "col", None, None),
            P("row", "col", None, None, None),
            P("row", "col", None, None),
            P("row", "col"),
            P("row", "col", None),
            P("row", "col", None, None),
            P(),
            P(),
            P(),
            P(),
        ),
        out_specs=(P("row", "col", None, None), P("row", "col", None, None)),
        check_vma=False,
    )
```

```python
import functools

import jax
import jax.numpy as jnp
from jax import lax
from jax.experimental import pallas as pl
from jax.experimental.pallas import tpu as pltpu
from jax.sharding import PartitionSpec as P

MESH_ID = pl.DeviceIdType.MESH


def exchange_kernel(axis, other_axis, n, spread, src_ref, out_ref, send_sem, recv_sem):
    me = lax.axis_index(axis)
    other = lax.axis_index(other_axis)

    def device(k):
        return (k, other) if axis == "row" else (other, k)

    def outgoing(k):
        source = src_ref.at[k] if spread else src_ref
        return pltpu.make_async_remote_copy(
            src_ref=source,
            dst_ref=out_ref.at[me],
            send_sem=send_sem.at[k],
            recv_sem=recv_sem.at[me],
            device_id=device(k),
            device_id_type=MESH_ID,
        )

    def incoming(k):
        source = src_ref.at[k] if spread else src_ref
        return pltpu.make_async_remote_copy(
            src_ref=source,
            dst_ref=out_ref.at[k],
            send_sem=send_sem.at[k],
            recv_sem=recv_sem.at[k],
            device_id=device(k),
            device_id_type=MESH_ID,
        )

    barrier = pltpu.get_barrier_semaphore()

    def greet(step, carry):
        k = lax.rem(me + step, n)
        pl.semaphore_signal(barrier, 1, device_id=device(k), device_id_type=MESH_ID)
        return carry

    lax.fori_loop(1, n, greet, 0)
    pl.semaphore_wait(barrier, n - 1)

    def send(step, carry):
        outgoing(lax.rem(me + step, n)).start()
        return carry

    lax.fori_loop(1, n, send, 0)
    out_ref[me] = src_ref[me] if spread else src_ref[...]

    def finish(step, carry):
        k = lax.rem(me + step, n)
        outgoing(k).wait_send()
        incoming(lax.rem(me + n - step, n)).wait_recv()
        return carry

    lax.fori_loop(1, n, finish, 0)


def exchange(block, axis, spread, tag):
    other_axis = "col" if axis == "row" else "row"
    n = lax.axis_size(axis)
    shape = block.shape[1:] if spread else block.shape
    vmem = pl.BlockSpec(memory_space=pltpu.VMEM)
    return pl.pallas_call(
        functools.partial(exchange_kernel, axis, other_axis, n, spread),
        out_shape=jax.ShapeDtypeStruct((n, *shape), block.dtype),
        in_specs=[vmem],
        out_specs=vmem,
        scratch_shapes=[pltpu.SemaphoreType.DMA((n,)), pltpu.SemaphoreType.DMA((n,))],
        compiler_params=pltpu.CompilerParams(collective_id=tag, has_side_effects=True),
    )(block)


def joined_along(tiles, dim):
    tiles = jnp.moveaxis(tiles, 0, dim)
    lengths = tiles.shape
    return tiles.reshape(*lengths[:dim], lengths[dim] * lengths[dim + 1], *lengths[dim + 2 :])


def copy_for_each(shard, axis):
    copies = jnp.broadcast_to(shard, (lax.axis_size(axis), *shard.shape))
    return lax.all_to_all(copies, axis, split_axis=0, concat_axis=0, tiled=True)


def collect(shard, axis, dim):
    return joined_along(copy_for_each(shard, axis), dim)


def in_blocks(shard, dim, size):
    lengths = shard.shape
    tiles = shard.reshape(*lengths[:dim], size, lengths[dim] // size, *lengths[dim + 1 :])
    return jnp.moveaxis(tiles, dim, 0)


def sent_and_summed(shard, axis, dim):
    tiles = in_blocks(shard, dim, lax.axis_size(axis))
    arrived = lax.all_to_all(tiles, axis, split_axis=0, concat_axis=0, tiled=True)
    return arrived.astype(jnp.float32).sum(axis=0)


def tile_products(gathered, tiles, coords, live_total, group_size, group_count):
    row_blocks = lax.axis_size("col")
    block_ids = jnp.arange(row_blocks, dtype=jnp.int32)

    def one_group(step, running):
        first = step * group_size
        tile_group = lax.dynamic_slice_in_dim(tiles, first, group_size, 0)
        coord_group = lax.dynamic_slice_in_dim(coords, first, group_size, 0)
        sources = jnp.take(gathered, coord_group[:, 1], axis=0)
        products = jnp.einsum(
            "gij,gjf->gif", tile_group, sources, preferred_element_type=jnp.float32
        )
        slot_ids = first + jnp.arange(group_size, dtype=jnp.int32)
        alive = (slot_ids < live_total).astype(jnp.float32)
        placing = (coord_group[:, 0][None, :] == block_ids[:, None]).astype(jnp.float32) * alive[
            None, :
        ]
        return running + jnp.einsum(
            "rg,gif->rif", placing, products, precision=lax.Precision.HIGHEST
        )

    start_total = jnp.zeros((row_blocks, gathered.shape[1], gathered.shape[2]), jnp.float32)
    return lax.fori_loop(0, group_count, one_group, start_total)


def on_device(
    features,
    tiles,
    tile_coords,
    tile_count,
    batch_mask,
    history,
    weight_one,
    bias_one,
    weight_two,
    bias_two,
):
    tile_set = tiles[0, 0]
    coord_set = tile_coords[0, 0]
    live_total = tile_count[0, 0]
    slots = tile_set.shape[0]
    group_size = 16
    group_count = (live_total + group_size - 1) // group_size
    gathered_input = exchange(features[0, 0], "row", False, 0)
    summed_one = tile_products(
        gathered_input, tile_set, coord_set, live_total, group_size, group_count
    )
    owned_one = exchange(summed_one.astype(jnp.bfloat16), "col", True, 1)
    owned_one = owned_one.astype(jnp.float32).sum(axis=0)
    agg_one = (features[0, 0].astype(jnp.float32) + owned_one).astype(jnp.bfloat16)
    pre_one = jnp.dot(agg_one, weight_one, preferred_element_type=jnp.float32) + bias_one
    hidden = jax.nn.relu(pre_one).astype(jnp.bfloat16)
    pushed = jnp.where(batch_mask[0, 0][:, None] == 1, hidden, history[0, 0])
    projected = jnp.dot(pushed, weight_two, preferred_element_type=jnp.float32).astype(jnp.bfloat16)
    gathered_proj = exchange(projected, "row", False, 2)
    summed_two = tile_products(
        gathered_proj, tile_set, coord_set, live_total, group_size, group_count
    )
    owned_two = exchange(summed_two.astype(jnp.bfloat16), "col", True, 3)
    owned_two = owned_two.astype(jnp.float32).sum(axis=0)
    scores = projected.astype(jnp.float32) + owned_two + bias_two
    return (pushed[None, None], scores[None, None])


def solution(mesh):
    return jax.shard_map(
        on_device,
        mesh=mesh,
        in_specs=(
            P("row", "col", None, None),
            P("row", "col", None, None, None),
            P("row", "col", None, None),
            P("row", "col"),
            P("row", "col", None),
            P("row", "col", None, None),
            P(),
            P(),
            P(),
            P(),
        ),
        out_specs=(P("row", "col", None, None), P("row", "col", None, None)),
        check_vma=False,
    )
```

```python
import functools

import jax
import jax.numpy as jnp
from jax import lax
from jax.experimental import pallas as pl
from jax.experimental.pallas import tpu as pltpu
from jax.sharding import PartitionSpec as P

MESH_ID = pl.DeviceIdType.MESH


def exchange_kernel(axis, other_axis, n, spread, src_ref, out_ref, send_sem, recv_sem):
    me = lax.axis_index(axis)
    other = lax.axis_index(other_axis)

    def device(k):
        return (k, other) if axis == "row" else (other, k)

    def outgoing(k):
        source = src_ref.at[k] if spread else src_ref
        return pltpu.make_async_remote_copy(
            src_ref=source,
            dst_ref=out_ref.at[me],
            send_sem=send_sem.at[k],
            recv_sem=recv_sem.at[me],
            device_id=device(k),
            device_id_type=MESH_ID,
        )

    def incoming(k):
        source = src_ref.at[k] if spread else src_ref
        return pltpu.make_async_remote_copy(
            src_ref=source,
            dst_ref=out_ref.at[k],
            send_sem=send_sem.at[k],
            recv_sem=recv_sem.at[k],
            device_id=device(k),
            device_id_type=MESH_ID,
        )

    barrier = pltpu.get_barrier_semaphore()

    def greet(step, carry):
        k = lax.rem(me + step, n)
        pl.semaphore_signal(barrier, 1, device_id=device(k), device_id_type=MESH_ID)
        return carry

    lax.fori_loop(1, n, greet, 0)
    pl.semaphore_wait(barrier, n - 1)

    def send(step, carry):
        outgoing(lax.rem(me + step, n)).start()
        return carry

    lax.fori_loop(1, n, send, 0)
    out_ref[me] = src_ref[me] if spread else src_ref[...]

    def finish(step, carry):
        k = lax.rem(me + step, n)
        outgoing(k).wait_send()
        incoming(lax.rem(me + n - step, n)).wait_recv()
        return carry

    lax.fori_loop(1, n, finish, 0)


def exchange(block, axis, spread, tag):
    other_axis = "col" if axis == "row" else "row"
    n = lax.axis_size(axis)
    shape = block.shape[1:] if spread else block.shape
    vmem = pl.BlockSpec(memory_space=pltpu.VMEM)
    return pl.pallas_call(
        functools.partial(exchange_kernel, axis, other_axis, n, spread),
        out_shape=jax.ShapeDtypeStruct((n, *shape), block.dtype),
        in_specs=[vmem],
        out_specs=vmem,
        scratch_shapes=[pltpu.SemaphoreType.DMA((n,)), pltpu.SemaphoreType.DMA((n,))],
        compiler_params=pltpu.CompilerParams(collective_id=tag, has_side_effects=True),
    )(block)


def joined_along(tiles, dim):
    tiles = jnp.moveaxis(tiles, 0, dim)
    lengths = tiles.shape
    return tiles.reshape(*lengths[:dim], lengths[dim] * lengths[dim + 1], *lengths[dim + 2 :])


def copy_for_each(shard, axis):
    copies = jnp.broadcast_to(shard, (lax.axis_size(axis), *shard.shape))
    return lax.all_to_all(copies, axis, split_axis=0, concat_axis=0, tiled=True)


def collect(shard, axis, dim):
    return joined_along(copy_for_each(shard, axis), dim)


def in_blocks(shard, dim, size):
    lengths = shard.shape
    tiles = shard.reshape(*lengths[:dim], size, lengths[dim] // size, *lengths[dim + 1 :])
    return jnp.moveaxis(tiles, dim, 0)


def sent_and_summed(shard, axis, dim):
    tiles = in_blocks(shard, dim, lax.axis_size(axis))
    arrived = lax.all_to_all(tiles, axis, split_axis=0, concat_axis=0, tiled=True)
    return arrived.astype(jnp.float32).sum(axis=0)


def products_kernel(group, coords_ref, count_ref, tiles_ref, gathered_ref, out_ref, total_ref):
    step = pl.program_id(0)

    @pl.when(step == 0)
    def _():
        total_ref[...] = jnp.zeros_like(total_ref)

    live = count_ref[0]

    def one_tile(j, carry):
        slot = step * group + j

        @pl.when(slot < live)
        def _():
            target = coords_ref[2 * slot]
            source = coords_ref[2 * slot + 1]
            total_ref[target] += jnp.dot(
                tiles_ref[j], gathered_ref[source], preferred_element_type=jnp.float32
            )

        return carry

    @pl.when(step * group < live)
    def _():
        lax.fori_loop(0, group, one_tile, 0, unroll=True)

    @pl.when(step == pl.num_programs(0) - 1)
    def _():
        out_ref[...] = total_ref[...].astype(out_ref.dtype)


def tile_products(gathered, tiles, coords, live_total, group=16):
    row_blocks = lax.axis_size("col")
    slots, size, _ = tiles.shape
    width = gathered.shape[-1]
    steps = slots // group

    def tile_map(step, coords_ref, count_ref):
        return (jnp.minimum(step, (count_ref[0] - 1) // group), 0, 0)

    def whole(step, coords_ref, count_ref):
        return (0, 0, 0)

    grid_spec = pltpu.PrefetchScalarGridSpec(
        num_scalar_prefetch=2,
        grid=(steps,),
        in_specs=[
            pl.BlockSpec((group, size, size), tile_map),
            pl.BlockSpec(gathered.shape, whole),
        ],
        out_specs=pl.BlockSpec((row_blocks, size, width), whole),
        scratch_shapes=[pltpu.VMEM((row_blocks, size, width), jnp.float32)],
    )
    return pl.pallas_call(
        functools.partial(products_kernel, group),
        grid_spec=grid_spec,
        out_shape=jax.ShapeDtypeStruct((row_blocks, size, width), jnp.bfloat16),
    )(coords.reshape(-1), live_total.reshape(1), tiles, gathered)


def on_device(
    features,
    tiles,
    tile_coords,
    tile_count,
    batch_mask,
    history,
    weight_one,
    bias_one,
    weight_two,
    bias_two,
):
    tile_set = tiles[0, 0]
    coord_set = tile_coords[0, 0]
    live_total = tile_count[0, 0]
    gathered_input = exchange(features[0, 0], "row", False, 0)
    summed_one = tile_products(gathered_input, tile_set, coord_set, live_total)
    owned_one = exchange(summed_one, "col", True, 1)
    owned_one = owned_one.astype(jnp.float32).sum(axis=0)
    agg_one = (features[0, 0].astype(jnp.float32) + owned_one).astype(jnp.bfloat16)
    pre_one = jnp.dot(agg_one, weight_one, preferred_element_type=jnp.float32) + bias_one
    hidden = jax.nn.relu(pre_one).astype(jnp.bfloat16)
    pushed = jnp.where(batch_mask[0, 0][:, None] == 1, hidden, history[0, 0])
    projected = jnp.dot(pushed, weight_two, preferred_element_type=jnp.float32).astype(jnp.bfloat16)
    gathered_proj = exchange(projected, "row", False, 2)
    summed_two = tile_products(gathered_proj, tile_set, coord_set, live_total)
    owned_two = exchange(summed_two, "col", True, 3)
    owned_two = owned_two.astype(jnp.float32).sum(axis=0)
    scores = projected.astype(jnp.float32) + owned_two + bias_two
    return (pushed[None, None], scores[None, None])


def solution(mesh):
    return jax.shard_map(
        on_device,
        mesh=mesh,
        in_specs=(
            P("row", "col", None, None),
            P("row", "col", None, None, None),
            P("row", "col", None, None),
            P("row", "col"),
            P("row", "col", None),
            P("row", "col", None, None),
            P(),
            P(),
            P(),
            P(),
        ),
        out_specs=(P("row", "col", None, None), P("row", "col", None, None)),
        check_vma=False,
    )
```

```python
import functools

import jax
import jax.numpy as jnp
from jax import lax
from jax.experimental import pallas as pl
from jax.experimental.pallas import tpu as pltpu
from jax.sharding import PartitionSpec as P

MESH_ID = pl.DeviceIdType.MESH


def exchange_kernel(axis, other_axis, n, spread, src_ref, out_ref, send_sem, recv_sem):
    me = lax.axis_index(axis)
    other = lax.axis_index(other_axis)

    def device(k):
        return (k, other) if axis == "row" else (other, k)

    def outgoing(k):
        source = src_ref.at[k] if spread else src_ref
        return pltpu.make_async_remote_copy(
            src_ref=source,
            dst_ref=out_ref.at[me],
            send_sem=send_sem.at[k],
            recv_sem=recv_sem.at[me],
            device_id=device(k),
            device_id_type=MESH_ID,
        )

    def incoming(k):
        source = src_ref.at[k] if spread else src_ref
        return pltpu.make_async_remote_copy(
            src_ref=source,
            dst_ref=out_ref.at[k],
            send_sem=send_sem.at[k],
            recv_sem=recv_sem.at[k],
            device_id=device(k),
            device_id_type=MESH_ID,
        )

    barrier = pltpu.get_barrier_semaphore()

    def greet(step, carry):
        k = lax.rem(me + step, n)
        pl.semaphore_signal(barrier, 1, device_id=device(k), device_id_type=MESH_ID)
        return carry

    lax.fori_loop(1, n, greet, 0)
    pl.semaphore_wait(barrier, n - 1)

    def send(step, carry):
        outgoing(lax.rem(me + step, n)).start()
        return carry

    lax.fori_loop(1, n, send, 0)
    out_ref[me] = src_ref[me] if spread else src_ref[...]

    def finish(step, carry):
        k = lax.rem(me + step, n)
        outgoing(k).wait_send()
        incoming(lax.rem(me + n - step, n)).wait_recv()
        return carry

    lax.fori_loop(1, n, finish, 0)


def exchange(block, axis, spread, tag):
    other_axis = "col" if axis == "row" else "row"
    n = lax.axis_size(axis)
    shape = block.shape[1:] if spread else block.shape
    vmem = pl.BlockSpec(memory_space=pltpu.VMEM)
    return pl.pallas_call(
        functools.partial(exchange_kernel, axis, other_axis, n, spread),
        out_shape=jax.ShapeDtypeStruct((n, *shape), block.dtype),
        in_specs=[vmem],
        out_specs=vmem,
        scratch_shapes=[pltpu.SemaphoreType.DMA((n,)), pltpu.SemaphoreType.DMA((n,))],
        compiler_params=pltpu.CompilerParams(collective_id=tag, has_side_effects=True),
    )(block)


def joined_along(tiles, dim):
    tiles = jnp.moveaxis(tiles, 0, dim)
    lengths = tiles.shape
    return tiles.reshape(*lengths[:dim], lengths[dim] * lengths[dim + 1], *lengths[dim + 2 :])


def copy_for_each(shard, axis):
    copies = jnp.broadcast_to(shard, (lax.axis_size(axis), *shard.shape))
    return lax.all_to_all(copies, axis, split_axis=0, concat_axis=0, tiled=True)


def collect(shard, axis, dim):
    return joined_along(copy_for_each(shard, axis), dim)


def in_blocks(shard, dim, size):
    lengths = shard.shape
    tiles = shard.reshape(*lengths[:dim], size, lengths[dim] // size, *lengths[dim + 1 :])
    return jnp.moveaxis(tiles, dim, 0)


def sent_and_summed(shard, axis, dim):
    tiles = in_blocks(shard, dim, lax.axis_size(axis))
    arrived = lax.all_to_all(tiles, axis, split_axis=0, concat_axis=0, tiled=True)
    return arrived.astype(jnp.float32).sum(axis=0)


def products_kernel(group, coords_ref, count_ref, tiles_ref, gathered_ref, out_ref, total_ref):
    step = pl.program_id(0)

    @pl.when(step == 0)
    def _():
        total_ref[...] = jnp.zeros_like(total_ref)

    live = count_ref[0]

    def one_tile(j, carry):
        slot = step * group + j

        @pl.when(slot < live)
        def _():
            target = coords_ref[2 * slot]
            source = coords_ref[2 * slot + 1]
            total_ref[target] += jnp.dot(
                tiles_ref[j], gathered_ref[source], preferred_element_type=jnp.float32
            )

        return carry

    @pl.when(step * group < live)
    def _():
        lax.fori_loop(0, group, one_tile, 0, unroll=True)

    @pl.when(step == pl.num_programs(0) - 1)
    def _():
        out_ref[...] = total_ref[...].astype(out_ref.dtype)


def tile_products(gathered, tiles, coords, live_total, group=16):
    row_blocks = lax.axis_size("col")
    slots, size, _ = tiles.shape
    width = gathered.shape[-1]
    steps = slots // group

    def tile_map(step, coords_ref, count_ref):
        return (jnp.minimum(step, (count_ref[0] - 1) // group), 0, 0)

    def whole(step, coords_ref, count_ref):
        return (0, 0, 0)

    grid_spec = pltpu.PrefetchScalarGridSpec(
        num_scalar_prefetch=2,
        grid=(steps,),
        in_specs=[
            pl.BlockSpec((group, size, size), tile_map),
            pl.BlockSpec(gathered.shape, whole),
        ],
        out_specs=pl.BlockSpec((row_blocks, size, width), whole),
        scratch_shapes=[pltpu.VMEM((row_blocks, size, width), jnp.float32)],
    )
    return pl.pallas_call(
        functools.partial(products_kernel, group),
        grid_spec=grid_spec,
        out_shape=jax.ShapeDtypeStruct((row_blocks, size, width), jnp.bfloat16),
    )(coords.reshape(-1), live_total.reshape(1), tiles, gathered)


def on_device(
    features,
    tiles,
    tile_coords,
    tile_count,
    batch_mask,
    history,
    weight_one,
    bias_one,
    weight_two,
    bias_two,
):
    tile_set = tiles[0, 0]
    coord_set = tile_coords[0, 0]
    live_total = tile_count[0, 0]
    gathered_input = exchange(features[0, 0], "row", False, 0)
    summed_one = tile_products(gathered_input, tile_set, coord_set, live_total)
    owned_one = exchange(summed_one, "col", True, 1)
    owned_one = owned_one.astype(jnp.float32).sum(axis=0)
    agg_one = (features[0, 0].astype(jnp.float32) + owned_one).astype(jnp.bfloat16)
    pre_one = jnp.dot(agg_one, weight_one, preferred_element_type=jnp.float32) + bias_one
    hidden = jax.nn.relu(pre_one).astype(jnp.bfloat16)
    pushed = jnp.where(batch_mask[0, 0][:, None] == 1, hidden, history[0, 0])
    projected = jnp.dot(pushed, weight_two, preferred_element_type=jnp.float32).astype(jnp.bfloat16)
    nodes, classes = projected.shape
    dense = projected.reshape(classes, nodes)
    gathered_proj = exchange(dense, "row", False, 2).reshape(-1, nodes, classes)
    summed_two = tile_products(gathered_proj, tile_set, coord_set, live_total)
    dense_two = summed_two.reshape(summed_two.shape[0], classes, nodes)
    owned_two = exchange(dense_two, "col", True, 3).astype(jnp.float32).sum(axis=0)
    owned_two = owned_two.reshape(nodes, classes)
    scores = projected.astype(jnp.float32) + owned_two + bias_two
    return (pushed[None, None], scores[None, None])


def solution(mesh):
    return jax.shard_map(
        on_device,
        mesh=mesh,
        in_specs=(
            P("row", "col", None, None),
            P("row", "col", None, None, None),
            P("row", "col", None, None),
            P("row", "col"),
            P("row", "col", None),
            P("row", "col", None, None),
            P(),
            P(),
            P(),
            P(),
        ),
        out_specs=(P("row", "col", None, None), P("row", "col", None, None)),
        check_vma=False,
    )
```

```python
import functools

import jax
import jax.numpy as jnp
from jax import lax
from jax.experimental import pallas as pl
from jax.experimental.pallas import tpu as pltpu
from jax.sharding import PartitionSpec as P

MESH_ID = pl.DeviceIdType.MESH


def exchange_kernel(axis, other_axis, n, spread, src_ref, out_ref, send_sem, recv_sem):
    me = lax.axis_index(axis)
    other = lax.axis_index(other_axis)

    def device(k):
        return (k, other) if axis == "row" else (other, k)

    def outgoing(k):
        source = src_ref.at[k] if spread else src_ref
        return pltpu.make_async_remote_copy(
            src_ref=source,
            dst_ref=out_ref.at[me],
            send_sem=send_sem.at[k],
            recv_sem=recv_sem.at[me],
            device_id=device(k),
            device_id_type=MESH_ID,
        )

    def incoming(k):
        source = src_ref.at[k] if spread else src_ref
        return pltpu.make_async_remote_copy(
            src_ref=source,
            dst_ref=out_ref.at[k],
            send_sem=send_sem.at[k],
            recv_sem=recv_sem.at[k],
            device_id=device(k),
            device_id_type=MESH_ID,
        )

    barrier = pltpu.get_barrier_semaphore()

    def greet(step, carry):
        k = lax.rem(me + step, n)
        pl.semaphore_signal(barrier, 1, device_id=device(k), device_id_type=MESH_ID)
        return carry

    lax.fori_loop(1, n, greet, 0)
    pl.semaphore_wait(barrier, n - 1)

    def send(step, carry):
        outgoing(lax.rem(me + step, n)).start()
        return carry

    lax.fori_loop(1, n, send, 0)
    out_ref[me] = src_ref[me] if spread else src_ref[...]

    def finish(step, carry):
        k = lax.rem(me + step, n)
        outgoing(k).wait_send()
        incoming(lax.rem(me + n - step, n)).wait_recv()
        return carry

    lax.fori_loop(1, n, finish, 0)


def exchange(block, axis, spread, tag):
    other_axis = "col" if axis == "row" else "row"
    n = lax.axis_size(axis)
    shape = block.shape[1:] if spread else block.shape
    vmem = pl.BlockSpec(memory_space=pltpu.VMEM)
    return pl.pallas_call(
        functools.partial(exchange_kernel, axis, other_axis, n, spread),
        out_shape=jax.ShapeDtypeStruct((n, *shape), block.dtype),
        in_specs=[vmem],
        out_specs=vmem,
        scratch_shapes=[pltpu.SemaphoreType.DMA((n,)), pltpu.SemaphoreType.DMA((n,))],
        compiler_params=pltpu.CompilerParams(collective_id=tag, has_side_effects=True),
    )(block)


def joined_along(tiles, dim):
    tiles = jnp.moveaxis(tiles, 0, dim)
    lengths = tiles.shape
    return tiles.reshape(*lengths[:dim], lengths[dim] * lengths[dim + 1], *lengths[dim + 2 :])


def copy_for_each(shard, axis):
    copies = jnp.broadcast_to(shard, (lax.axis_size(axis), *shard.shape))
    return lax.all_to_all(copies, axis, split_axis=0, concat_axis=0, tiled=True)


def collect(shard, axis, dim):
    return joined_along(copy_for_each(shard, axis), dim)


def in_blocks(shard, dim, size):
    lengths = shard.shape
    tiles = shard.reshape(*lengths[:dim], size, lengths[dim] // size, *lengths[dim + 1 :])
    return jnp.moveaxis(tiles, dim, 0)


def sent_and_summed(shard, axis, dim):
    tiles = in_blocks(shard, dim, lax.axis_size(axis))
    arrived = lax.all_to_all(tiles, axis, split_axis=0, concat_axis=0, tiled=True)
    return arrived.astype(jnp.float32).sum(axis=0)


def products_kernel(group, flipped, coords_ref, count_ref, tiles_ref, gathered_ref, out_ref, total_ref):
    step = pl.program_id(0)

    @pl.when(step == 0)
    def _():
        total_ref[...] = jnp.zeros_like(total_ref)

    live = count_ref[0]

    def one_tile(j, carry):
        slot = step * group + j

        @pl.when(slot < live)
        def _():
            target = coords_ref[2 * slot]
            source = coords_ref[2 * slot + 1]
            if flipped:
                product = lax.dot_general(
                    gathered_ref[source],
                    tiles_ref[j],
                    (((1,), (1,)), ((), ())),
                    preferred_element_type=jnp.float32,
                )
            else:
                product = jnp.dot(
                    tiles_ref[j], gathered_ref[source], preferred_element_type=jnp.float32
                )
            total_ref[target] += product

        return carry

    @pl.when(step * group < live)
    def _():
        lax.fori_loop(0, group, one_tile, 0, unroll=True)

    @pl.when(step == pl.num_programs(0) - 1)
    def _():
        out_ref[...] = total_ref[...].astype(out_ref.dtype)


def tile_products(gathered, tiles, coords, live_total, flipped=False, group=16):
    row_blocks = lax.axis_size("col")
    slots, size, _ = tiles.shape
    block_shape = gathered.shape[1:]
    steps = slots // group

    def tile_map(step, coords_ref, count_ref):
        return (jnp.minimum(step, (count_ref[0] - 1) // group), 0, 0)

    def whole(step, coords_ref, count_ref):
        return (0, 0, 0)

    grid_spec = pltpu.PrefetchScalarGridSpec(
        num_scalar_prefetch=2,
        grid=(steps,),
        in_specs=[
            pl.BlockSpec((group, size, size), tile_map),
            pl.BlockSpec(gathered.shape, whole),
        ],
        out_specs=pl.BlockSpec((row_blocks, *block_shape), whole),
        scratch_shapes=[pltpu.VMEM((row_blocks, *block_shape), jnp.float32)],
    )
    return pl.pallas_call(
        functools.partial(products_kernel, group, flipped),
        grid_spec=grid_spec,
        out_shape=jax.ShapeDtypeStruct((row_blocks, *block_shape), jnp.bfloat16),
    )(coords.reshape(-1), live_total.reshape(1), tiles, gathered)


def on_device(
    features,
    tiles,
    tile_coords,
    tile_count,
    batch_mask,
    history,
    weight_one,
    bias_one,
    weight_two,
    bias_two,
):
    tile_set = tiles[0, 0]
    coord_set = tile_coords[0, 0]
    live_total = tile_count[0, 0]
    gathered_input = exchange(features[0, 0], "row", False, 0)
    summed_one = tile_products(gathered_input, tile_set, coord_set, live_total)
    owned_one = exchange(summed_one, "col", True, 1)
    owned_one = owned_one.astype(jnp.float32).sum(axis=0)
    agg_one = (features[0, 0].astype(jnp.float32) + owned_one).astype(jnp.bfloat16)
    pre_one = jnp.dot(agg_one, weight_one, preferred_element_type=jnp.float32) + bias_one
    hidden = jax.nn.relu(pre_one).astype(jnp.bfloat16)
    pushed = jnp.where(batch_mask[0, 0][:, None] == 1, hidden, history[0, 0])
    projected = jnp.dot(pushed, weight_two, preferred_element_type=jnp.float32).astype(jnp.bfloat16)
    gathered_proj = exchange(projected.T, "row", False, 2)
    summed_two = tile_products(gathered_proj, tile_set, coord_set, live_total, True)
    owned_two = exchange(summed_two, "col", True, 3).astype(jnp.float32).sum(axis=0).T
    scores = projected.astype(jnp.float32) + owned_two + bias_two
    return (pushed[None, None], scores[None, None])


def solution(mesh):
    return jax.shard_map(
        on_device,
        mesh=mesh,
        in_specs=(
            P("row", "col", None, None),
            P("row", "col", None, None, None),
            P("row", "col", None, None),
            P("row", "col"),
            P("row", "col", None),
            P("row", "col", None, None),
            P(),
            P(),
            P(),
            P(),
        ),
        out_specs=(P("row", "col", None, None), P("row", "col", None, None)),
        check_vma=False,
    )
```

```python
import functools

import jax
import jax.numpy as jnp
from jax import lax
from jax.experimental import pallas as pl
from jax.experimental.pallas import tpu as pltpu
from jax.sharding import PartitionSpec as P

MESH_ID = pl.DeviceIdType.MESH


def exchange_kernel(axis, other_axis, n, spread, src_ref, out_ref, send_sem, recv_sem):
    me = lax.axis_index(axis)
    other = lax.axis_index(other_axis)

    def device(k):
        return (k, other) if axis == "row" else (other, k)

    def outgoing(k):
        source = src_ref.at[k] if spread else src_ref
        return pltpu.make_async_remote_copy(
            src_ref=source,
            dst_ref=out_ref.at[me],
            send_sem=send_sem.at[k],
            recv_sem=recv_sem.at[me],
            device_id=device(k),
            device_id_type=MESH_ID,
        )

    def incoming(k):
        source = src_ref.at[k] if spread else src_ref
        return pltpu.make_async_remote_copy(
            src_ref=source,
            dst_ref=out_ref.at[k],
            send_sem=send_sem.at[k],
            recv_sem=recv_sem.at[k],
            device_id=device(k),
            device_id_type=MESH_ID,
        )

    barrier = pltpu.get_barrier_semaphore()

    def greet(step, carry):
        k = lax.rem(me + step, n)
        pl.semaphore_signal(barrier, 1, device_id=device(k), device_id_type=MESH_ID)
        return carry

    lax.fori_loop(1, n, greet, 0)
    pl.semaphore_wait(barrier, n - 1)

    def send(step, carry):
        outgoing(lax.rem(me + step, n)).start()
        return carry

    lax.fori_loop(1, n, send, 0)
    out_ref[me] = src_ref[me] if spread else src_ref[...]

    def finish(step, carry):
        k = lax.rem(me + step, n)
        outgoing(k).wait_send()
        incoming(lax.rem(me + n - step, n)).wait_recv()
        return carry

    lax.fori_loop(1, n, finish, 0)


def gather_kernel(n, src_ref, out_ref, send_sem, pass_sem, recv_sem):
    me = lax.axis_index("row")
    other = lax.axis_index("col")
    twin = me + 1 - 2 * lax.rem(me, 2)
    half = n // 2

    def copy(source, slot, sems, k):
        return pltpu.make_async_remote_copy(
            src_ref=source,
            dst_ref=out_ref.at[slot],
            send_sem=sems.at[k],
            recv_sem=recv_sem.at[slot],
            device_id=(k, other),
            device_id_type=MESH_ID,
        )

    def peer(step):
        return lax.rem(me + 2 * step, n)

    def far(step):
        return lax.rem(twin + 2 * step, n)

    barrier = pltpu.get_barrier_semaphore()
    pl.semaphore_signal(barrier, 1, device_id=(twin, other), device_id_type=MESH_ID)

    def greet(step, carry):
        pl.semaphore_signal(barrier, 1, device_id=(peer(step), other), device_id_type=MESH_ID)
        return carry

    lax.fori_loop(1, half, greet, 0)
    pl.semaphore_wait(barrier, half)

    def send(step, carry):
        copy(src_ref, me, send_sem, peer(step)).start()
        return carry

    lax.fori_loop(1, half, send, 0)
    copy(src_ref, me, send_sem, twin).start()
    out_ref[me] = src_ref[...]

    def relay(step, carry):
        k = peer(step)
        copy(src_ref, k, send_sem, k).wait_recv()
        copy(out_ref.at[k], k, pass_sem, twin).start()
        return carry

    lax.fori_loop(1, half, relay, 0)

    def finish(step, carry):
        k = peer(step)
        copy(src_ref, me, send_sem, k).wait_send()
        copy(out_ref.at[k], k, pass_sem, twin).wait_send()
        copy(src_ref, far(step), send_sem, twin).wait_recv()
        return carry

    lax.fori_loop(1, half, finish, 0)
    copy(src_ref, me, send_sem, twin).wait_send()
    copy(src_ref, twin, send_sem, twin).wait_recv()


def gather(block, tag):
    n = lax.axis_size("row")
    vmem = pl.BlockSpec(memory_space=pltpu.VMEM)
    return pl.pallas_call(
        functools.partial(gather_kernel, n),
        out_shape=jax.ShapeDtypeStruct((n, *block.shape), block.dtype),
        in_specs=[vmem],
        out_specs=vmem,
        scratch_shapes=[pltpu.SemaphoreType.DMA((n,))] * 3,
        compiler_params=pltpu.CompilerParams(collective_id=tag, has_side_effects=True),
    )(block)


def exchange(block, axis, spread, tag):
    other_axis = "col" if axis == "row" else "row"
    n = lax.axis_size(axis)
    shape = block.shape[1:] if spread else block.shape
    vmem = pl.BlockSpec(memory_space=pltpu.VMEM)
    return pl.pallas_call(
        functools.partial(exchange_kernel, axis, other_axis, n, spread),
        out_shape=jax.ShapeDtypeStruct((n, *shape), block.dtype),
        in_specs=[vmem],
        out_specs=vmem,
        scratch_shapes=[pltpu.SemaphoreType.DMA((n,)), pltpu.SemaphoreType.DMA((n,))],
        compiler_params=pltpu.CompilerParams(collective_id=tag, has_side_effects=True),
    )(block)


def joined_along(tiles, dim):
    tiles = jnp.moveaxis(tiles, 0, dim)
    lengths = tiles.shape
    return tiles.reshape(*lengths[:dim], lengths[dim] * lengths[dim + 1], *lengths[dim + 2 :])


def copy_for_each(shard, axis):
    copies = jnp.broadcast_to(shard, (lax.axis_size(axis), *shard.shape))
    return lax.all_to_all(copies, axis, split_axis=0, concat_axis=0, tiled=True)


def collect(shard, axis, dim):
    return joined_along(copy_for_each(shard, axis), dim)


def in_blocks(shard, dim, size):
    lengths = shard.shape
    tiles = shard.reshape(*lengths[:dim], size, lengths[dim] // size, *lengths[dim + 1 :])
    return jnp.moveaxis(tiles, dim, 0)


def sent_and_summed(shard, axis, dim):
    tiles = in_blocks(shard, dim, lax.axis_size(axis))
    arrived = lax.all_to_all(tiles, axis, split_axis=0, concat_axis=0, tiled=True)
    return arrived.astype(jnp.float32).sum(axis=0)


def products_kernel(group, flipped, coords_ref, count_ref, tiles_ref, gathered_ref, out_ref, total_ref):
    step = pl.program_id(0)

    @pl.when(step == 0)
    def _():
        total_ref[...] = jnp.zeros_like(total_ref)

    live = count_ref[0]

    def one_tile(j, carry):
        slot = step * group + j

        @pl.when(slot < live)
        def _():
            target = coords_ref[2 * slot]
            source = coords_ref[2 * slot + 1]
            if flipped:
                product = lax.dot_general(
                    gathered_ref[source],
                    tiles_ref[j],
                    (((1,), (1,)), ((), ())),
                    preferred_element_type=jnp.float32,
                )
            else:
                product = jnp.dot(
                    tiles_ref[j], gathered_ref[source], preferred_element_type=jnp.float32
                )
            total_ref[target] += product

        return carry

    @pl.when(step * group < live)
    def _():
        lax.fori_loop(0, group, one_tile, 0, unroll=True)

    @pl.when(step == pl.num_programs(0) - 1)
    def _():
        out_ref[...] = total_ref[...].astype(out_ref.dtype)


def tile_products(gathered, tiles, coords, live_total, flipped=False, group=16):
    row_blocks = lax.axis_size("col")
    slots, size, _ = tiles.shape
    block_shape = gathered.shape[1:]
    steps = slots // group

    def tile_map(step, coords_ref, count_ref):
        return (jnp.minimum(step, (count_ref[0] - 1) // group), 0, 0)

    def whole(step, coords_ref, count_ref):
        return (0, 0, 0)

    grid_spec = pltpu.PrefetchScalarGridSpec(
        num_scalar_prefetch=2,
        grid=(steps,),
        in_specs=[
            pl.BlockSpec((group, size, size), tile_map),
            pl.BlockSpec(gathered.shape, whole),
        ],
        out_specs=pl.BlockSpec((row_blocks, *block_shape), whole),
        scratch_shapes=[pltpu.VMEM((row_blocks, *block_shape), jnp.float32)],
    )
    return pl.pallas_call(
        functools.partial(products_kernel, group, flipped),
        grid_spec=grid_spec,
        out_shape=jax.ShapeDtypeStruct((row_blocks, *block_shape), jnp.bfloat16),
    )(coords.reshape(-1), live_total.reshape(1), tiles, gathered)


def on_device(
    features,
    tiles,
    tile_coords,
    tile_count,
    batch_mask,
    history,
    weight_one,
    bias_one,
    weight_two,
    bias_two,
):
    tile_set = tiles[0, 0]
    coord_set = tile_coords[0, 0]
    live_total = tile_count[0, 0]
    gathered_input = gather(features[0, 0], 0)
    summed_one = tile_products(gathered_input, tile_set, coord_set, live_total)
    owned_one = exchange(summed_one, "col", True, 1)
    owned_one = owned_one.astype(jnp.float32).sum(axis=0)
    agg_one = (features[0, 0].astype(jnp.float32) + owned_one).astype(jnp.bfloat16)
    pre_one = jnp.dot(agg_one, weight_one, preferred_element_type=jnp.float32) + bias_one
    hidden = jax.nn.relu(pre_one).astype(jnp.bfloat16)
    pushed = jnp.where(batch_mask[0, 0][:, None] == 1, hidden, history[0, 0])
    projected = jnp.dot(pushed, weight_two, preferred_element_type=jnp.float32).astype(jnp.bfloat16)
    gathered_proj = gather(projected.T, 2)
    summed_two = tile_products(gathered_proj, tile_set, coord_set, live_total, True)
    owned_two = exchange(summed_two, "col", True, 3).astype(jnp.float32).sum(axis=0).T
    scores = projected.astype(jnp.float32) + owned_two + bias_two
    return (pushed[None, None], scores[None, None])


def solution(mesh):
    return jax.shard_map(
        on_device,
        mesh=mesh,
        in_specs=(
            P("row", "col", None, None),
            P("row", "col", None, None, None),
            P("row", "col", None, None),
            P("row", "col"),
            P("row", "col", None),
            P("row", "col", None, None),
            P(),
            P(),
            P(),
            P(),
        ),
        out_specs=(P("row", "col", None, None), P("row", "col", None, None)),
        check_vma=False,
    )
```

```python
import functools

import jax
import jax.numpy as jnp
from jax import lax
from jax.experimental import pallas as pl
from jax.experimental.pallas import tpu as pltpu
from jax.sharding import PartitionSpec as P

MESH_ID = pl.DeviceIdType.MESH


def exchange_kernel(axis, other_axis, n, spread, src_ref, out_ref, send_sem, recv_sem):
    me = lax.axis_index(axis)
    other = lax.axis_index(other_axis)

    def device(k):
        return (k, other) if axis == "row" else (other, k)

    def outgoing(k):
        source = src_ref.at[k] if spread else src_ref
        return pltpu.make_async_remote_copy(
            src_ref=source,
            dst_ref=out_ref.at[me],
            send_sem=send_sem.at[k],
            recv_sem=recv_sem.at[me],
            device_id=device(k),
            device_id_type=MESH_ID,
        )

    def incoming(k):
        source = src_ref.at[k] if spread else src_ref
        return pltpu.make_async_remote_copy(
            src_ref=source,
            dst_ref=out_ref.at[k],
            send_sem=send_sem.at[k],
            recv_sem=recv_sem.at[k],
            device_id=device(k),
            device_id_type=MESH_ID,
        )

    barrier = pltpu.get_barrier_semaphore()

    def greet(step, carry):
        k = lax.rem(me + step, n)
        pl.semaphore_signal(barrier, 1, device_id=device(k), device_id_type=MESH_ID)
        return carry

    lax.fori_loop(1, n, greet, 0)
    pl.semaphore_wait(barrier, n - 1)

    def send(step, carry):
        outgoing(lax.rem(me + step, n)).start()
        return carry

    lax.fori_loop(1, n, send, 0)
    out_ref[me] = src_ref[me] if spread else src_ref[...]

    def finish(step, carry):
        k = lax.rem(me + step, n)
        outgoing(k).wait_send()
        incoming(lax.rem(me + n - step, n)).wait_recv()
        return carry

    lax.fori_loop(1, n, finish, 0)


def gather_kernel(n, src_ref, out_ref, send_sem, pass_sem, recv_sem):
    me = lax.axis_index("row")
    other = lax.axis_index("col")
    twin = me + 1 - 2 * lax.rem(me, 2)
    half = n // 2

    def copy(source, slot, sems, k):
        return pltpu.make_async_remote_copy(
            src_ref=source,
            dst_ref=out_ref.at[slot],
            send_sem=sems.at[k],
            recv_sem=recv_sem.at[slot],
            device_id=(k, other),
            device_id_type=MESH_ID,
        )

    def peer(step):
        return lax.rem(me + 2 * step, n)

    def far(step):
        return lax.rem(twin + 2 * step, n)

    barrier = pltpu.get_barrier_semaphore()
    pl.semaphore_signal(barrier, 1, device_id=(twin, other), device_id_type=MESH_ID)

    def greet(step, carry):
        pl.semaphore_signal(barrier, 1, device_id=(peer(step), other), device_id_type=MESH_ID)
        return carry

    lax.fori_loop(1, half, greet, 0)
    pl.semaphore_wait(barrier, half)

    def send(step, carry):
        copy(src_ref, me, send_sem, peer(step)).start()
        return carry

    lax.fori_loop(1, half, send, 0)
    copy(src_ref, me, send_sem, twin).start()
    out_ref[me] = src_ref[...]

    def relay(step, carry):
        k = peer(step)
        copy(src_ref, k, send_sem, k).wait_recv()
        copy(out_ref.at[k], k, pass_sem, twin).start()
        return carry

    lax.fori_loop(1, half, relay, 0)

    def finish(step, carry):
        k = peer(step)
        copy(src_ref, me, send_sem, k).wait_send()
        copy(out_ref.at[k], k, pass_sem, twin).wait_send()
        copy(src_ref, far(step), send_sem, twin).wait_recv()
        return carry

    lax.fori_loop(1, half, finish, 0)
    copy(src_ref, me, send_sem, twin).wait_send()
    copy(src_ref, twin, send_sem, twin).wait_recv()


def gather(block, tag):
    n = lax.axis_size("row")
    vmem = pl.BlockSpec(memory_space=pltpu.VMEM)
    return pl.pallas_call(
        functools.partial(gather_kernel, n),
        out_shape=jax.ShapeDtypeStruct((n, *block.shape), block.dtype),
        in_specs=[vmem],
        out_specs=vmem,
        scratch_shapes=[pltpu.SemaphoreType.DMA((n,))] * 3,
        compiler_params=pltpu.CompilerParams(collective_id=tag, has_side_effects=True),
    )(block)


def exchange(block, axis, spread, tag):
    other_axis = "col" if axis == "row" else "row"
    n = lax.axis_size(axis)
    shape = block.shape[1:] if spread else block.shape
    vmem = pl.BlockSpec(memory_space=pltpu.VMEM)
    return pl.pallas_call(
        functools.partial(exchange_kernel, axis, other_axis, n, spread),
        out_shape=jax.ShapeDtypeStruct((n, *shape), block.dtype),
        in_specs=[vmem],
        out_specs=vmem,
        scratch_shapes=[pltpu.SemaphoreType.DMA((n,)), pltpu.SemaphoreType.DMA((n,))],
        compiler_params=pltpu.CompilerParams(collective_id=tag, has_side_effects=True),
    )(block)


def joined_along(tiles, dim):
    tiles = jnp.moveaxis(tiles, 0, dim)
    lengths = tiles.shape
    return tiles.reshape(*lengths[:dim], lengths[dim] * lengths[dim + 1], *lengths[dim + 2 :])


def copy_for_each(shard, axis):
    copies = jnp.broadcast_to(shard, (lax.axis_size(axis), *shard.shape))
    return lax.all_to_all(copies, axis, split_axis=0, concat_axis=0, tiled=True)


def collect(shard, axis, dim):
    return joined_along(copy_for_each(shard, axis), dim)


def in_blocks(shard, dim, size):
    lengths = shard.shape
    tiles = shard.reshape(*lengths[:dim], size, lengths[dim] // size, *lengths[dim + 1 :])
    return jnp.moveaxis(tiles, dim, 0)


def sent_and_summed(shard, axis, dim):
    tiles = in_blocks(shard, dim, lax.axis_size(axis))
    arrived = lax.all_to_all(tiles, axis, split_axis=0, concat_axis=0, tiled=True)
    return arrived.astype(jnp.float32).sum(axis=0)


def products_kernel(
    flipped, coords_ref, count_ref, tiles_ref, gathered_ref, out_ref, order_ref, bounds_ref, cursor_ref
):
    blocks = out_ref.shape[0]
    live = count_ref[0]
    for target in range(blocks + 1):
        bounds_ref[target] = 0

    def count(slot, carry):
        target = coords_ref[2 * slot]
        bounds_ref[target + 1] = bounds_ref[target + 1] + 1
        return carry

    lax.fori_loop(0, live, count, 0)
    for target in range(blocks):
        bounds_ref[target + 1] = bounds_ref[target + 1] + bounds_ref[target]
        cursor_ref[target] = bounds_ref[target]

    def place(slot, carry):
        target = coords_ref[2 * slot]
        position = cursor_ref[target]
        order_ref[position] = slot
        cursor_ref[target] = position + 1
        return carry

    lax.fori_loop(0, live, place, 0)

    def product(slot, total):
        source = coords_ref[2 * slot + 1]
        if flipped:
            return total + lax.dot_general(
                gathered_ref[source],
                tiles_ref[slot],
                (((1,), (1,)), ((), ())),
                preferred_element_type=jnp.float32,
            )
        return total + jnp.dot(
            tiles_ref[slot], gathered_ref[source], preferred_element_type=jnp.float32
        )

    for target in range(blocks):
        total = lax.fori_loop(
            bounds_ref[target],
            bounds_ref[target + 1],
            lambda position, total: product(order_ref[position], total),
            jnp.zeros(out_ref.shape[1:], jnp.float32),
        )
        out_ref[target] = total.astype(out_ref.dtype)


def tile_products(gathered, tiles, coords, live_total, flipped=False):
    row_blocks = lax.axis_size("col")
    slots = tiles.shape[0]
    block_shape = gathered.shape[1:]
    vmem = pl.BlockSpec(memory_space=pltpu.VMEM)
    smem = pl.BlockSpec(memory_space=pltpu.SMEM)
    return pl.pallas_call(
        functools.partial(products_kernel, flipped),
        in_specs=[smem, smem, vmem, vmem],
        out_specs=vmem,
        out_shape=jax.ShapeDtypeStruct((row_blocks, *block_shape), jnp.bfloat16),
        scratch_shapes=[
            pltpu.SMEM((slots,), jnp.int32),
            pltpu.SMEM((row_blocks + 1,), jnp.int32),
            pltpu.SMEM((row_blocks,), jnp.int32),
        ],
    )(coords.reshape(-1), live_total.reshape(1), tiles, gathered)


def on_device(
    features,
    tiles,
    tile_coords,
    tile_count,
    batch_mask,
    history,
    weight_one,
    bias_one,
    weight_two,
    bias_two,
):
    tile_set = tiles[0, 0]
    coord_set = tile_coords[0, 0]
    live_total = tile_count[0, 0]
    gathered_input = gather(features[0, 0], 0)
    summed_one = tile_products(gathered_input, tile_set, coord_set, live_total)
    owned_one = exchange(summed_one, "col", True, 1)
    owned_one = owned_one.astype(jnp.float32).sum(axis=0)
    agg_one = (features[0, 0].astype(jnp.float32) + owned_one).astype(jnp.bfloat16)
    pre_one = jnp.dot(agg_one, weight_one, preferred_element_type=jnp.float32) + bias_one
    hidden = jax.nn.relu(pre_one).astype(jnp.bfloat16)
    pushed = jnp.where(batch_mask[0, 0][:, None] == 1, hidden, history[0, 0])
    projected = jnp.dot(pushed, weight_two, preferred_element_type=jnp.float32).astype(jnp.bfloat16)
    gathered_proj = gather(projected.T, 2)
    summed_two = tile_products(gathered_proj, tile_set, coord_set, live_total, True)
    owned_two = exchange(summed_two, "col", True, 3).astype(jnp.float32).sum(axis=0).T
    scores = projected.astype(jnp.float32) + owned_two + bias_two
    return (pushed[None, None], scores[None, None])


def solution(mesh):
    return jax.shard_map(
        on_device,
        mesh=mesh,
        in_specs=(
            P("row", "col", None, None),
            P("row", "col", None, None, None),
            P("row", "col", None, None),
            P("row", "col"),
            P("row", "col", None),
            P("row", "col", None, None),
            P(),
            P(),
            P(),
            P(),
        ),
        out_specs=(P("row", "col", None, None), P("row", "col", None, None)),
        check_vma=False,
    )
```

```python
import functools

import jax
import jax.numpy as jnp
from jax import lax
from jax.experimental import pallas as pl
from jax.experimental.pallas import tpu as pltpu
from jax.sharding import PartitionSpec as P

MESH_ID = pl.DeviceIdType.MESH


def exchange_kernel(axis, other_axis, n, spread, src_ref, out_ref, send_sem, recv_sem):
    me = lax.axis_index(axis)
    other = lax.axis_index(other_axis)

    def device(k):
        return (k, other) if axis == "row" else (other, k)

    def outgoing(k):
        source = src_ref.at[k] if spread else src_ref
        return pltpu.make_async_remote_copy(
            src_ref=source,
            dst_ref=out_ref.at[me],
            send_sem=send_sem.at[k],
            recv_sem=recv_sem.at[me],
            device_id=device(k),
            device_id_type=MESH_ID,
        )

    def incoming(k):
        source = src_ref.at[k] if spread else src_ref
        return pltpu.make_async_remote_copy(
            src_ref=source,
            dst_ref=out_ref.at[k],
            send_sem=send_sem.at[k],
            recv_sem=recv_sem.at[k],
            device_id=device(k),
            device_id_type=MESH_ID,
        )

    barrier = pltpu.get_barrier_semaphore()

    def greet(step, carry):
        k = lax.rem(me + step, n)
        pl.semaphore_signal(barrier, 1, device_id=device(k), device_id_type=MESH_ID)
        return carry

    lax.fori_loop(1, n, greet, 0)
    pl.semaphore_wait(barrier, n - 1)

    def send(step, carry):
        outgoing(lax.rem(me + step, n)).start()
        return carry

    lax.fori_loop(1, n, send, 0)
    out_ref[me] = src_ref[me] if spread else src_ref[...]

    def finish(step, carry):
        k = lax.rem(me + step, n)
        outgoing(k).wait_send()
        incoming(lax.rem(me + n - step, n)).wait_recv()
        return carry

    lax.fori_loop(1, n, finish, 0)


def gather_kernel(n, src_ref, out_ref, send_sem, pass_sem, recv_sem):
    me = lax.axis_index("row")
    other = lax.axis_index("col")
    twin = me + 1 - 2 * lax.rem(me, 2)
    half = n // 2

    def copy(source, slot, sems, k):
        return pltpu.make_async_remote_copy(
            src_ref=source,
            dst_ref=out_ref.at[slot],
            send_sem=sems.at[k],
            recv_sem=recv_sem.at[slot],
            device_id=(k, other),
            device_id_type=MESH_ID,
        )

    def peer(step):
        return lax.rem(me + 2 * step, n)

    def far(step):
        return lax.rem(twin + 2 * step, n)

    barrier = pltpu.get_barrier_semaphore()
    pl.semaphore_signal(barrier, 1, device_id=(twin, other), device_id_type=MESH_ID)

    def greet(step, carry):
        pl.semaphore_signal(barrier, 1, device_id=(peer(step), other), device_id_type=MESH_ID)
        return carry

    lax.fori_loop(1, half, greet, 0)
    pl.semaphore_wait(barrier, half)

    def send(step, carry):
        copy(src_ref, me, send_sem, peer(step)).start()
        return carry

    lax.fori_loop(1, half, send, 0)
    copy(src_ref, me, send_sem, twin).start()
    out_ref[me] = src_ref[...]

    def relay(step, carry):
        k = peer(step)
        copy(src_ref, k, send_sem, k).wait_recv()
        copy(out_ref.at[k], k, pass_sem, twin).start()
        return carry

    lax.fori_loop(1, half, relay, 0)

    def finish(step, carry):
        k = peer(step)
        copy(src_ref, me, send_sem, k).wait_send()
        copy(out_ref.at[k], k, pass_sem, twin).wait_send()
        copy(src_ref, far(step), send_sem, twin).wait_recv()
        return carry

    lax.fori_loop(1, half, finish, 0)
    copy(src_ref, me, send_sem, twin).wait_send()
    copy(src_ref, twin, send_sem, twin).wait_recv()


def gather(block, tag):
    n = lax.axis_size("row")
    vmem = pl.BlockSpec(memory_space=pltpu.VMEM)
    return pl.pallas_call(
        functools.partial(gather_kernel, n),
        out_shape=jax.ShapeDtypeStruct((n, *block.shape), block.dtype),
        in_specs=[vmem],
        out_specs=vmem,
        scratch_shapes=[pltpu.SemaphoreType.DMA((n,))] * 3,
        compiler_params=pltpu.CompilerParams(collective_id=tag, has_side_effects=True),
    )(block)


def exchange(block, axis, spread, tag):
    other_axis = "col" if axis == "row" else "row"
    n = lax.axis_size(axis)
    shape = block.shape[1:] if spread else block.shape
    vmem = pl.BlockSpec(memory_space=pltpu.VMEM)
    return pl.pallas_call(
        functools.partial(exchange_kernel, axis, other_axis, n, spread),
        out_shape=jax.ShapeDtypeStruct((n, *shape), block.dtype),
        in_specs=[vmem],
        out_specs=vmem,
        scratch_shapes=[pltpu.SemaphoreType.DMA((n,)), pltpu.SemaphoreType.DMA((n,))],
        compiler_params=pltpu.CompilerParams(collective_id=tag, has_side_effects=True),
    )(block)


def joined_along(tiles, dim):
    tiles = jnp.moveaxis(tiles, 0, dim)
    lengths = tiles.shape
    return tiles.reshape(*lengths[:dim], lengths[dim] * lengths[dim + 1], *lengths[dim + 2 :])


def copy_for_each(shard, axis):
    copies = jnp.broadcast_to(shard, (lax.axis_size(axis), *shard.shape))
    return lax.all_to_all(copies, axis, split_axis=0, concat_axis=0, tiled=True)


def collect(shard, axis, dim):
    return joined_along(copy_for_each(shard, axis), dim)


def in_blocks(shard, dim, size):
    lengths = shard.shape
    tiles = shard.reshape(*lengths[:dim], size, lengths[dim] // size, *lengths[dim + 1 :])
    return jnp.moveaxis(tiles, dim, 0)


def sent_and_summed(shard, axis, dim):
    tiles = in_blocks(shard, dim, lax.axis_size(axis))
    arrived = lax.all_to_all(tiles, axis, split_axis=0, concat_axis=0, tiled=True)
    return arrived.astype(jnp.float32).sum(axis=0)


def products_kernel(
    flipped, pack, coords_ref, count_ref, tiles_ref, gathered_ref, out_ref, order_ref, bounds_ref, cursor_ref
):
    blocks = out_ref.shape[0]
    live = count_ref[0]
    for target in range(blocks + 1):
        bounds_ref[target] = 0

    def count(slot, carry):
        target = coords_ref[2 * slot]
        bounds_ref[target + 1] = bounds_ref[target + 1] + 1
        return carry

    lax.fori_loop(0, live, count, 0)
    for target in range(blocks):
        bounds_ref[target + 1] = bounds_ref[target + 1] + bounds_ref[target]
        cursor_ref[target] = bounds_ref[target]

    def place(slot, carry):
        target = coords_ref[2 * slot]
        position = cursor_ref[target]
        order_ref[position] = slot
        cursor_ref[target] = position + 1
        return carry

    lax.fori_loop(0, live, place, 0)

    def product(first, end, total):
        tiles, sources = [], []
        for offset in range(pack):
            slot = order_ref[jnp.minimum(first + offset, end - 1)]
            tile = tiles_ref[slot]
            tiles.append(jnp.where(first + offset < end, tile, jnp.zeros_like(tile)))
            sources.append(gathered_ref[coords_ref[2 * slot + 1]])
        if flipped:
            return total + lax.dot_general(
                jnp.concatenate(sources, axis=1),
                jnp.concatenate(tiles, axis=1),
                (((1,), (1,)), ((), ())),
                preferred_element_type=jnp.float32,
            )
        return total + jnp.dot(
            jnp.concatenate(tiles, axis=1),
            jnp.concatenate(sources, axis=0),
            preferred_element_type=jnp.float32,
        )

    for target in range(blocks):
        first, end = bounds_ref[target], bounds_ref[target + 1]
        total = lax.fori_loop(
            0,
            (end - first + pack - 1) // pack,
            lambda step, total: product(first + step * pack, end, total),
            jnp.zeros(out_ref.shape[1:], jnp.float32),
        )
        out_ref[target] = total.astype(out_ref.dtype)


def tile_products(gathered, tiles, coords, live_total, flipped=False, pack=4):
    row_blocks = lax.axis_size("col")
    slots = tiles.shape[0]
    block_shape = gathered.shape[1:]
    vmem = pl.BlockSpec(memory_space=pltpu.VMEM)
    smem = pl.BlockSpec(memory_space=pltpu.SMEM)
    return pl.pallas_call(
        functools.partial(products_kernel, flipped, pack),
        in_specs=[smem, smem, vmem, vmem],
        out_specs=vmem,
        out_shape=jax.ShapeDtypeStruct((row_blocks, *block_shape), jnp.bfloat16),
        scratch_shapes=[
            pltpu.SMEM((slots,), jnp.int32),
            pltpu.SMEM((row_blocks + 1,), jnp.int32),
            pltpu.SMEM((row_blocks,), jnp.int32),
        ],
    )(coords.reshape(-1), live_total.reshape(1), tiles, gathered)


def on_device(
    features,
    tiles,
    tile_coords,
    tile_count,
    batch_mask,
    history,
    weight_one,
    bias_one,
    weight_two,
    bias_two,
):
    tile_set = tiles[0, 0]
    coord_set = tile_coords[0, 0]
    live_total = tile_count[0, 0]
    gathered_input = gather(features[0, 0], 0)
    summed_one = tile_products(gathered_input, tile_set, coord_set, live_total)
    owned_one = exchange(summed_one, "col", True, 1)
    owned_one = owned_one.astype(jnp.float32).sum(axis=0)
    agg_one = (features[0, 0].astype(jnp.float32) + owned_one).astype(jnp.bfloat16)
    pre_one = jnp.dot(agg_one, weight_one, preferred_element_type=jnp.float32) + bias_one
    hidden = jax.nn.relu(pre_one).astype(jnp.bfloat16)
    pushed = jnp.where(batch_mask[0, 0][:, None] == 1, hidden, history[0, 0])
    projected = jnp.dot(pushed, weight_two, preferred_element_type=jnp.float32).astype(jnp.bfloat16)
    gathered_proj = gather(projected.T, 2)
    summed_two = tile_products(gathered_proj, tile_set, coord_set, live_total, True)
    owned_two = exchange(summed_two, "col", True, 3).astype(jnp.float32).sum(axis=0).T
    scores = projected.astype(jnp.float32) + owned_two + bias_two
    return (pushed[None, None], scores[None, None])


def solution(mesh):
    return jax.shard_map(
        on_device,
        mesh=mesh,
        in_specs=(
            P("row", "col", None, None),
            P("row", "col", None, None, None),
            P("row", "col", None, None),
            P("row", "col"),
            P("row", "col", None),
            P("row", "col", None, None),
            P(),
            P(),
            P(),
            P(),
        ),
        out_specs=(P("row", "col", None, None), P("row", "col", None, None)),
        check_vma=False,
    )
```

```python
import functools

import jax
import jax.numpy as jnp
from jax import lax
from jax.experimental import pallas as pl
from jax.experimental.pallas import tpu as pltpu
from jax.sharding import PartitionSpec as P

MESH_ID = pl.DeviceIdType.MESH


def exchange_kernel(axis, other_axis, n, spread, src_ref, out_ref, send_sem, recv_sem):
    me = lax.axis_index(axis)
    other = lax.axis_index(other_axis)

    def device(k):
        return (k, other) if axis == "row" else (other, k)

    def outgoing(k):
        source = src_ref.at[k] if spread else src_ref
        return pltpu.make_async_remote_copy(
            src_ref=source,
            dst_ref=out_ref.at[me],
            send_sem=send_sem.at[k],
            recv_sem=recv_sem.at[me],
            device_id=device(k),
            device_id_type=MESH_ID,
        )

    def incoming(k):
        source = src_ref.at[k] if spread else src_ref
        return pltpu.make_async_remote_copy(
            src_ref=source,
            dst_ref=out_ref.at[k],
            send_sem=send_sem.at[k],
            recv_sem=recv_sem.at[k],
            device_id=device(k),
            device_id_type=MESH_ID,
        )

    barrier = pltpu.get_barrier_semaphore()

    def greet(step, carry):
        k = lax.rem(me + step, n)
        pl.semaphore_signal(barrier, 1, device_id=device(k), device_id_type=MESH_ID)
        return carry

    lax.fori_loop(1, n, greet, 0)
    pl.semaphore_wait(barrier, n - 1)

    def send(step, carry):
        outgoing(lax.rem(me + step, n)).start()
        return carry

    lax.fori_loop(1, n, send, 0)
    out_ref[me] = src_ref[me] if spread else src_ref[...]

    def finish(step, carry):
        k = lax.rem(me + step, n)
        outgoing(k).wait_send()
        incoming(lax.rem(me + n - step, n)).wait_recv()
        return carry

    lax.fori_loop(1, n, finish, 0)


def gather_kernel(n, src_ref, out_ref, send_sem, pass_sem, recv_sem):
    me = lax.axis_index("row")
    other = lax.axis_index("col")
    twin = me + 1 - 2 * lax.rem(me, 2)
    half = n // 2

    def copy(source, slot, sems, k):
        return pltpu.make_async_remote_copy(
            src_ref=source,
            dst_ref=out_ref.at[slot],
            send_sem=sems.at[k],
            recv_sem=recv_sem.at[slot],
            device_id=(k, other),
            device_id_type=MESH_ID,
        )

    def peer(step):
        return lax.rem(me + 2 * step, n)

    def far(step):
        return lax.rem(twin + 2 * step, n)

    barrier = pltpu.get_barrier_semaphore()
    pl.semaphore_signal(barrier, 1, device_id=(twin, other), device_id_type=MESH_ID)

    def greet(step, carry):
        pl.semaphore_signal(barrier, 1, device_id=(peer(step), other), device_id_type=MESH_ID)
        return carry

    lax.fori_loop(1, half, greet, 0)
    pl.semaphore_wait(barrier, half)

    def send(step, carry):
        copy(src_ref, me, send_sem, peer(step)).start()
        return carry

    lax.fori_loop(1, half, send, 0)
    copy(src_ref, me, send_sem, twin).start()
    out_ref[me] = src_ref[...]

    def relay(step, carry):
        k = peer(step)
        copy(src_ref, k, send_sem, k).wait_recv()
        copy(out_ref.at[k], k, pass_sem, twin).start()
        return carry

    lax.fori_loop(1, half, relay, 0)

    def finish(step, carry):
        k = peer(step)
        copy(src_ref, me, send_sem, k).wait_send()
        copy(out_ref.at[k], k, pass_sem, twin).wait_send()
        copy(src_ref, far(step), send_sem, twin).wait_recv()
        return carry

    lax.fori_loop(1, half, finish, 0)
    copy(src_ref, me, send_sem, twin).wait_send()
    copy(src_ref, twin, send_sem, twin).wait_recv()


def gather(block, tag):
    n = lax.axis_size("row")
    vmem = pl.BlockSpec(memory_space=pltpu.VMEM)
    return pl.pallas_call(
        functools.partial(gather_kernel, n),
        out_shape=jax.ShapeDtypeStruct((n, *block.shape), block.dtype),
        in_specs=[vmem],
        out_specs=vmem,
        scratch_shapes=[pltpu.SemaphoreType.DMA((n,))] * 3,
        compiler_params=pltpu.CompilerParams(collective_id=tag, has_side_effects=True),
    )(block)


def exchange(block, axis, spread, tag):
    other_axis = "col" if axis == "row" else "row"
    n = lax.axis_size(axis)
    shape = block.shape[1:] if spread else block.shape
    vmem = pl.BlockSpec(memory_space=pltpu.VMEM)
    return pl.pallas_call(
        functools.partial(exchange_kernel, axis, other_axis, n, spread),
        out_shape=jax.ShapeDtypeStruct((n, *shape), block.dtype),
        in_specs=[vmem],
        out_specs=vmem,
        scratch_shapes=[pltpu.SemaphoreType.DMA((n,)), pltpu.SemaphoreType.DMA((n,))],
        compiler_params=pltpu.CompilerParams(collective_id=tag, has_side_effects=True),
    )(block)


def joined_along(tiles, dim):
    tiles = jnp.moveaxis(tiles, 0, dim)
    lengths = tiles.shape
    return tiles.reshape(*lengths[:dim], lengths[dim] * lengths[dim + 1], *lengths[dim + 2 :])


def copy_for_each(shard, axis):
    copies = jnp.broadcast_to(shard, (lax.axis_size(axis), *shard.shape))
    return lax.all_to_all(copies, axis, split_axis=0, concat_axis=0, tiled=True)


def collect(shard, axis, dim):
    return joined_along(copy_for_each(shard, axis), dim)


def in_blocks(shard, dim, size):
    lengths = shard.shape
    tiles = shard.reshape(*lengths[:dim], size, lengths[dim] // size, *lengths[dim + 1 :])
    return jnp.moveaxis(tiles, dim, 0)


def sent_and_summed(shard, axis, dim):
    tiles = in_blocks(shard, dim, lax.axis_size(axis))
    arrived = lax.all_to_all(tiles, axis, split_axis=0, concat_axis=0, tiled=True)
    return arrived.astype(jnp.float32).sum(axis=0)


def products_kernel(
    flipped, pack, coords_ref, count_ref, tiles_ref, gathered_ref, out_ref, order_ref, bounds_ref, cursor_ref
):
    blocks = out_ref.shape[0]
    live = count_ref[0]
    for target in range(blocks + 1):
        bounds_ref[target] = 0

    def count(slot, carry):
        target = coords_ref[2 * slot]
        bounds_ref[target + 1] = bounds_ref[target + 1] + 1
        return carry

    lax.fori_loop(0, live, count, 0)
    for target in range(blocks):
        bounds_ref[target + 1] = bounds_ref[target + 1] + bounds_ref[target]
        cursor_ref[target] = bounds_ref[target]

    def place(slot, carry):
        target = coords_ref[2 * slot]
        position = cursor_ref[target]
        order_ref[position] = slot
        cursor_ref[target] = position + 1
        return carry

    lax.fori_loop(0, live, place, 0)

    def product(first, end, total):
        tiles, sources = [], []
        for offset in range(pack):
            slot = order_ref[jnp.minimum(first + offset, end - 1)]
            tile = tiles_ref[slot]
            tiles.append(jnp.where(first + offset < end, tile, jnp.zeros_like(tile)))
            sources.append(gathered_ref[coords_ref[2 * slot + 1]])
        if flipped:
            return total + lax.dot_general(
                jnp.concatenate(sources, axis=1),
                jnp.concatenate(tiles, axis=1),
                (((1,), (1,)), ((), ())),
                preferred_element_type=jnp.float32,
            )
        return total + jnp.dot(
            jnp.concatenate(tiles, axis=1),
            jnp.concatenate(sources, axis=0),
            preferred_element_type=jnp.float32,
        )

    for target in range(blocks):
        first, end = bounds_ref[target], bounds_ref[target + 1]
        total = lax.fori_loop(
            0,
            (end - first + pack - 1) // pack,
            lambda step, total: product(first + step * pack, end, total),
            jnp.zeros(out_ref.shape[1:], jnp.float32),
        )
        out_ref[target] = total.astype(out_ref.dtype)


def tile_products(gathered, tiles, coords, live_total, flipped=False, pack=8):
    row_blocks = lax.axis_size("col")
    slots = tiles.shape[0]
    block_shape = gathered.shape[1:]
    vmem = pl.BlockSpec(memory_space=pltpu.VMEM)
    smem = pl.BlockSpec(memory_space=pltpu.SMEM)
    return pl.pallas_call(
        functools.partial(products_kernel, flipped, pack),
        in_specs=[smem, smem, vmem, vmem],
        out_specs=vmem,
        out_shape=jax.ShapeDtypeStruct((row_blocks, *block_shape), jnp.bfloat16),
        scratch_shapes=[
            pltpu.SMEM((slots,), jnp.int32),
            pltpu.SMEM((row_blocks + 1,), jnp.int32),
            pltpu.SMEM((row_blocks,), jnp.int32),
        ],
    )(coords.reshape(-1), live_total.reshape(1), tiles, gathered)


def on_device(
    features,
    tiles,
    tile_coords,
    tile_count,
    batch_mask,
    history,
    weight_one,
    bias_one,
    weight_two,
    bias_two,
):
    tile_set = tiles[0, 0]
    coord_set = tile_coords[0, 0]
    live_total = tile_count[0, 0]
    gathered_input = gather(features[0, 0], 0)
    summed_one = tile_products(gathered_input, tile_set, coord_set, live_total)
    owned_one = exchange(summed_one, "col", True, 1)
    owned_one = owned_one.astype(jnp.float32).sum(axis=0)
    agg_one = (features[0, 0].astype(jnp.float32) + owned_one).astype(jnp.bfloat16)
    pre_one = jnp.dot(agg_one, weight_one, preferred_element_type=jnp.float32) + bias_one
    hidden = jax.nn.relu(pre_one).astype(jnp.bfloat16)
    pushed = jnp.where(batch_mask[0, 0][:, None] == 1, hidden, history[0, 0])
    projected = jnp.dot(pushed, weight_two, preferred_element_type=jnp.float32).astype(jnp.bfloat16)
    gathered_proj = gather(projected.T, 2)
    summed_two = tile_products(gathered_proj, tile_set, coord_set, live_total, True)
    owned_two = exchange(summed_two, "col", True, 3).astype(jnp.float32).sum(axis=0).T
    scores = projected.astype(jnp.float32) + owned_two + bias_two
    return (pushed[None, None], scores[None, None])


def solution(mesh):
    return jax.shard_map(
        on_device,
        mesh=mesh,
        in_specs=(
            P("row", "col", None, None),
            P("row", "col", None, None, None),
            P("row", "col", None, None),
            P("row", "col"),
            P("row", "col", None),
            P("row", "col", None, None),
            P(),
            P(),
            P(),
            P(),
        ),
        out_specs=(P("row", "col", None, None), P("row", "col", None, None)),
        check_vma=False,
    )
```

```python
import functools

import jax
import jax.numpy as jnp
from jax import lax
from jax.experimental import pallas as pl
from jax.experimental.pallas import tpu as pltpu
from jax.sharding import PartitionSpec as P

MESH_ID = pl.DeviceIdType.MESH


def exchange_kernel(axis, other_axis, n, spread, src_ref, out_ref, send_sem, recv_sem):
    me = lax.axis_index(axis)
    other = lax.axis_index(other_axis)

    def device(k):
        return (k, other) if axis == "row" else (other, k)

    def outgoing(k):
        source = src_ref.at[k] if spread else src_ref
        return pltpu.make_async_remote_copy(
            src_ref=source,
            dst_ref=out_ref.at[me],
            send_sem=send_sem.at[k],
            recv_sem=recv_sem.at[me],
            device_id=device(k),
            device_id_type=MESH_ID,
        )

    def incoming(k):
        source = src_ref.at[k] if spread else src_ref
        return pltpu.make_async_remote_copy(
            src_ref=source,
            dst_ref=out_ref.at[k],
            send_sem=send_sem.at[k],
            recv_sem=recv_sem.at[k],
            device_id=device(k),
            device_id_type=MESH_ID,
        )

    barrier = pltpu.get_barrier_semaphore()

    def greet(step, carry):
        k = lax.rem(me + step, n)
        pl.semaphore_signal(barrier, 1, device_id=device(k), device_id_type=MESH_ID)
        return carry

    lax.fori_loop(1, n, greet, 0)
    pl.semaphore_wait(barrier, n - 1)

    def send(step, carry):
        outgoing(lax.rem(me + step, n)).start()
        return carry

    lax.fori_loop(1, n, send, 0)
    out_ref[me] = src_ref[me] if spread else src_ref[...]

    def finish(step, carry):
        k = lax.rem(me + step, n)
        outgoing(k).wait_send()
        incoming(lax.rem(me + n - step, n)).wait_recv()
        return carry

    lax.fori_loop(1, n, finish, 0)


def gather_kernel(n, src_ref, out_ref, send_sem, pass_sem, recv_sem):
    me = lax.axis_index("row")
    other = lax.axis_index("col")
    twin = me + 1 - 2 * lax.rem(me, 2)
    half = n // 2

    def copy(source, slot, sems, k):
        return pltpu.make_async_remote_copy(
            src_ref=source,
            dst_ref=out_ref.at[slot],
            send_sem=sems.at[k],
            recv_sem=recv_sem.at[slot],
            device_id=(k, other),
            device_id_type=MESH_ID,
        )

    def peer(step):
        return lax.rem(me + 2 * step, n)

    def far(step):
        return lax.rem(twin + 2 * step, n)

    barrier = pltpu.get_barrier_semaphore()
    pl.semaphore_signal(barrier, 1, device_id=(twin, other), device_id_type=MESH_ID)

    def greet(step, carry):
        pl.semaphore_signal(barrier, 1, device_id=(peer(step), other), device_id_type=MESH_ID)
        return carry

    lax.fori_loop(1, half, greet, 0)
    pl.semaphore_wait(barrier, half)

    def send(step, carry):
        copy(src_ref, me, send_sem, peer(step)).start()
        return carry

    lax.fori_loop(1, half, send, 0)
    copy(src_ref, me, send_sem, twin).start()
    out_ref[me] = src_ref[...]

    def relay(step, carry):
        k = peer(step)
        copy(src_ref, k, send_sem, k).wait_recv()
        copy(out_ref.at[k], k, pass_sem, twin).start()
        return carry

    lax.fori_loop(1, half, relay, 0)

    def finish(step, carry):
        k = peer(step)
        copy(src_ref, me, send_sem, k).wait_send()
        copy(out_ref.at[k], k, pass_sem, twin).wait_send()
        copy(src_ref, far(step), send_sem, twin).wait_recv()
        return carry

    lax.fori_loop(1, half, finish, 0)
    copy(src_ref, me, send_sem, twin).wait_send()
    copy(src_ref, twin, send_sem, twin).wait_recv()


def gather(block, tag):
    n = lax.axis_size("row")
    vmem = pl.BlockSpec(memory_space=pltpu.VMEM)
    return pl.pallas_call(
        functools.partial(gather_kernel, n),
        out_shape=jax.ShapeDtypeStruct((n, *block.shape), block.dtype),
        in_specs=[vmem],
        out_specs=vmem,
        scratch_shapes=[pltpu.SemaphoreType.DMA((n,))] * 3,
        compiler_params=pltpu.CompilerParams(collective_id=tag, has_side_effects=True),
    )(block)


def exchange(block, axis, spread, tag):
    other_axis = "col" if axis == "row" else "row"
    n = lax.axis_size(axis)
    shape = block.shape[1:] if spread else block.shape
    vmem = pl.BlockSpec(memory_space=pltpu.VMEM)
    return pl.pallas_call(
        functools.partial(exchange_kernel, axis, other_axis, n, spread),
        out_shape=jax.ShapeDtypeStruct((n, *shape), block.dtype),
        in_specs=[vmem],
        out_specs=vmem,
        scratch_shapes=[pltpu.SemaphoreType.DMA((n,)), pltpu.SemaphoreType.DMA((n,))],
        compiler_params=pltpu.CompilerParams(collective_id=tag, has_side_effects=True),
    )(block)


def joined_along(tiles, dim):
    tiles = jnp.moveaxis(tiles, 0, dim)
    lengths = tiles.shape
    return tiles.reshape(*lengths[:dim], lengths[dim] * lengths[dim + 1], *lengths[dim + 2 :])


def copy_for_each(shard, axis):
    copies = jnp.broadcast_to(shard, (lax.axis_size(axis), *shard.shape))
    return lax.all_to_all(copies, axis, split_axis=0, concat_axis=0, tiled=True)


def collect(shard, axis, dim):
    return joined_along(copy_for_each(shard, axis), dim)


def in_blocks(shard, dim, size):
    lengths = shard.shape
    tiles = shard.reshape(*lengths[:dim], size, lengths[dim] // size, *lengths[dim + 1 :])
    return jnp.moveaxis(tiles, dim, 0)


def sent_and_summed(shard, axis, dim):
    tiles = in_blocks(shard, dim, lax.axis_size(axis))
    arrived = lax.all_to_all(tiles, axis, split_axis=0, concat_axis=0, tiled=True)
    return arrived.astype(jnp.float32).sum(axis=0)


def products_kernel(
    flipped, pack, coords_ref, count_ref, tiles_ref, gathered_ref, out_ref, order_ref, bounds_ref, cursor_ref
):
    blocks = out_ref.shape[0]
    live = count_ref[0]
    for target in range(blocks + 1):
        bounds_ref[target] = 0

    def count(slot, carry):
        target = coords_ref[2 * slot]
        bounds_ref[target + 1] = bounds_ref[target + 1] + 1
        return carry

    lax.fori_loop(0, live, count, 0)
    for target in range(blocks):
        bounds_ref[target + 1] = bounds_ref[target + 1] + bounds_ref[target]
        cursor_ref[target] = bounds_ref[target]

    def place(slot, carry):
        target = coords_ref[2 * slot]
        position = cursor_ref[target]
        order_ref[position] = slot
        cursor_ref[target] = position + 1
        return carry

    lax.fori_loop(0, live, place, 0)

    def product(first, end, total):
        tiles, sources = [], []
        for offset in range(pack):
            slot = order_ref[jnp.minimum(first + offset, end - 1)]
            tile = tiles_ref[slot]
            tiles.append(jnp.where(first + offset < end, tile, jnp.zeros_like(tile)))
            sources.append(gathered_ref[coords_ref[2 * slot + 1]])
        if flipped:
            return total + lax.dot_general(
                jnp.concatenate(sources, axis=1),
                jnp.concatenate(tiles, axis=1),
                (((1,), (1,)), ((), ())),
                preferred_element_type=jnp.float32,
            )
        return total + jnp.dot(
            jnp.concatenate(tiles, axis=1),
            jnp.concatenate(sources, axis=0),
            preferred_element_type=jnp.float32,
        )

    for target in range(blocks):
        first, end = bounds_ref[target], bounds_ref[target + 1]
        total = lax.fori_loop(
            0,
            (end - first + pack - 1) // pack,
            lambda step, total: product(first + step * pack, end, total),
            jnp.zeros(out_ref.shape[1:], jnp.float32),
        )
        out_ref[target] = total.astype(out_ref.dtype)


def tile_products(gathered, tiles, coords, live_total, flipped=False, pack=16):
    row_blocks = lax.axis_size("col")
    slots = tiles.shape[0]
    block_shape = gathered.shape[1:]
    vmem = pl.BlockSpec(memory_space=pltpu.VMEM)
    smem = pl.BlockSpec(memory_space=pltpu.SMEM)
    return pl.pallas_call(
        functools.partial(products_kernel, flipped, pack),
        in_specs=[smem, smem, vmem, vmem],
        out_specs=vmem,
        out_shape=jax.ShapeDtypeStruct((row_blocks, *block_shape), jnp.bfloat16),
        scratch_shapes=[
            pltpu.SMEM((slots,), jnp.int32),
            pltpu.SMEM((row_blocks + 1,), jnp.int32),
            pltpu.SMEM((row_blocks,), jnp.int32),
        ],
    )(coords.reshape(-1), live_total.reshape(1), tiles, gathered)


def on_device(
    features,
    tiles,
    tile_coords,
    tile_count,
    batch_mask,
    history,
    weight_one,
    bias_one,
    weight_two,
    bias_two,
):
    tile_set = tiles[0, 0]
    coord_set = tile_coords[0, 0]
    live_total = tile_count[0, 0]
    gathered_input = gather(features[0, 0], 0)
    summed_one = tile_products(gathered_input, tile_set, coord_set, live_total)
    owned_one = exchange(summed_one, "col", True, 1)
    owned_one = owned_one.astype(jnp.float32).sum(axis=0)
    agg_one = (features[0, 0].astype(jnp.float32) + owned_one).astype(jnp.bfloat16)
    pre_one = jnp.dot(agg_one, weight_one, preferred_element_type=jnp.float32) + bias_one
    hidden = jax.nn.relu(pre_one).astype(jnp.bfloat16)
    pushed = jnp.where(batch_mask[0, 0][:, None] == 1, hidden, history[0, 0])
    projected = jnp.dot(pushed, weight_two, preferred_element_type=jnp.float32).astype(jnp.bfloat16)
    gathered_proj = gather(projected.T, 2)
    summed_two = tile_products(gathered_proj, tile_set, coord_set, live_total, True)
    owned_two = exchange(summed_two, "col", True, 3).astype(jnp.float32).sum(axis=0).T
    scores = projected.astype(jnp.float32) + owned_two + bias_two
    return (pushed[None, None], scores[None, None])


def solution(mesh):
    return jax.shard_map(
        on_device,
        mesh=mesh,
        in_specs=(
            P("row", "col", None, None),
            P("row", "col", None, None, None),
            P("row", "col", None, None),
            P("row", "col"),
            P("row", "col", None),
            P("row", "col", None, None),
            P(),
            P(),
            P(),
            P(),
        ),
        out_specs=(P("row", "col", None, None), P("row", "col", None, None)),
        check_vma=False,
    )
```

```python
import functools

import jax
import jax.numpy as jnp
from jax import lax
from jax.experimental import pallas as pl
from jax.experimental.pallas import tpu as pltpu
from jax.sharding import PartitionSpec as P

MESH_ID = pl.DeviceIdType.MESH


def exchange_kernel(axis, other_axis, n, spread, src_ref, out_ref, send_sem, recv_sem):
    me = lax.axis_index(axis)
    other = lax.axis_index(other_axis)

    def device(k):
        return (k, other) if axis == "row" else (other, k)

    def outgoing(k):
        source = src_ref.at[k] if spread else src_ref
        return pltpu.make_async_remote_copy(
            src_ref=source,
            dst_ref=out_ref.at[me],
            send_sem=send_sem.at[k],
            recv_sem=recv_sem.at[me],
            device_id=device(k),
            device_id_type=MESH_ID,
        )

    def incoming(k):
        source = src_ref.at[k] if spread else src_ref
        return pltpu.make_async_remote_copy(
            src_ref=source,
            dst_ref=out_ref.at[k],
            send_sem=send_sem.at[k],
            recv_sem=recv_sem.at[k],
            device_id=device(k),
            device_id_type=MESH_ID,
        )

    barrier = pltpu.get_barrier_semaphore()

    def greet(step, carry):
        k = lax.rem(me + step, n)
        pl.semaphore_signal(barrier, 1, device_id=device(k), device_id_type=MESH_ID)
        return carry

    lax.fori_loop(1, n, greet, 0)
    pl.semaphore_wait(barrier, n - 1)

    def send(step, carry):
        outgoing(lax.rem(me + step, n)).start()
        return carry

    lax.fori_loop(1, n, send, 0)
    out_ref[me] = src_ref[me] if spread else src_ref[...]

    def finish(step, carry):
        k = lax.rem(me + step, n)
        outgoing(k).wait_send()
        incoming(lax.rem(me + n - step, n)).wait_recv()
        return carry

    lax.fori_loop(1, n, finish, 0)


def row_partners():
    me = lax.axis_index("row")
    return me, lax.axis_index("col"), me + 1 - 2 * lax.rem(me, 2)


def row_greet(barrier, n):
    me, other, twin = row_partners()
    pl.semaphore_signal(barrier, 1, device_id=(twin, other), device_id_type=MESH_ID)

    def greet(step, carry):
        peer = lax.rem(me + 2 * step, n)
        pl.semaphore_signal(barrier, 1, device_id=(peer, other), device_id_type=MESH_ID)
        return carry

    lax.fori_loop(1, n // 2, greet, 0)
    return n // 2


def row_transfer(n, src_ref, out_ref, send_sem, pass_sem, recv_sem):
    me, other, twin = row_partners()
    half = n // 2

    def copy(source, slot, sems, k):
        return pltpu.make_async_remote_copy(
            src_ref=source,
            dst_ref=out_ref.at[slot],
            send_sem=sems.at[k],
            recv_sem=recv_sem.at[slot],
            device_id=(k, other),
            device_id_type=MESH_ID,
        )

    def peer(step):
        return lax.rem(me + 2 * step, n)

    def far(step):
        return lax.rem(twin + 2 * step, n)

    def send(step, carry):
        copy(src_ref, me, send_sem, peer(step)).start()
        return carry

    lax.fori_loop(1, half, send, 0)
    copy(src_ref, me, send_sem, twin).start()

    def relay(step, carry):
        k = peer(step)
        copy(src_ref, k, send_sem, k).wait_recv()
        copy(out_ref.at[k], k, pass_sem, twin).start()
        return carry

    lax.fori_loop(1, half, relay, 0)

    def finish(step, carry):
        k = peer(step)
        copy(src_ref, me, send_sem, k).wait_send()
        copy(out_ref.at[k], k, pass_sem, twin).wait_send()
        copy(src_ref, far(step), send_sem, twin).wait_recv()
        return carry

    lax.fori_loop(1, half, finish, 0)
    copy(src_ref, me, send_sem, twin).wait_send()
    copy(src_ref, twin, send_sem, twin).wait_recv()


def gather_kernel(n, src_ref, out_ref, send_sem, pass_sem, recv_sem):
    barrier = pltpu.get_barrier_semaphore()
    pl.semaphore_wait(barrier, row_greet(barrier, n))
    out_ref[lax.axis_index("row")] = src_ref[...]
    row_transfer(n, src_ref, out_ref, send_sem, pass_sem, recv_sem)


def gather(block, tag):
    n = lax.axis_size("row")
    vmem = pl.BlockSpec(memory_space=pltpu.VMEM)
    return pl.pallas_call(
        functools.partial(gather_kernel, n),
        out_shape=jax.ShapeDtypeStruct((n, *block.shape), block.dtype),
        in_specs=[vmem],
        out_specs=vmem,
        scratch_shapes=[pltpu.SemaphoreType.DMA((n,))] * 3,
        compiler_params=pltpu.CompilerParams(collective_id=tag, has_side_effects=True),
    )(block)


def middle_kernel(
    n_row,
    n_col,
    parts_ref,
    features_ref,
    weight_one_ref,
    bias_one_ref,
    mask_ref,
    history_ref,
    weight_two_ref,
    pushed_ref,
    out_ref,
    landing_ref,
    col_send,
    col_recv,
    send_sem,
    pass_sem,
    recv_sem,
):
    row = lax.axis_index("row")
    me = lax.axis_index("col")

    def col_copy(k, slot):
        return pltpu.make_async_remote_copy(
            src_ref=parts_ref.at[k],
            dst_ref=landing_ref.at[slot],
            send_sem=col_send.at[k],
            recv_sem=col_recv.at[slot],
            device_id=(row, k),
            device_id_type=MESH_ID,
        )

    barrier = pltpu.get_barrier_semaphore()

    def greet(step, carry):
        k = lax.rem(me + step, n_col)
        pl.semaphore_signal(barrier, 1, device_id=(row, k), device_id_type=MESH_ID)
        return carry

    lax.fori_loop(1, n_col, greet, 0)
    expected = row_greet(barrier, n_row)
    pl.semaphore_wait(barrier, n_col - 1 + expected)

    def send(step, carry):
        col_copy(lax.rem(me + step, n_col), me).start()
        return carry

    lax.fori_loop(1, n_col, send, 0)
    landing_ref[me] = parts_ref[me]

    def finish(step, carry):
        col_copy(lax.rem(me + step, n_col), me).wait_send()
        col_copy(me, lax.rem(me + n_col - step, n_col)).wait_recv()
        return carry

    lax.fori_loop(1, n_col, finish, 0)
    total = features_ref[...].astype(jnp.float32)
    for k in range(n_col):
        total = total + landing_ref[k].astype(jnp.float32)
    agg = total.astype(jnp.bfloat16)
    pre = jnp.dot(agg, weight_one_ref[...], preferred_element_type=jnp.float32)
    hidden = jnp.maximum(pre + bias_one_ref[...], 0.0).astype(jnp.bfloat16)
    pushed = jnp.where(mask_ref[...] == 1, hidden, history_ref[...])
    pushed_ref[...] = pushed
    projected = lax.dot_general(
        weight_two_ref[...], pushed, (((1,), (1,)), ((), ())), preferred_element_type=jnp.float32
    )
    out_ref[row] = projected.astype(out_ref.dtype)
    row_transfer(n_row, out_ref.at[row], out_ref, send_sem, pass_sem, recv_sem)


def middle(parts, features, weight_one, bias_one, mask, history, weight_two, tag):
    n_row = lax.axis_size("row")
    n_col = lax.axis_size("col")
    classes = weight_two.shape[1]
    nodes = features.shape[0]
    vmem = pl.BlockSpec(memory_space=pltpu.VMEM)
    return pl.pallas_call(
        functools.partial(middle_kernel, n_row, n_col),
        out_shape=(
            jax.ShapeDtypeStruct(history.shape, history.dtype),
            jax.ShapeDtypeStruct((n_row, classes, nodes), jnp.bfloat16),
        ),
        in_specs=[vmem] * 7,
        out_specs=(vmem, vmem),
        scratch_shapes=[
            pltpu.VMEM(parts.shape, parts.dtype),
            pltpu.SemaphoreType.DMA((n_col,)),
            pltpu.SemaphoreType.DMA((n_col,)),
        ]
        + [pltpu.SemaphoreType.DMA((n_row,))] * 3,
        compiler_params=pltpu.CompilerParams(collective_id=tag, has_side_effects=True),
    )(
        parts,
        features,
        weight_one,
        bias_one.reshape(1, -1),
        mask.reshape(-1, 1),
        history,
        weight_two.T,
    )


def exchange(block, axis, spread, tag):
    other_axis = "col" if axis == "row" else "row"
    n = lax.axis_size(axis)
    shape = block.shape[1:] if spread else block.shape
    vmem = pl.BlockSpec(memory_space=pltpu.VMEM)
    return pl.pallas_call(
        functools.partial(exchange_kernel, axis, other_axis, n, spread),
        out_shape=jax.ShapeDtypeStruct((n, *shape), block.dtype),
        in_specs=[vmem],
        out_specs=vmem,
        scratch_shapes=[pltpu.SemaphoreType.DMA((n,)), pltpu.SemaphoreType.DMA((n,))],
        compiler_params=pltpu.CompilerParams(collective_id=tag, has_side_effects=True),
    )(block)


def joined_along(tiles, dim):
    tiles = jnp.moveaxis(tiles, 0, dim)
    lengths = tiles.shape
    return tiles.reshape(*lengths[:dim], lengths[dim] * lengths[dim + 1], *lengths[dim + 2 :])


def copy_for_each(shard, axis):
    copies = jnp.broadcast_to(shard, (lax.axis_size(axis), *shard.shape))
    return lax.all_to_all(copies, axis, split_axis=0, concat_axis=0, tiled=True)


def collect(shard, axis, dim):
    return joined_along(copy_for_each(shard, axis), dim)


def in_blocks(shard, dim, size):
    lengths = shard.shape
    tiles = shard.reshape(*lengths[:dim], size, lengths[dim] // size, *lengths[dim + 1 :])
    return jnp.moveaxis(tiles, dim, 0)


def sent_and_summed(shard, axis, dim):
    tiles = in_blocks(shard, dim, lax.axis_size(axis))
    arrived = lax.all_to_all(tiles, axis, split_axis=0, concat_axis=0, tiled=True)
    return arrived.astype(jnp.float32).sum(axis=0)


def products_kernel(
    flipped, pack, coords_ref, count_ref, tiles_ref, gathered_ref, out_ref, order_ref, bounds_ref, cursor_ref
):
    blocks = out_ref.shape[0]
    live = count_ref[0]
    for target in range(blocks + 1):
        bounds_ref[target] = 0

    def count(slot, carry):
        target = coords_ref[2 * slot]
        bounds_ref[target + 1] = bounds_ref[target + 1] + 1
        return carry

    lax.fori_loop(0, live, count, 0)
    for target in range(blocks):
        bounds_ref[target + 1] = bounds_ref[target + 1] + bounds_ref[target]
        cursor_ref[target] = bounds_ref[target]

    def place(slot, carry):
        target = coords_ref[2 * slot]
        position = cursor_ref[target]
        order_ref[position] = slot
        cursor_ref[target] = position + 1
        return carry

    lax.fori_loop(0, live, place, 0)

    def product(first, end, total):
        tiles, sources = [], []
        for offset in range(pack):
            slot = order_ref[jnp.minimum(first + offset, end - 1)]
            tile = tiles_ref[slot]
            tiles.append(jnp.where(first + offset < end, tile, jnp.zeros_like(tile)))
            sources.append(gathered_ref[coords_ref[2 * slot + 1]])
        if flipped:
            return total + lax.dot_general(
                jnp.concatenate(sources, axis=1),
                jnp.concatenate(tiles, axis=1),
                (((1,), (1,)), ((), ())),
                preferred_element_type=jnp.float32,
            )
        return total + jnp.dot(
            jnp.concatenate(tiles, axis=1),
            jnp.concatenate(sources, axis=0),
            preferred_element_type=jnp.float32,
        )

    for target in range(blocks):
        first, end = bounds_ref[target], bounds_ref[target + 1]
        total = lax.fori_loop(
            0,
            (end - first + pack - 1) // pack,
            lambda step, total: product(first + step * pack, end, total),
            jnp.zeros(out_ref.shape[1:], jnp.float32),
        )
        out_ref[target] = total.astype(out_ref.dtype)


def tile_products(gathered, tiles, coords, live_total, flipped=False, pack=8):
    row_blocks = lax.axis_size("col")
    slots = tiles.shape[0]
    block_shape = gathered.shape[1:]
    vmem = pl.BlockSpec(memory_space=pltpu.VMEM)
    smem = pl.BlockSpec(memory_space=pltpu.SMEM)
    return pl.pallas_call(
        functools.partial(products_kernel, flipped, pack),
        in_specs=[smem, smem, vmem, vmem],
        out_specs=vmem,
        out_shape=jax.ShapeDtypeStruct((row_blocks, *block_shape), jnp.bfloat16),
        scratch_shapes=[
            pltpu.SMEM((slots,), jnp.int32),
            pltpu.SMEM((row_blocks + 1,), jnp.int32),
            pltpu.SMEM((row_blocks,), jnp.int32),
        ],
    )(coords.reshape(-1), live_total.reshape(1), tiles, gathered)


def on_device(
    features,
    tiles,
    tile_coords,
    tile_count,
    batch_mask,
    history,
    weight_one,
    bias_one,
    weight_two,
    bias_two,
):
    tile_set = tiles[0, 0]
    coord_set = tile_coords[0, 0]
    live_total = tile_count[0, 0]
    gathered_input = gather(features[0, 0], 0)
    summed_one = tile_products(gathered_input, tile_set, coord_set, live_total)
    pushed, gathered_proj = middle(
        summed_one,
        features[0, 0],
        weight_one,
        bias_one,
        batch_mask[0, 0],
        history[0, 0],
        weight_two,
        1,
    )
    summed_two = tile_products(gathered_proj, tile_set, coord_set, live_total, True)
    owned_two = exchange(summed_two, "col", True, 3).astype(jnp.float32).sum(axis=0)
    own_block = gathered_proj[lax.axis_index("row")].astype(jnp.float32)
    scores = (own_block + owned_two).T + bias_two
    return (pushed[None, None], scores[None, None])


def solution(mesh):
    return jax.shard_map(
        on_device,
        mesh=mesh,
        in_specs=(
            P("row", "col", None, None),
            P("row", "col", None, None, None),
            P("row", "col", None, None),
            P("row", "col"),
            P("row", "col", None),
            P("row", "col", None, None),
            P(),
            P(),
            P(),
            P(),
        ),
        out_specs=(P("row", "col", None, None), P("row", "col", None, None)),
        check_vma=False,
    )
```

```python
import functools

import jax
import jax.numpy as jnp
from jax import lax
from jax.experimental import pallas as pl
from jax.experimental.pallas import tpu as pltpu
from jax.sharding import PartitionSpec as P

MESH_ID = pl.DeviceIdType.MESH


def exchange_kernel(axis, other_axis, n, spread, src_ref, out_ref, send_sem, recv_sem):
    me = lax.axis_index(axis)
    other = lax.axis_index(other_axis)

    def device(k):
        return (k, other) if axis == "row" else (other, k)

    def outgoing(k):
        source = src_ref.at[k] if spread else src_ref
        return pltpu.make_async_remote_copy(
            src_ref=source,
            dst_ref=out_ref.at[me],
            send_sem=send_sem.at[k],
            recv_sem=recv_sem.at[me],
            device_id=device(k),
            device_id_type=MESH_ID,
        )

    def incoming(k):
        source = src_ref.at[k] if spread else src_ref
        return pltpu.make_async_remote_copy(
            src_ref=source,
            dst_ref=out_ref.at[k],
            send_sem=send_sem.at[k],
            recv_sem=recv_sem.at[k],
            device_id=device(k),
            device_id_type=MESH_ID,
        )

    barrier = pltpu.get_barrier_semaphore()

    def greet(step, carry):
        k = lax.rem(me + step, n)
        pl.semaphore_signal(barrier, 1, device_id=device(k), device_id_type=MESH_ID)
        return carry

    lax.fori_loop(1, n, greet, 0)
    pl.semaphore_wait(barrier, n - 1)

    def send(step, carry):
        outgoing(lax.rem(me + step, n)).start()
        return carry

    lax.fori_loop(1, n, send, 0)
    out_ref[me] = src_ref[me] if spread else src_ref[...]

    def finish(step, carry):
        k = lax.rem(me + step, n)
        outgoing(k).wait_send()
        incoming(lax.rem(me + n - step, n)).wait_recv()
        return carry

    lax.fori_loop(1, n, finish, 0)


def row_partners():
    me = lax.axis_index("row")
    return me, lax.axis_index("col"), me + 1 - 2 * lax.rem(me, 2)


def row_greet(barrier, n):
    me, other, twin = row_partners()
    pl.semaphore_signal(barrier, 1, device_id=(twin, other), device_id_type=MESH_ID)

    def greet(step, carry):
        peer = lax.rem(me + 2 * step, n)
        pl.semaphore_signal(barrier, 1, device_id=(peer, other), device_id_type=MESH_ID)
        return carry

    lax.fori_loop(1, n // 2, greet, 0)
    return n // 2


def row_transfer(n, src_ref, out_ref, send_sem, pass_sem, recv_sem):
    me, other, twin = row_partners()
    half = n // 2

    def copy(source, slot, sems, k):
        return pltpu.make_async_remote_copy(
            src_ref=source,
            dst_ref=out_ref.at[slot],
            send_sem=sems.at[k],
            recv_sem=recv_sem.at[slot],
            device_id=(k, other),
            device_id_type=MESH_ID,
        )

    def peer(step):
        return lax.rem(me + 2 * step, n)

    def far(step):
        return lax.rem(twin + 2 * step, n)

    def send(step, carry):
        copy(src_ref, me, send_sem, peer(step)).start()
        return carry

    lax.fori_loop(1, half, send, 0)
    copy(src_ref, me, send_sem, twin).start()

    def relay(step, carry):
        k = peer(step)
        copy(src_ref, k, send_sem, k).wait_recv()
        copy(out_ref.at[k], k, pass_sem, twin).start()
        return carry

    lax.fori_loop(1, half, relay, 0)

    def finish(step, carry):
        k = peer(step)
        copy(src_ref, me, send_sem, k).wait_send()
        copy(out_ref.at[k], k, pass_sem, twin).wait_send()
        copy(src_ref, far(step), send_sem, twin).wait_recv()
        return carry

    lax.fori_loop(1, half, finish, 0)
    copy(src_ref, me, send_sem, twin).wait_send()
    copy(src_ref, twin, send_sem, twin).wait_recv()


def gather_kernel(n, src_ref, out_ref, send_sem, pass_sem, recv_sem):
    barrier = pltpu.get_barrier_semaphore()
    pl.semaphore_wait(barrier, row_greet(barrier, n))
    out_ref[lax.axis_index("row")] = src_ref[...]
    row_transfer(n, src_ref, out_ref, send_sem, pass_sem, recv_sem)


def gather(block, tag):
    n = lax.axis_size("row")
    vmem = pl.BlockSpec(memory_space=pltpu.VMEM)
    return pl.pallas_call(
        functools.partial(gather_kernel, n),
        out_shape=jax.ShapeDtypeStruct((n, *block.shape), block.dtype),
        in_specs=[vmem],
        out_specs=vmem,
        scratch_shapes=[pltpu.SemaphoreType.DMA((n,))] * 3,
        compiler_params=pltpu.CompilerParams(collective_id=tag, has_side_effects=True),
    )(block)


def middle_kernel(
    n_row,
    n_col,
    parts_ref,
    features_ref,
    weight_one_ref,
    bias_one_ref,
    mask_ref,
    history_ref,
    weight_two_ref,
    pushed_ref,
    out_ref,
    own_ref,
    landing_ref,
    col_send,
    col_recv,
    send_sem,
    pass_sem,
    recv_sem,
):
    row = lax.axis_index("row")
    me = lax.axis_index("col")

    def col_copy(k, slot):
        return pltpu.make_async_remote_copy(
            src_ref=parts_ref.at[k],
            dst_ref=landing_ref.at[slot],
            send_sem=col_send.at[k],
            recv_sem=col_recv.at[slot],
            device_id=(row, k),
            device_id_type=MESH_ID,
        )

    barrier = pltpu.get_barrier_semaphore()

    def greet(step, carry):
        k = lax.rem(me + step, n_col)
        pl.semaphore_signal(barrier, 1, device_id=(row, k), device_id_type=MESH_ID)
        return carry

    lax.fori_loop(1, n_col, greet, 0)
    expected = row_greet(barrier, n_row)
    pl.semaphore_wait(barrier, n_col - 1 + expected)

    def send(step, carry):
        col_copy(lax.rem(me + step, n_col), me).start()
        return carry

    lax.fori_loop(1, n_col, send, 0)
    landing_ref[me] = parts_ref[me]

    def finish(step, carry):
        col_copy(lax.rem(me + step, n_col), me).wait_send()
        col_copy(me, lax.rem(me + n_col - step, n_col)).wait_recv()
        return carry

    lax.fori_loop(1, n_col, finish, 0)
    total = features_ref[...].astype(jnp.float32)
    for k in range(n_col):
        total = total + landing_ref[k].astype(jnp.float32)
    agg = total.astype(jnp.bfloat16)
    pre = jnp.dot(agg, weight_one_ref[...], preferred_element_type=jnp.float32)
    hidden = jnp.maximum(pre + bias_one_ref[...], 0.0).astype(jnp.bfloat16)
    pushed = jnp.where(mask_ref[...] == 1, hidden, history_ref[...])
    pushed_ref[...] = pushed
    projected = lax.dot_general(
        weight_two_ref[...], pushed, (((1,), (1,)), ((), ())), preferred_element_type=jnp.float32
    )
    own_ref[...] = projected.astype(own_ref.dtype)
    out_ref[row] = own_ref[...]
    row_transfer(n_row, out_ref.at[row], out_ref, send_sem, pass_sem, recv_sem)


def middle(parts, features, weight_one, bias_one, mask, history, weight_two, tag):
    n_row = lax.axis_size("row")
    n_col = lax.axis_size("col")
    classes = weight_two.shape[1]
    nodes = features.shape[0]
    vmem = pl.BlockSpec(memory_space=pltpu.VMEM)
    return pl.pallas_call(
        functools.partial(middle_kernel, n_row, n_col),
        out_shape=(
            jax.ShapeDtypeStruct(history.shape, history.dtype),
            jax.ShapeDtypeStruct((n_row, classes, nodes), jnp.bfloat16),
            jax.ShapeDtypeStruct((classes, nodes), jnp.bfloat16),
        ),
        in_specs=[vmem] * 7,
        out_specs=(vmem, vmem, vmem),
        scratch_shapes=[
            pltpu.VMEM(parts.shape, parts.dtype),
            pltpu.SemaphoreType.DMA((n_col,)),
            pltpu.SemaphoreType.DMA((n_col,)),
        ]
        + [pltpu.SemaphoreType.DMA((n_row,))] * 3,
        compiler_params=pltpu.CompilerParams(collective_id=tag, has_side_effects=True),
    )(
        parts,
        features,
        weight_one,
        bias_one.reshape(1, -1),
        mask.reshape(-1, 1),
        history,
        weight_two.T,
    )


def exchange(block, axis, spread, tag):
    other_axis = "col" if axis == "row" else "row"
    n = lax.axis_size(axis)
    shape = block.shape[1:] if spread else block.shape
    vmem = pl.BlockSpec(memory_space=pltpu.VMEM)
    return pl.pallas_call(
        functools.partial(exchange_kernel, axis, other_axis, n, spread),
        out_shape=jax.ShapeDtypeStruct((n, *shape), block.dtype),
        in_specs=[vmem],
        out_specs=vmem,
        scratch_shapes=[pltpu.SemaphoreType.DMA((n,)), pltpu.SemaphoreType.DMA((n,))],
        compiler_params=pltpu.CompilerParams(collective_id=tag, has_side_effects=True),
    )(block)


def joined_along(tiles, dim):
    tiles = jnp.moveaxis(tiles, 0, dim)
    lengths = tiles.shape
    return tiles.reshape(*lengths[:dim], lengths[dim] * lengths[dim + 1], *lengths[dim + 2 :])


def copy_for_each(shard, axis):
    copies = jnp.broadcast_to(shard, (lax.axis_size(axis), *shard.shape))
    return lax.all_to_all(copies, axis, split_axis=0, concat_axis=0, tiled=True)


def collect(shard, axis, dim):
    return joined_along(copy_for_each(shard, axis), dim)


def in_blocks(shard, dim, size):
    lengths = shard.shape
    tiles = shard.reshape(*lengths[:dim], size, lengths[dim] // size, *lengths[dim + 1 :])
    return jnp.moveaxis(tiles, dim, 0)


def sent_and_summed(shard, axis, dim):
    tiles = in_blocks(shard, dim, lax.axis_size(axis))
    arrived = lax.all_to_all(tiles, axis, split_axis=0, concat_axis=0, tiled=True)
    return arrived.astype(jnp.float32).sum(axis=0)


def final_kernel(n, parts_ref, own_ref, out_ref, landing_ref, send_sem, recv_sem):
    exchange_kernel("col", "row", n, True, parts_ref, landing_ref, send_sem, recv_sem)
    total = own_ref[...].astype(jnp.float32)
    for k in range(n):
        total = total + landing_ref[k].astype(jnp.float32)
    out_ref[...] = total


def final_sum(parts, own, tag):
    n = lax.axis_size("col")
    vmem = pl.BlockSpec(memory_space=pltpu.VMEM)
    return pl.pallas_call(
        functools.partial(final_kernel, n),
        out_shape=jax.ShapeDtypeStruct(own.shape, jnp.float32),
        in_specs=[vmem, vmem],
        out_specs=vmem,
        scratch_shapes=[
            pltpu.VMEM(parts.shape, parts.dtype),
            pltpu.SemaphoreType.DMA((n,)),
            pltpu.SemaphoreType.DMA((n,)),
        ],
        compiler_params=pltpu.CompilerParams(collective_id=tag, has_side_effects=True),
    )(parts, own)


def products_kernel(
    flipped, pack, coords_ref, count_ref, tiles_ref, gathered_ref, out_ref, order_ref, bounds_ref, cursor_ref
):
    blocks = out_ref.shape[0]
    live = count_ref[0]
    for target in range(blocks + 1):
        bounds_ref[target] = 0

    def count(slot, carry):
        target = coords_ref[2 * slot]
        bounds_ref[target + 1] = bounds_ref[target + 1] + 1
        return carry

    lax.fori_loop(0, live, count, 0)
    for target in range(blocks):
        bounds_ref[target + 1] = bounds_ref[target + 1] + bounds_ref[target]
        cursor_ref[target] = bounds_ref[target]

    def place(slot, carry):
        target = coords_ref[2 * slot]
        position = cursor_ref[target]
        order_ref[position] = slot
        cursor_ref[target] = position + 1
        return carry

    lax.fori_loop(0, live, place, 0)

    def product(first, end, total):
        tiles, sources = [], []
        for offset in range(pack):
            slot = order_ref[jnp.minimum(first + offset, end - 1)]
            tile = tiles_ref[slot]
            tiles.append(jnp.where(first + offset < end, tile, jnp.zeros_like(tile)))
            sources.append(gathered_ref[coords_ref[2 * slot + 1]])
        if flipped:
            return total + lax.dot_general(
                jnp.concatenate(sources, axis=1),
                jnp.concatenate(tiles, axis=1),
                (((1,), (1,)), ((), ())),
                preferred_element_type=jnp.float32,
            )
        return total + jnp.dot(
            jnp.concatenate(tiles, axis=1),
            jnp.concatenate(sources, axis=0),
            preferred_element_type=jnp.float32,
        )

    for target in range(blocks):
        first, end = bounds_ref[target], bounds_ref[target + 1]
        total = lax.fori_loop(
            0,
            (end - first + pack - 1) // pack,
            lambda step, total: product(first + step * pack, end, total),
            jnp.zeros(out_ref.shape[1:], jnp.float32),
        )
        out_ref[target] = total.astype(out_ref.dtype)


def tile_products(gathered, tiles, coords, live_total, flipped=False, pack=8):
    row_blocks = lax.axis_size("col")
    slots = tiles.shape[0]
    block_shape = gathered.shape[1:]
    vmem = pl.BlockSpec(memory_space=pltpu.VMEM)
    smem = pl.BlockSpec(memory_space=pltpu.SMEM)
    return pl.pallas_call(
        functools.partial(products_kernel, flipped, pack),
        in_specs=[smem, smem, vmem, vmem],
        out_specs=vmem,
        out_shape=jax.ShapeDtypeStruct((row_blocks, *block_shape), jnp.bfloat16),
        scratch_shapes=[
            pltpu.SMEM((slots,), jnp.int32),
            pltpu.SMEM((row_blocks + 1,), jnp.int32),
            pltpu.SMEM((row_blocks,), jnp.int32),
        ],
    )(coords.reshape(-1), live_total.reshape(1), tiles, gathered)


def on_device(
    features,
    tiles,
    tile_coords,
    tile_count,
    batch_mask,
    history,
    weight_one,
    bias_one,
    weight_two,
    bias_two,
):
    tile_set = tiles[0, 0]
    coord_set = tile_coords[0, 0]
    live_total = tile_count[0, 0]
    gathered_input = gather(features[0, 0], 0)
    summed_one = tile_products(gathered_input, tile_set, coord_set, live_total)
    pushed, gathered_proj, own_block = middle(
        summed_one,
        features[0, 0],
        weight_one,
        bias_one,
        batch_mask[0, 0],
        history[0, 0],
        weight_two,
        1,
    )
    summed_two = tile_products(gathered_proj, tile_set, coord_set, live_total, True)
    scores = final_sum(summed_two, own_block, 3).T + bias_two
    return (pushed[None, None], scores[None, None])


def solution(mesh):
    return jax.shard_map(
        on_device,
        mesh=mesh,
        in_specs=(
            P("row", "col", None, None),
            P("row", "col", None, None, None),
            P("row", "col", None, None),
            P("row", "col"),
            P("row", "col", None),
            P("row", "col", None, None),
            P(),
            P(),
            P(),
            P(),
        ),
        out_specs=(P("row", "col", None, None), P("row", "col", None, None)),
        check_vma=False,
    )
```

```python
import functools

import jax
import jax.numpy as jnp
from jax import lax
from jax.experimental import pallas as pl
from jax.experimental.pallas import tpu as pltpu
from jax.sharding import PartitionSpec as P

MESH_ID = pl.DeviceIdType.MESH


def exchange_kernel(axis, other_axis, n, spread, src_ref, out_ref, send_sem, recv_sem):
    me = lax.axis_index(axis)
    other = lax.axis_index(other_axis)

    def device(k):
        return (k, other) if axis == "row" else (other, k)

    def outgoing(k):
        source = src_ref.at[k] if spread else src_ref
        return pltpu.make_async_remote_copy(
            src_ref=source,
            dst_ref=out_ref.at[me],
            send_sem=send_sem.at[k],
            recv_sem=recv_sem.at[me],
            device_id=device(k),
            device_id_type=MESH_ID,
        )

    def incoming(k):
        source = src_ref.at[k] if spread else src_ref
        return pltpu.make_async_remote_copy(
            src_ref=source,
            dst_ref=out_ref.at[k],
            send_sem=send_sem.at[k],
            recv_sem=recv_sem.at[k],
            device_id=device(k),
            device_id_type=MESH_ID,
        )

    barrier = pltpu.get_barrier_semaphore()

    def greet(step, carry):
        k = lax.rem(me + step, n)
        pl.semaphore_signal(barrier, 1, device_id=device(k), device_id_type=MESH_ID)
        return carry

    lax.fori_loop(1, n, greet, 0)
    pl.semaphore_wait(barrier, n - 1)

    def send(step, carry):
        outgoing(lax.rem(me + step, n)).start()
        return carry

    lax.fori_loop(1, n, send, 0)
    out_ref[me] = src_ref[me] if spread else src_ref[...]

    def finish(step, carry):
        k = lax.rem(me + step, n)
        outgoing(k).wait_send()
        incoming(lax.rem(me + n - step, n)).wait_recv()
        return carry

    lax.fori_loop(1, n, finish, 0)


def row_partners():
    me = lax.axis_index("row")
    return me, lax.axis_index("col"), me + 1 - 2 * lax.rem(me, 2)


def row_greet(barrier, n):
    me, other, twin = row_partners()
    pl.semaphore_signal(barrier, 1, device_id=(twin, other), device_id_type=MESH_ID)

    def greet(step, carry):
        peer = lax.rem(me + 2 * step, n)
        pl.semaphore_signal(barrier, 1, device_id=(peer, other), device_id_type=MESH_ID)
        return carry

    lax.fori_loop(1, n // 2, greet, 0)
    return n // 2


def row_transfer(n, src_ref, out_ref, send_sem, pass_sem, recv_sem):
    me, other, twin = row_partners()
    half = n // 2

    def copy(source, slot, sems, k):
        return pltpu.make_async_remote_copy(
            src_ref=source,
            dst_ref=out_ref.at[slot],
            send_sem=sems.at[k],
            recv_sem=recv_sem.at[slot],
            device_id=(k, other),
            device_id_type=MESH_ID,
        )

    def peer(step):
        return lax.rem(me + 2 * step, n)

    def far(step):
        return lax.rem(twin + 2 * step, n)

    def send(step, carry):
        copy(src_ref, me, send_sem, peer(step)).start()
        return carry

    lax.fori_loop(1, half, send, 0)
    copy(src_ref, me, send_sem, twin).start()

    def relay(step, carry):
        k = peer(step)
        copy(src_ref, k, send_sem, k).wait_recv()
        copy(out_ref.at[k], k, pass_sem, twin).start()
        return carry

    lax.fori_loop(1, half, relay, 0)

    def finish(step, carry):
        k = peer(step)
        copy(src_ref, me, send_sem, k).wait_send()
        copy(out_ref.at[k], k, pass_sem, twin).wait_send()
        copy(src_ref, far(step), send_sem, twin).wait_recv()
        return carry

    lax.fori_loop(1, half, finish, 0)
    copy(src_ref, me, send_sem, twin).wait_send()
    copy(src_ref, twin, send_sem, twin).wait_recv()


def gather_kernel(n, src_ref, out_ref, send_sem, pass_sem, recv_sem):
    barrier = pltpu.get_barrier_semaphore()
    pl.semaphore_wait(barrier, row_greet(barrier, n))
    out_ref[lax.axis_index("row")] = src_ref[...]
    row_transfer(n, src_ref, out_ref, send_sem, pass_sem, recv_sem)


def gather(block, tag):
    n = lax.axis_size("row")
    vmem = pl.BlockSpec(memory_space=pltpu.VMEM)
    return pl.pallas_call(
        functools.partial(gather_kernel, n),
        out_shape=jax.ShapeDtypeStruct((n, *block.shape), block.dtype),
        in_specs=[vmem],
        out_specs=vmem,
        scratch_shapes=[pltpu.SemaphoreType.DMA((n,))] * 3,
        compiler_params=pltpu.CompilerParams(collective_id=tag, has_side_effects=True),
    )(block)


def middle_kernel(
    n_row,
    n_col,
    parts_ref,
    features_ref,
    weight_one_ref,
    bias_one_ref,
    mask_ref,
    history_ref,
    weight_two_ref,
    pushed_ref,
    out_ref,
    landing_ref,
    col_send,
    col_recv,
    send_sem,
    pass_sem,
    recv_sem,
):
    row = lax.axis_index("row")
    me = lax.axis_index("col")

    def col_copy(k, slot):
        return pltpu.make_async_remote_copy(
            src_ref=parts_ref.at[k],
            dst_ref=landing_ref.at[slot],
            send_sem=col_send.at[k],
            recv_sem=col_recv.at[slot],
            device_id=(row, k),
            device_id_type=MESH_ID,
        )

    barrier = pltpu.get_barrier_semaphore()

    def greet(step, carry):
        k = lax.rem(me + step, n_col)
        pl.semaphore_signal(barrier, 1, device_id=(row, k), device_id_type=MESH_ID)
        return carry

    lax.fori_loop(1, n_col, greet, 0)
    expected = row_greet(barrier, n_row)
    pl.semaphore_wait(barrier, n_col - 1 + expected)

    def send(step, carry):
        col_copy(lax.rem(me + step, n_col), me).start()
        return carry

    lax.fori_loop(1, n_col, send, 0)
    landing_ref[me] = parts_ref[me]

    def finish(step, carry):
        col_copy(lax.rem(me + step, n_col), me).wait_send()
        col_copy(me, lax.rem(me + n_col - step, n_col)).wait_recv()
        return carry

    lax.fori_loop(1, n_col, finish, 0)
    total = features_ref[...].astype(jnp.float32)
    for k in range(n_col):
        total = total + landing_ref[k].astype(jnp.float32)
    agg = total.astype(jnp.bfloat16)
    pre = jnp.dot(agg, weight_one_ref[...], preferred_element_type=jnp.float32)
    hidden = jnp.maximum(pre + bias_one_ref[...], 0.0).astype(jnp.bfloat16)
    pushed = jnp.where(mask_ref[...] == 1, hidden, history_ref[...])
    pushed_ref[...] = pushed
    projected = lax.dot_general(
        weight_two_ref[...], pushed, (((1,), (1,)), ((), ())), preferred_element_type=jnp.float32
    )
    out_ref[row] = projected.astype(out_ref.dtype)
    row_transfer(n_row, out_ref.at[row], out_ref, send_sem, pass_sem, recv_sem)


def middle(parts, features, weight_one, bias_one, mask, history, weight_two, tag):
    n_row = lax.axis_size("row")
    n_col = lax.axis_size("col")
    classes = weight_two.shape[1]
    nodes = features.shape[0]
    vmem = pl.BlockSpec(memory_space=pltpu.VMEM)
    return pl.pallas_call(
        functools.partial(middle_kernel, n_row, n_col),
        out_shape=(
            jax.ShapeDtypeStruct(history.shape, history.dtype),
            jax.ShapeDtypeStruct((n_row, classes, nodes), jnp.bfloat16),
        ),
        in_specs=[vmem] * 7,
        out_specs=(vmem, vmem),
        scratch_shapes=[
            pltpu.VMEM(parts.shape, parts.dtype),
            pltpu.SemaphoreType.DMA((n_col,)),
            pltpu.SemaphoreType.DMA((n_col,)),
        ]
        + [pltpu.SemaphoreType.DMA((n_row,))] * 3,
        compiler_params=pltpu.CompilerParams(collective_id=tag, has_side_effects=True),
    )(
        parts,
        features,
        weight_one,
        bias_one.reshape(1, -1),
        mask.reshape(-1, 1),
        history,
        weight_two.T,
    )


def exchange(block, axis, spread, tag):
    other_axis = "col" if axis == "row" else "row"
    n = lax.axis_size(axis)
    shape = block.shape[1:] if spread else block.shape
    vmem = pl.BlockSpec(memory_space=pltpu.VMEM)
    return pl.pallas_call(
        functools.partial(exchange_kernel, axis, other_axis, n, spread),
        out_shape=jax.ShapeDtypeStruct((n, *shape), block.dtype),
        in_specs=[vmem],
        out_specs=vmem,
        scratch_shapes=[pltpu.SemaphoreType.DMA((n,)), pltpu.SemaphoreType.DMA((n,))],
        compiler_params=pltpu.CompilerParams(collective_id=tag, has_side_effects=True),
    )(block)


def joined_along(tiles, dim):
    tiles = jnp.moveaxis(tiles, 0, dim)
    lengths = tiles.shape
    return tiles.reshape(*lengths[:dim], lengths[dim] * lengths[dim + 1], *lengths[dim + 2 :])


def copy_for_each(shard, axis):
    copies = jnp.broadcast_to(shard, (lax.axis_size(axis), *shard.shape))
    return lax.all_to_all(copies, axis, split_axis=0, concat_axis=0, tiled=True)


def collect(shard, axis, dim):
    return joined_along(copy_for_each(shard, axis), dim)


def in_blocks(shard, dim, size):
    lengths = shard.shape
    tiles = shard.reshape(*lengths[:dim], size, lengths[dim] // size, *lengths[dim + 1 :])
    return jnp.moveaxis(tiles, dim, 0)


def sent_and_summed(shard, axis, dim):
    tiles = in_blocks(shard, dim, lax.axis_size(axis))
    arrived = lax.all_to_all(tiles, axis, split_axis=0, concat_axis=0, tiled=True)
    return arrived.astype(jnp.float32).sum(axis=0)


def products_kernel(
    flipped,
    pack,
    coords_ref,
    count_ref,
    tiles_hbm,
    gathered_ref,
    out_ref,
    order_ref,
    bounds_ref,
    cursor_ref,
    tiles_ref,
    load_sem,
):
    chunks = load_sem.shape[0]
    size = tiles_ref.shape[0] // chunks
    loads = [
        pltpu.make_async_copy(
            tiles_hbm.at[pl.ds(c * size, size)], tiles_ref.at[pl.ds(c * size, size)], load_sem.at[c]
        )
        for c in range(chunks)
    ]
    for load in loads:
        load.start()
    blocks = out_ref.shape[0]
    live = count_ref[0]
    for target in range(blocks + 1):
        bounds_ref[target] = 0

    def count(slot, carry):
        target = coords_ref[2 * slot]
        bounds_ref[target + 1] = bounds_ref[target + 1] + 1
        return carry

    lax.fori_loop(0, live, count, 0)
    for target in range(blocks):
        bounds_ref[target + 1] = bounds_ref[target + 1] + bounds_ref[target]
        cursor_ref[target] = bounds_ref[target]

    def place(slot, carry):
        target = coords_ref[2 * slot]
        position = cursor_ref[target]
        order_ref[position] = slot
        cursor_ref[target] = position + 1
        return carry

    lax.fori_loop(0, live, place, 0)
    for load in loads:
        load.wait()

    def product(first, end, total):
        tiles, sources = [], []
        for offset in range(pack):
            slot = order_ref[jnp.minimum(first + offset, end - 1)]
            tile = tiles_ref[slot]
            tiles.append(jnp.where(first + offset < end, tile, jnp.zeros_like(tile)))
            sources.append(gathered_ref[coords_ref[2 * slot + 1]])
        if flipped:
            return total + lax.dot_general(
                jnp.concatenate(sources, axis=1),
                jnp.concatenate(tiles, axis=1),
                (((1,), (1,)), ((), ())),
                preferred_element_type=jnp.float32,
            )
        return total + jnp.dot(
            jnp.concatenate(tiles, axis=1),
            jnp.concatenate(sources, axis=0),
            preferred_element_type=jnp.float32,
        )

    for target in range(blocks):
        first, end = bounds_ref[target], bounds_ref[target + 1]
        total = lax.fori_loop(
            0,
            (end - first + pack - 1) // pack,
            lambda step, total: product(first + step * pack, end, total),
            jnp.zeros(out_ref.shape[1:], jnp.float32),
        )
        out_ref[target] = total.astype(out_ref.dtype)


def tile_products(gathered, tiles, coords, live_total, flipped=False, pack=8):
    row_blocks = lax.axis_size("col")
    slots = tiles.shape[0]
    block_shape = gathered.shape[1:]
    vmem = pl.BlockSpec(memory_space=pltpu.VMEM)
    smem = pl.BlockSpec(memory_space=pltpu.SMEM)
    return pl.pallas_call(
        functools.partial(products_kernel, flipped, pack),
        in_specs=[smem, smem, pl.BlockSpec(memory_space=pl.ANY), vmem],
        out_specs=vmem,
        out_shape=jax.ShapeDtypeStruct((row_blocks, *block_shape), jnp.bfloat16),
        scratch_shapes=[
            pltpu.SMEM((slots,), jnp.int32),
            pltpu.SMEM((row_blocks + 1,), jnp.int32),
            pltpu.SMEM((row_blocks,), jnp.int32),
            pltpu.VMEM(tiles.shape, tiles.dtype),
            pltpu.SemaphoreType.DMA((8,)),
        ],
    )(coords.reshape(-1), live_total.reshape(1), tiles, gathered)


def on_device(
    features,
    tiles,
    tile_coords,
    tile_count,
    batch_mask,
    history,
    weight_one,
    bias_one,
    weight_two,
    bias_two,
):
    tile_set = tiles[0, 0]
    coord_set = tile_coords[0, 0]
    live_total = tile_count[0, 0]
    gathered_input = gather(features[0, 0], 0)
    summed_one = tile_products(gathered_input, tile_set, coord_set, live_total)
    pushed, gathered_proj = middle(
        summed_one,
        features[0, 0],
        weight_one,
        bias_one,
        batch_mask[0, 0],
        history[0, 0],
        weight_two,
        1,
    )
    summed_two = tile_products(gathered_proj, tile_set, coord_set, live_total, True)
    owned_two = exchange(summed_two, "col", True, 3).astype(jnp.float32).sum(axis=0)
    own_block = gathered_proj[lax.axis_index("row")].astype(jnp.float32)
    scores = (own_block + owned_two).T + bias_two
    return (pushed[None, None], scores[None, None])


def solution(mesh):
    return jax.shard_map(
        on_device,
        mesh=mesh,
        in_specs=(
            P("row", "col", None, None),
            P("row", "col", None, None, None),
            P("row", "col", None, None),
            P("row", "col"),
            P("row", "col", None),
            P("row", "col", None, None),
            P(),
            P(),
            P(),
            P(),
        ),
        out_specs=(P("row", "col", None, None), P("row", "col", None, None)),
        check_vma=False,
    )
```

```python
import functools

import jax
import jax.numpy as jnp
from jax import lax
from jax.experimental import pallas as pl
from jax.experimental.pallas import tpu as pltpu
from jax.sharding import PartitionSpec as P

MESH_ID = pl.DeviceIdType.MESH


def exchange_kernel(axis, other_axis, n, spread, src_ref, out_ref, send_sem, recv_sem):
    me = lax.axis_index(axis)
    other = lax.axis_index(other_axis)

    def device(k):
        return (k, other) if axis == "row" else (other, k)

    def outgoing(k):
        source = src_ref.at[k] if spread else src_ref
        return pltpu.make_async_remote_copy(
            src_ref=source,
            dst_ref=out_ref.at[me],
            send_sem=send_sem.at[k],
            recv_sem=recv_sem.at[me],
            device_id=device(k),
            device_id_type=MESH_ID,
        )

    def incoming(k):
        source = src_ref.at[k] if spread else src_ref
        return pltpu.make_async_remote_copy(
            src_ref=source,
            dst_ref=out_ref.at[k],
            send_sem=send_sem.at[k],
            recv_sem=recv_sem.at[k],
            device_id=device(k),
            device_id_type=MESH_ID,
        )

    barrier = pltpu.get_barrier_semaphore()

    def greet(step, carry):
        k = lax.rem(me + step, n)
        pl.semaphore_signal(barrier, 1, device_id=device(k), device_id_type=MESH_ID)
        return carry

    lax.fori_loop(1, n, greet, 0)
    pl.semaphore_wait(barrier, n - 1)

    def send(step, carry):
        outgoing(lax.rem(me + step, n)).start()
        return carry

    lax.fori_loop(1, n, send, 0)
    out_ref[me] = src_ref[me] if spread else src_ref[...]

    def finish(step, carry):
        k = lax.rem(me + step, n)
        outgoing(k).wait_send()
        incoming(lax.rem(me + n - step, n)).wait_recv()
        return carry

    lax.fori_loop(1, n, finish, 0)


def row_partners():
    me = lax.axis_index("row")
    return me, lax.axis_index("col"), me + 1 - 2 * lax.rem(me, 2)


def near_first(n):
    rings = n // 4
    order = sorted(range(1, rings), key=lambda d: (min(d, rings - d), d))
    return [(d, 0) for d in order] + [(d, 1) for d in [0] + order]


def row_peer(me, n, shift):
    rings = n // 4
    ring, half_index = me // 4, lax.rem(me // 2, 2)
    ring = lax.rem(ring + shift[0], rings)
    half_index = lax.rem(half_index + shift[1], 2)
    return (ring * 2 + half_index) * 2 + lax.rem(me, 2)


def row_greet(barrier, n):
    me, other, twin = row_partners()
    pl.semaphore_signal(barrier, 1, device_id=(twin, other), device_id_type=MESH_ID)
    for shift in near_first(n):
        peer = row_peer(me, n, shift)
        pl.semaphore_signal(barrier, 1, device_id=(peer, other), device_id_type=MESH_ID)
    return n // 2


def row_transfer(n, src_ref, out_ref, send_sem, pass_sem, recv_sem):
    me, other, twin = row_partners()
    half = n // 2

    def copy(source, slot, sems, k):
        return pltpu.make_async_remote_copy(
            src_ref=source,
            dst_ref=out_ref.at[slot],
            send_sem=sems.at[k],
            recv_sem=recv_sem.at[slot],
            device_id=(k, other),
            device_id_type=MESH_ID,
        )

    shifts = near_first(n)
    for shift in shifts:
        copy(src_ref, me, send_sem, row_peer(me, n, shift)).start()
    copy(src_ref, me, send_sem, twin).start()
    for shift in shifts:
        k = row_peer(me, n, shift)
        copy(src_ref, k, send_sem, k).wait_recv()
        copy(out_ref.at[k], k, pass_sem, twin).start()
    for shift in shifts:
        k = row_peer(me, n, shift)
        copy(src_ref, me, send_sem, k).wait_send()
        copy(out_ref.at[k], k, pass_sem, twin).wait_send()
        far = row_peer(twin, n, shift)
        copy(src_ref, far, send_sem, twin).wait_recv()
    copy(src_ref, me, send_sem, twin).wait_send()
    copy(src_ref, twin, send_sem, twin).wait_recv()


def gather_kernel(n, src_ref, out_ref, send_sem, pass_sem, recv_sem):
    barrier = pltpu.get_barrier_semaphore()
    pl.semaphore_wait(barrier, row_greet(barrier, n))
    out_ref[lax.axis_index("row")] = src_ref[...]
    row_transfer(n, src_ref, out_ref, send_sem, pass_sem, recv_sem)


def gather(block, tag):
    n = lax.axis_size("row")
    vmem = pl.BlockSpec(memory_space=pltpu.VMEM)
    return pl.pallas_call(
        functools.partial(gather_kernel, n),
        out_shape=jax.ShapeDtypeStruct((n, *block.shape), block.dtype),
        in_specs=[vmem],
        out_specs=vmem,
        scratch_shapes=[pltpu.SemaphoreType.DMA((n,))] * 3,
        compiler_params=pltpu.CompilerParams(collective_id=tag, has_side_effects=True),
    )(block)


def middle_kernel(
    n_row,
    n_col,
    parts_ref,
    features_ref,
    weight_one_ref,
    bias_one_ref,
    mask_ref,
    history_ref,
    weight_two_ref,
    pushed_ref,
    out_ref,
    landing_ref,
    col_send,
    col_recv,
    send_sem,
    pass_sem,
    recv_sem,
):
    row = lax.axis_index("row")
    me = lax.axis_index("col")

    def col_copy(k, slot):
        return pltpu.make_async_remote_copy(
            src_ref=parts_ref.at[k],
            dst_ref=landing_ref.at[slot],
            send_sem=col_send.at[k],
            recv_sem=col_recv.at[slot],
            device_id=(row, k),
            device_id_type=MESH_ID,
        )

    barrier = pltpu.get_barrier_semaphore()

    def greet(step, carry):
        k = lax.rem(me + step, n_col)
        pl.semaphore_signal(barrier, 1, device_id=(row, k), device_id_type=MESH_ID)
        return carry

    lax.fori_loop(1, n_col, greet, 0)
    expected = row_greet(barrier, n_row)
    pl.semaphore_wait(barrier, n_col - 1 + expected)

    def send(step, carry):
        col_copy(lax.rem(me + step, n_col), me).start()
        return carry

    lax.fori_loop(1, n_col, send, 0)
    landing_ref[me] = parts_ref[me]

    def finish(step, carry):
        col_copy(lax.rem(me + step, n_col), me).wait_send()
        col_copy(me, lax.rem(me + n_col - step, n_col)).wait_recv()
        return carry

    lax.fori_loop(1, n_col, finish, 0)
    total = features_ref[...].astype(jnp.float32)
    for k in range(n_col):
        total = total + landing_ref[k].astype(jnp.float32)
    agg = total.astype(jnp.bfloat16)
    pre = jnp.dot(agg, weight_one_ref[...], preferred_element_type=jnp.float32)
    hidden = jnp.maximum(pre + bias_one_ref[...], 0.0).astype(jnp.bfloat16)
    pushed = jnp.where(mask_ref[...] == 1, hidden, history_ref[...])
    pushed_ref[...] = pushed
    projected = lax.dot_general(
        weight_two_ref[...], pushed, (((1,), (1,)), ((), ())), preferred_element_type=jnp.float32
    )
    out_ref[row] = projected.astype(out_ref.dtype)
    row_transfer(n_row, out_ref.at[row], out_ref, send_sem, pass_sem, recv_sem)


def middle(parts, features, weight_one, bias_one, mask, history, weight_two, tag):
    n_row = lax.axis_size("row")
    n_col = lax.axis_size("col")
    classes = weight_two.shape[1]
    nodes = features.shape[0]
    vmem = pl.BlockSpec(memory_space=pltpu.VMEM)
    return pl.pallas_call(
        functools.partial(middle_kernel, n_row, n_col),
        out_shape=(
            jax.ShapeDtypeStruct(history.shape, history.dtype),
            jax.ShapeDtypeStruct((n_row, classes, nodes), jnp.bfloat16),
        ),
        in_specs=[vmem] * 7,
        out_specs=(vmem, vmem),
        scratch_shapes=[
            pltpu.VMEM(parts.shape, parts.dtype),
            pltpu.SemaphoreType.DMA((n_col,)),
            pltpu.SemaphoreType.DMA((n_col,)),
        ]
        + [pltpu.SemaphoreType.DMA((n_row,))] * 3,
        compiler_params=pltpu.CompilerParams(collective_id=tag, has_side_effects=True),
    )(
        parts,
        features,
        weight_one,
        bias_one.reshape(1, -1),
        mask.reshape(-1, 1),
        history,
        weight_two.T,
    )


def exchange(block, axis, spread, tag):
    other_axis = "col" if axis == "row" else "row"
    n = lax.axis_size(axis)
    shape = block.shape[1:] if spread else block.shape
    vmem = pl.BlockSpec(memory_space=pltpu.VMEM)
    return pl.pallas_call(
        functools.partial(exchange_kernel, axis, other_axis, n, spread),
        out_shape=jax.ShapeDtypeStruct((n, *shape), block.dtype),
        in_specs=[vmem],
        out_specs=vmem,
        scratch_shapes=[pltpu.SemaphoreType.DMA((n,)), pltpu.SemaphoreType.DMA((n,))],
        compiler_params=pltpu.CompilerParams(collective_id=tag, has_side_effects=True),
    )(block)


def joined_along(tiles, dim):
    tiles = jnp.moveaxis(tiles, 0, dim)
    lengths = tiles.shape
    return tiles.reshape(*lengths[:dim], lengths[dim] * lengths[dim + 1], *lengths[dim + 2 :])


def copy_for_each(shard, axis):
    copies = jnp.broadcast_to(shard, (lax.axis_size(axis), *shard.shape))
    return lax.all_to_all(copies, axis, split_axis=0, concat_axis=0, tiled=True)


def collect(shard, axis, dim):
    return joined_along(copy_for_each(shard, axis), dim)


def in_blocks(shard, dim, size):
    lengths = shard.shape
    tiles = shard.reshape(*lengths[:dim], size, lengths[dim] // size, *lengths[dim + 1 :])
    return jnp.moveaxis(tiles, dim, 0)


def sent_and_summed(shard, axis, dim):
    tiles = in_blocks(shard, dim, lax.axis_size(axis))
    arrived = lax.all_to_all(tiles, axis, split_axis=0, concat_axis=0, tiled=True)
    return arrived.astype(jnp.float32).sum(axis=0)


def products_kernel(
    flipped,
    pack,
    coords_ref,
    count_ref,
    tiles_hbm,
    gathered_ref,
    out_ref,
    order_ref,
    bounds_ref,
    cursor_ref,
    tiles_ref,
    load_sem,
):
    chunks = load_sem.shape[0]
    size = tiles_ref.shape[0] // chunks
    loads = [
        pltpu.make_async_copy(
            tiles_hbm.at[pl.ds(c * size, size)], tiles_ref.at[pl.ds(c * size, size)], load_sem.at[c]
        )
        for c in range(chunks)
    ]
    for load in loads:
        load.start()
    blocks = out_ref.shape[0]
    live = count_ref[0]
    for target in range(blocks + 1):
        bounds_ref[target] = 0

    def count(slot, carry):
        target = coords_ref[2 * slot]
        bounds_ref[target + 1] = bounds_ref[target + 1] + 1
        return carry

    lax.fori_loop(0, live, count, 0)
    for target in range(blocks):
        bounds_ref[target + 1] = bounds_ref[target + 1] + bounds_ref[target]
        cursor_ref[target] = bounds_ref[target]

    def place(slot, carry):
        target = coords_ref[2 * slot]
        position = cursor_ref[target]
        order_ref[position] = slot
        cursor_ref[target] = position + 1
        return carry

    lax.fori_loop(0, live, place, 0)
    for load in loads:
        load.wait()

    def product(first, end, total):
        tiles, sources = [], []
        for offset in range(pack):
            slot = order_ref[jnp.minimum(first + offset, end - 1)]
            tile = tiles_ref[slot]
            tiles.append(jnp.where(first + offset < end, tile, jnp.zeros_like(tile)))
            sources.append(gathered_ref[coords_ref[2 * slot + 1]])
        if flipped:
            return total + lax.dot_general(
                jnp.concatenate(sources, axis=1),
                jnp.concatenate(tiles, axis=1),
                (((1,), (1,)), ((), ())),
                preferred_element_type=jnp.float32,
            )
        return total + jnp.dot(
            jnp.concatenate(tiles, axis=1),
            jnp.concatenate(sources, axis=0),
            preferred_element_type=jnp.float32,
        )

    for target in range(blocks):
        first, end = bounds_ref[target], bounds_ref[target + 1]
        total = lax.fori_loop(
            0,
            (end - first + pack - 1) // pack,
            lambda step, total: product(first + step * pack, end, total),
            jnp.zeros(out_ref.shape[1:], jnp.float32),
        )
        out_ref[target] = total.astype(out_ref.dtype)


def tile_products(gathered, tiles, coords, live_total, flipped=False, pack=8):
    row_blocks = lax.axis_size("col")
    slots = tiles.shape[0]
    block_shape = gathered.shape[1:]
    vmem = pl.BlockSpec(memory_space=pltpu.VMEM)
    smem = pl.BlockSpec(memory_space=pltpu.SMEM)
    return pl.pallas_call(
        functools.partial(products_kernel, flipped, pack),
        in_specs=[smem, smem, pl.BlockSpec(memory_space=pl.ANY), vmem],
        out_specs=vmem,
        out_shape=jax.ShapeDtypeStruct((row_blocks, *block_shape), jnp.bfloat16),
        scratch_shapes=[
            pltpu.SMEM((slots,), jnp.int32),
            pltpu.SMEM((row_blocks + 1,), jnp.int32),
            pltpu.SMEM((row_blocks,), jnp.int32),
            pltpu.VMEM(tiles.shape, tiles.dtype),
            pltpu.SemaphoreType.DMA((8,)),
        ],
    )(coords.reshape(-1), live_total.reshape(1), tiles, gathered)


def on_device(
    features,
    tiles,
    tile_coords,
    tile_count,
    batch_mask,
    history,
    weight_one,
    bias_one,
    weight_two,
    bias_two,
):
    tile_set = tiles[0, 0]
    coord_set = tile_coords[0, 0]
    live_total = tile_count[0, 0]
    gathered_input = gather(features[0, 0], 0)
    summed_one = tile_products(gathered_input, tile_set, coord_set, live_total)
    pushed, gathered_proj = middle(
        summed_one,
        features[0, 0],
        weight_one,
        bias_one,
        batch_mask[0, 0],
        history[0, 0],
        weight_two,
        1,
    )
    summed_two = tile_products(gathered_proj, tile_set, coord_set, live_total, True)
    owned_two = exchange(summed_two, "col", True, 3).astype(jnp.float32).sum(axis=0)
    own_block = gathered_proj[lax.axis_index("row")].astype(jnp.float32)
    scores = (own_block + owned_two).T + bias_two
    return (pushed[None, None], scores[None, None])


def solution(mesh):
    return jax.shard_map(
        on_device,
        mesh=mesh,
        in_specs=(
            P("row", "col", None, None),
            P("row", "col", None, None, None),
            P("row", "col", None, None),
            P("row", "col"),
            P("row", "col", None),
            P("row", "col", None, None),
            P(),
            P(),
            P(),
            P(),
        ),
        out_specs=(P("row", "col", None, None), P("row", "col", None, None)),
        check_vma=False,
    )
```

```python
import functools

import jax
import jax.numpy as jnp
from jax import lax
from jax.experimental import pallas as pl
from jax.experimental.pallas import tpu as pltpu
from jax.sharding import PartitionSpec as P

MESH_ID = pl.DeviceIdType.MESH


def exchange_kernel(axis, other_axis, n, spread, src_ref, out_ref, send_sem, recv_sem):
    me = lax.axis_index(axis)
    other = lax.axis_index(other_axis)

    def device(k):
        return (k, other) if axis == "row" else (other, k)

    def outgoing(k):
        source = src_ref.at[k] if spread else src_ref
        return pltpu.make_async_remote_copy(
            src_ref=source,
            dst_ref=out_ref.at[me],
            send_sem=send_sem.at[k],
            recv_sem=recv_sem.at[me],
            device_id=device(k),
            device_id_type=MESH_ID,
        )

    def incoming(k):
        source = src_ref.at[k] if spread else src_ref
        return pltpu.make_async_remote_copy(
            src_ref=source,
            dst_ref=out_ref.at[k],
            send_sem=send_sem.at[k],
            recv_sem=recv_sem.at[k],
            device_id=device(k),
            device_id_type=MESH_ID,
        )

    barrier = pltpu.get_barrier_semaphore()

    def greet(step, carry):
        k = lax.rem(me + step, n)
        pl.semaphore_signal(barrier, 1, device_id=device(k), device_id_type=MESH_ID)
        return carry

    lax.fori_loop(1, n, greet, 0)
    pl.semaphore_wait(barrier, n - 1)

    def send(step, carry):
        outgoing(lax.rem(me + step, n)).start()
        return carry

    lax.fori_loop(1, n, send, 0)
    out_ref[me] = src_ref[me] if spread else src_ref[...]

    def finish(step, carry):
        k = lax.rem(me + step, n)
        outgoing(k).wait_send()
        incoming(lax.rem(me + n - step, n)).wait_recv()
        return carry

    lax.fori_loop(1, n, finish, 0)


def row_partners():
    me = lax.axis_index("row")
    return me, lax.axis_index("col"), me + 1 - 2 * lax.rem(me, 2)


def near_first(n):
    rings = n // 4
    order = sorted(range(1, rings), key=lambda d: (min(d, rings - d), d))
    return [(d, 0) for d in order] + [(d, 1) for d in [0] + order]


def row_peer(me, n, shift):
    rings = n // 4
    ring, half_index = me // 4, lax.rem(me // 2, 2)
    ring = lax.rem(ring + shift[0], rings)
    half_index = lax.rem(half_index + shift[1], 2)
    return (ring * 2 + half_index) * 2 + lax.rem(me, 2)


def row_greet(barrier, n):
    me, other, twin = row_partners()
    pl.semaphore_signal(barrier, 1, device_id=(twin, other), device_id_type=MESH_ID)
    for shift in near_first(n):
        peer = row_peer(me, n, shift)
        pl.semaphore_signal(barrier, 1, device_id=(peer, other), device_id_type=MESH_ID)
    return n // 2


def row_transfer(n, src_ref, out_ref, send_sem, pass_sem, recv_sem):
    me, other, twin = row_partners()
    half = n // 2

    def copy(source, slot, sems, k):
        return pltpu.make_async_remote_copy(
            src_ref=source,
            dst_ref=out_ref.at[slot],
            send_sem=sems.at[k],
            recv_sem=recv_sem.at[slot],
            device_id=(k, other),
            device_id_type=MESH_ID,
        )

    shifts = near_first(n)
    for shift in reversed(shifts):
        copy(src_ref, me, send_sem, row_peer(me, n, shift)).start()
    copy(src_ref, me, send_sem, twin).start()
    for shift in shifts:
        k = row_peer(me, n, shift)
        copy(src_ref, k, send_sem, k).wait_recv()
        copy(out_ref.at[k], k, pass_sem, twin).start()
    for shift in shifts:
        k = row_peer(me, n, shift)
        copy(src_ref, me, send_sem, k).wait_send()
        copy(out_ref.at[k], k, pass_sem, twin).wait_send()
        far = row_peer(twin, n, shift)
        copy(src_ref, far, send_sem, twin).wait_recv()
    copy(src_ref, me, send_sem, twin).wait_send()
    copy(src_ref, twin, send_sem, twin).wait_recv()


def gather_kernel(n, src_ref, out_ref, send_sem, pass_sem, recv_sem):
    barrier = pltpu.get_barrier_semaphore()
    pl.semaphore_wait(barrier, row_greet(barrier, n))
    out_ref[lax.axis_index("row")] = src_ref[...]
    row_transfer(n, src_ref, out_ref, send_sem, pass_sem, recv_sem)


def gather(block, tag):
    n = lax.axis_size("row")
    vmem = pl.BlockSpec(memory_space=pltpu.VMEM)
    return pl.pallas_call(
        functools.partial(gather_kernel, n),
        out_shape=jax.ShapeDtypeStruct((n, *block.shape), block.dtype),
        in_specs=[vmem],
        out_specs=vmem,
        scratch_shapes=[pltpu.SemaphoreType.DMA((n,))] * 3,
        compiler_params=pltpu.CompilerParams(collective_id=tag, has_side_effects=True),
    )(block)


def middle_kernel(
    n_row,
    n_col,
    parts_ref,
    features_ref,
    weight_one_ref,
    bias_one_ref,
    mask_ref,
    history_ref,
    weight_two_ref,
    pushed_ref,
    out_ref,
    landing_ref,
    col_send,
    col_recv,
    send_sem,
    pass_sem,
    recv_sem,
):
    row = lax.axis_index("row")
    me = lax.axis_index("col")

    def col_copy(k, slot):
        return pltpu.make_async_remote_copy(
            src_ref=parts_ref.at[k],
            dst_ref=landing_ref.at[slot],
            send_sem=col_send.at[k],
            recv_sem=col_recv.at[slot],
            device_id=(row, k),
            device_id_type=MESH_ID,
        )

    barrier = pltpu.get_barrier_semaphore()

    def greet(step, carry):
        k = lax.rem(me + step, n_col)
        pl.semaphore_signal(barrier, 1, device_id=(row, k), device_id_type=MESH_ID)
        return carry

    lax.fori_loop(1, n_col, greet, 0)
    expected = row_greet(barrier, n_row)
    pl.semaphore_wait(barrier, n_col - 1 + expected)

    def send(step, carry):
        col_copy(lax.rem(me + step, n_col), me).start()
        return carry

    lax.fori_loop(1, n_col, send, 0)
    landing_ref[me] = parts_ref[me]

    def finish(step, carry):
        col_copy(lax.rem(me + step, n_col), me).wait_send()
        col_copy(me, lax.rem(me + n_col - step, n_col)).wait_recv()
        return carry

    lax.fori_loop(1, n_col, finish, 0)
    total = features_ref[...].astype(jnp.float32)
    for k in range(n_col):
        total = total + landing_ref[k].astype(jnp.float32)
    agg = total.astype(jnp.bfloat16)
    pre = jnp.dot(agg, weight_one_ref[...], preferred_element_type=jnp.float32)
    hidden = jnp.maximum(pre + bias_one_ref[...], 0.0).astype(jnp.bfloat16)
    pushed = jnp.where(mask_ref[...] == 1, hidden, history_ref[...])
    pushed_ref[...] = pushed
    projected = lax.dot_general(
        weight_two_ref[...], pushed, (((1,), (1,)), ((), ())), preferred_element_type=jnp.float32
    )
    out_ref[row] = projected.astype(out_ref.dtype)
    row_transfer(n_row, out_ref.at[row], out_ref, send_sem, pass_sem, recv_sem)


def middle(parts, features, weight_one, bias_one, mask, history, weight_two, tag):
    n_row = lax.axis_size("row")
    n_col = lax.axis_size("col")
    classes = weight_two.shape[1]
    nodes = features.shape[0]
    vmem = pl.BlockSpec(memory_space=pltpu.VMEM)
    return pl.pallas_call(
        functools.partial(middle_kernel, n_row, n_col),
        out_shape=(
            jax.ShapeDtypeStruct(history.shape, history.dtype),
            jax.ShapeDtypeStruct((n_row, classes, nodes), jnp.bfloat16),
        ),
        in_specs=[vmem] * 7,
        out_specs=(vmem, vmem),
        scratch_shapes=[
            pltpu.VMEM(parts.shape, parts.dtype),
            pltpu.SemaphoreType.DMA((n_col,)),
            pltpu.SemaphoreType.DMA((n_col,)),
        ]
        + [pltpu.SemaphoreType.DMA((n_row,))] * 3,
        compiler_params=pltpu.CompilerParams(collective_id=tag, has_side_effects=True),
    )(
        parts,
        features,
        weight_one,
        bias_one.reshape(1, -1),
        mask.reshape(-1, 1),
        history,
        weight_two.T,
    )


def exchange(block, axis, spread, tag):
    other_axis = "col" if axis == "row" else "row"
    n = lax.axis_size(axis)
    shape = block.shape[1:] if spread else block.shape
    vmem = pl.BlockSpec(memory_space=pltpu.VMEM)
    return pl.pallas_call(
        functools.partial(exchange_kernel, axis, other_axis, n, spread),
        out_shape=jax.ShapeDtypeStruct((n, *shape), block.dtype),
        in_specs=[vmem],
        out_specs=vmem,
        scratch_shapes=[pltpu.SemaphoreType.DMA((n,)), pltpu.SemaphoreType.DMA((n,))],
        compiler_params=pltpu.CompilerParams(collective_id=tag, has_side_effects=True),
    )(block)


def joined_along(tiles, dim):
    tiles = jnp.moveaxis(tiles, 0, dim)
    lengths = tiles.shape
    return tiles.reshape(*lengths[:dim], lengths[dim] * lengths[dim + 1], *lengths[dim + 2 :])


def copy_for_each(shard, axis):
    copies = jnp.broadcast_to(shard, (lax.axis_size(axis), *shard.shape))
    return lax.all_to_all(copies, axis, split_axis=0, concat_axis=0, tiled=True)


def collect(shard, axis, dim):
    return joined_along(copy_for_each(shard, axis), dim)


def in_blocks(shard, dim, size):
    lengths = shard.shape
    tiles = shard.reshape(*lengths[:dim], size, lengths[dim] // size, *lengths[dim + 1 :])
    return jnp.moveaxis(tiles, dim, 0)


def sent_and_summed(shard, axis, dim):
    tiles = in_blocks(shard, dim, lax.axis_size(axis))
    arrived = lax.all_to_all(tiles, axis, split_axis=0, concat_axis=0, tiled=True)
    return arrived.astype(jnp.float32).sum(axis=0)


def products_kernel(
    flipped,
    pack,
    coords_ref,
    count_ref,
    tiles_hbm,
    gathered_ref,
    out_ref,
    order_ref,
    bounds_ref,
    cursor_ref,
    tiles_ref,
    load_sem,
):
    chunks = load_sem.shape[0]
    size = tiles_ref.shape[0] // chunks
    loads = [
        pltpu.make_async_copy(
            tiles_hbm.at[pl.ds(c * size, size)], tiles_ref.at[pl.ds(c * size, size)], load_sem.at[c]
        )
        for c in range(chunks)
    ]
    for load in loads:
        load.start()
    blocks = out_ref.shape[0]
    live = count_ref[0]
    for target in range(blocks + 1):
        bounds_ref[target] = 0

    def count(slot, carry):
        target = coords_ref[2 * slot]
        bounds_ref[target + 1] = bounds_ref[target + 1] + 1
        return carry

    lax.fori_loop(0, live, count, 0)
    for target in range(blocks):
        bounds_ref[target + 1] = bounds_ref[target + 1] + bounds_ref[target]
        cursor_ref[target] = bounds_ref[target]

    def place(slot, carry):
        target = coords_ref[2 * slot]
        position = cursor_ref[target]
        order_ref[position] = slot
        cursor_ref[target] = position + 1
        return carry

    lax.fori_loop(0, live, place, 0)
    for load in loads:
        load.wait()

    def product(first, end, total):
        tiles, sources = [], []
        for offset in range(pack):
            slot = order_ref[jnp.minimum(first + offset, end - 1)]
            tile = tiles_ref[slot]
            tiles.append(jnp.where(first + offset < end, tile, jnp.zeros_like(tile)))
            sources.append(gathered_ref[coords_ref[2 * slot + 1]])
        if flipped:
            return total + lax.dot_general(
                jnp.concatenate(sources, axis=1),
                jnp.concatenate(tiles, axis=1),
                (((1,), (1,)), ((), ())),
                preferred_element_type=jnp.float32,
            )
        return total + jnp.dot(
            jnp.concatenate(tiles, axis=1),
            jnp.concatenate(sources, axis=0),
            preferred_element_type=jnp.float32,
        )

    for target in range(blocks):
        first, end = bounds_ref[target], bounds_ref[target + 1]
        total = lax.fori_loop(
            0,
            (end - first + pack - 1) // pack,
            lambda step, total: product(first + step * pack, end, total),
            jnp.zeros(out_ref.shape[1:], jnp.float32),
        )
        out_ref[target] = total.astype(out_ref.dtype)


def tile_products(gathered, tiles, coords, live_total, flipped=False, pack=8):
    row_blocks = lax.axis_size("col")
    slots = tiles.shape[0]
    block_shape = gathered.shape[1:]
    vmem = pl.BlockSpec(memory_space=pltpu.VMEM)
    smem = pl.BlockSpec(memory_space=pltpu.SMEM)
    return pl.pallas_call(
        functools.partial(products_kernel, flipped, pack),
        in_specs=[smem, smem, pl.BlockSpec(memory_space=pl.ANY), vmem],
        out_specs=vmem,
        out_shape=jax.ShapeDtypeStruct((row_blocks, *block_shape), jnp.bfloat16),
        scratch_shapes=[
            pltpu.SMEM((slots,), jnp.int32),
            pltpu.SMEM((row_blocks + 1,), jnp.int32),
            pltpu.SMEM((row_blocks,), jnp.int32),
            pltpu.VMEM(tiles.shape, tiles.dtype),
            pltpu.SemaphoreType.DMA((8,)),
        ],
    )(coords.reshape(-1), live_total.reshape(1), tiles, gathered)


def on_device(
    features,
    tiles,
    tile_coords,
    tile_count,
    batch_mask,
    history,
    weight_one,
    bias_one,
    weight_two,
    bias_two,
):
    tile_set = tiles[0, 0]
    coord_set = tile_coords[0, 0]
    live_total = tile_count[0, 0]
    gathered_input = gather(features[0, 0], 0)
    summed_one = tile_products(gathered_input, tile_set, coord_set, live_total)
    pushed, gathered_proj = middle(
        summed_one,
        features[0, 0],
        weight_one,
        bias_one,
        batch_mask[0, 0],
        history[0, 0],
        weight_two,
        1,
    )
    summed_two = tile_products(gathered_proj, tile_set, coord_set, live_total, True)
    owned_two = exchange(summed_two, "col", True, 3).astype(jnp.float32).sum(axis=0)
    own_block = gathered_proj[lax.axis_index("row")].astype(jnp.float32)
    scores = (own_block + owned_two).T + bias_two
    return (pushed[None, None], scores[None, None])


def solution(mesh):
    return jax.shard_map(
        on_device,
        mesh=mesh,
        in_specs=(
            P("row", "col", None, None),
            P("row", "col", None, None, None),
            P("row", "col", None, None),
            P("row", "col"),
            P("row", "col", None),
            P("row", "col", None, None),
            P(),
            P(),
            P(),
            P(),
        ),
        out_specs=(P("row", "col", None, None), P("row", "col", None, None)),
        check_vma=False,
    )
```

```python
import functools

import jax
import jax.numpy as jnp
from jax import lax
from jax.experimental import pallas as pl
from jax.experimental.pallas import tpu as pltpu
from jax.sharding import PartitionSpec as P

MESH_ID = pl.DeviceIdType.MESH


def exchange_kernel(axis, other_axis, n, spread, src_ref, out_ref, send_sem, recv_sem):
    me = lax.axis_index(axis)
    other = lax.axis_index(other_axis)

    def device(k):
        return (k, other) if axis == "row" else (other, k)

    def outgoing(k):
        source = src_ref.at[k] if spread else src_ref
        return pltpu.make_async_remote_copy(
            src_ref=source,
            dst_ref=out_ref.at[me],
            send_sem=send_sem.at[k],
            recv_sem=recv_sem.at[me],
            device_id=device(k),
            device_id_type=MESH_ID,
        )

    def incoming(k):
        source = src_ref.at[k] if spread else src_ref
        return pltpu.make_async_remote_copy(
            src_ref=source,
            dst_ref=out_ref.at[k],
            send_sem=send_sem.at[k],
            recv_sem=recv_sem.at[k],
            device_id=device(k),
            device_id_type=MESH_ID,
        )

    barrier = pltpu.get_barrier_semaphore()

    def greet(step, carry):
        k = lax.rem(me + step, n)
        pl.semaphore_signal(barrier, 1, device_id=device(k), device_id_type=MESH_ID)
        return carry

    lax.fori_loop(1, n, greet, 0)
    pl.semaphore_wait(barrier, n - 1)

    def send(step, carry):
        outgoing(lax.rem(me + step, n)).start()
        return carry

    lax.fori_loop(1, n, send, 0)
    out_ref[me] = src_ref[me] if spread else src_ref[...]

    def finish(step, carry):
        k = lax.rem(me + step, n)
        outgoing(k).wait_send()
        incoming(lax.rem(me + n - step, n)).wait_recv()
        return carry

    lax.fori_loop(1, n, finish, 0)


def row_partners():
    me = lax.axis_index("row")
    return me, lax.axis_index("col"), me + 1 - 2 * lax.rem(me, 2)


def row_greet(barrier, n):
    me, other, twin = row_partners()
    pl.semaphore_signal(barrier, 1, device_id=(twin, other), device_id_type=MESH_ID)

    def greet(step, carry):
        peer = lax.rem(me + 2 * step, n)
        pl.semaphore_signal(barrier, 1, device_id=(peer, other), device_id_type=MESH_ID)
        return carry

    lax.fori_loop(1, n // 2, greet, 0)
    return n // 2


def row_transfer(n, src_ref, out_ref, send_sem, pass_sem, recv_sem):
    me, other, twin = row_partners()
    half = n // 2

    def copy(source, slot, sems, k):
        return pltpu.make_async_remote_copy(
            src_ref=source,
            dst_ref=out_ref.at[slot],
            send_sem=sems.at[k],
            recv_sem=recv_sem.at[slot],
            device_id=(k, other),
            device_id_type=MESH_ID,
        )

    def peer(step):
        return lax.rem(me + 2 * step, n)

    def far(step):
        return lax.rem(twin + 2 * step, n)

    def send(step, carry):
        copy(src_ref, me, send_sem, peer(step)).start()
        return carry

    lax.fori_loop(1, half, send, 0)
    copy(src_ref, me, send_sem, twin).start()

    def relay(step, carry):
        k = peer(step)
        copy(src_ref, k, send_sem, k).wait_recv()
        copy(out_ref.at[k], k, pass_sem, twin).start()
        return carry

    lax.fori_loop(1, half, relay, 0)

    def finish(step, carry):
        k = peer(step)
        copy(src_ref, me, send_sem, k).wait_send()
        copy(out_ref.at[k], k, pass_sem, twin).wait_send()
        copy(src_ref, far(step), send_sem, twin).wait_recv()
        return carry

    lax.fori_loop(1, half, finish, 0)
    copy(src_ref, me, send_sem, twin).wait_send()
    copy(src_ref, twin, send_sem, twin).wait_recv()


def gather_kernel(n, src_ref, out_ref, send_sem, pass_sem, recv_sem):
    barrier = pltpu.get_barrier_semaphore()
    pl.semaphore_wait(barrier, row_greet(barrier, n))
    out_ref[lax.axis_index("row")] = src_ref[...]
    row_transfer(n, src_ref, out_ref, send_sem, pass_sem, recv_sem)


def gather(block, tag):
    n = lax.axis_size("row")
    vmem = pl.BlockSpec(memory_space=pltpu.VMEM)
    return pl.pallas_call(
        functools.partial(gather_kernel, n),
        out_shape=jax.ShapeDtypeStruct((n, *block.shape), block.dtype),
        in_specs=[vmem],
        out_specs=vmem,
        scratch_shapes=[pltpu.SemaphoreType.DMA((n,))] * 3,
        compiler_params=pltpu.CompilerParams(collective_id=tag, has_side_effects=True),
    )(block)


def middle_kernel(
    n_row,
    n_col,
    parts_ref,
    features_ref,
    weight_one_ref,
    bias_one_ref,
    mask_ref,
    history_ref,
    weight_two_ref,
    pushed_ref,
    out_ref,
    landing_ref,
    col_send,
    col_recv,
    send_sem,
    pass_sem,
    recv_sem,
):
    row = lax.axis_index("row")
    me = lax.axis_index("col")

    def col_copy(k, slot):
        return pltpu.make_async_remote_copy(
            src_ref=parts_ref.at[k],
            dst_ref=landing_ref.at[slot],
            send_sem=col_send.at[k],
            recv_sem=col_recv.at[slot],
            device_id=(row, k),
            device_id_type=MESH_ID,
        )

    barrier = pltpu.get_barrier_semaphore()

    def greet(step, carry):
        k = lax.rem(me + step, n_col)
        pl.semaphore_signal(barrier, 1, device_id=(row, k), device_id_type=MESH_ID)
        return carry

    lax.fori_loop(1, n_col, greet, 0)
    expected = row_greet(barrier, n_row)
    pl.semaphore_wait(barrier, n_col - 1 + expected)

    def send(step, carry):
        col_copy(lax.rem(me + step, n_col), me).start()
        return carry

    lax.fori_loop(1, n_col, send, 0)
    landing_ref[me] = parts_ref[me]

    def finish(step, carry):
        col_copy(lax.rem(me + step, n_col), me).wait_send()
        col_copy(me, lax.rem(me + n_col - step, n_col)).wait_recv()
        return carry

    lax.fori_loop(1, n_col, finish, 0)
    total = features_ref[...].astype(jnp.float32)
    for k in range(n_col):
        total = total + landing_ref[k].astype(jnp.float32)
    agg = total.astype(jnp.bfloat16)
    pre = jnp.dot(agg, weight_one_ref[...], preferred_element_type=jnp.float32)
    hidden = jnp.maximum(pre + bias_one_ref[...], 0.0).astype(jnp.bfloat16)
    pushed = jnp.where(mask_ref[...] == 1, hidden, history_ref[...])
    pushed_ref[...] = pushed
    projected = lax.dot_general(
        weight_two_ref[...], pushed, (((1,), (1,)), ((), ())), preferred_element_type=jnp.float32
    )
    out_ref[row] = projected.astype(out_ref.dtype)
    row_transfer(n_row, out_ref.at[row], out_ref, send_sem, pass_sem, recv_sem)


def middle(parts, features, weight_one, bias_one, mask, history, weight_two, tag):
    n_row = lax.axis_size("row")
    n_col = lax.axis_size("col")
    classes = weight_two.shape[1]
    nodes = features.shape[0]
    vmem = pl.BlockSpec(memory_space=pltpu.VMEM)
    return pl.pallas_call(
        functools.partial(middle_kernel, n_row, n_col),
        out_shape=(
            jax.ShapeDtypeStruct(history.shape, history.dtype),
            jax.ShapeDtypeStruct((n_row, classes, nodes), jnp.bfloat16),
        ),
        in_specs=[vmem] * 7,
        out_specs=(vmem, vmem),
        scratch_shapes=[
            pltpu.VMEM(parts.shape, parts.dtype),
            pltpu.SemaphoreType.DMA((n_col,)),
            pltpu.SemaphoreType.DMA((n_col,)),
        ]
        + [pltpu.SemaphoreType.DMA((n_row,))] * 3,
        compiler_params=pltpu.CompilerParams(collective_id=tag, has_side_effects=True),
    )(
        parts,
        features,
        weight_one,
        bias_one.reshape(1, -1),
        mask.reshape(-1, 1),
        history,
        weight_two.T,
    )


def exchange(block, axis, spread, tag):
    other_axis = "col" if axis == "row" else "row"
    n = lax.axis_size(axis)
    shape = block.shape[1:] if spread else block.shape
    vmem = pl.BlockSpec(memory_space=pltpu.VMEM)
    return pl.pallas_call(
        functools.partial(exchange_kernel, axis, other_axis, n, spread),
        out_shape=jax.ShapeDtypeStruct((n, *shape), block.dtype),
        in_specs=[vmem],
        out_specs=vmem,
        scratch_shapes=[pltpu.SemaphoreType.DMA((n,)), pltpu.SemaphoreType.DMA((n,))],
        compiler_params=pltpu.CompilerParams(collective_id=tag, has_side_effects=True),
    )(block)


def joined_along(tiles, dim):
    tiles = jnp.moveaxis(tiles, 0, dim)
    lengths = tiles.shape
    return tiles.reshape(*lengths[:dim], lengths[dim] * lengths[dim + 1], *lengths[dim + 2 :])


def copy_for_each(shard, axis):
    copies = jnp.broadcast_to(shard, (lax.axis_size(axis), *shard.shape))
    return lax.all_to_all(copies, axis, split_axis=0, concat_axis=0, tiled=True)


def collect(shard, axis, dim):
    return joined_along(copy_for_each(shard, axis), dim)


def in_blocks(shard, dim, size):
    lengths = shard.shape
    tiles = shard.reshape(*lengths[:dim], size, lengths[dim] // size, *lengths[dim + 1 :])
    return jnp.moveaxis(tiles, dim, 0)


def sent_and_summed(shard, axis, dim):
    tiles = in_blocks(shard, dim, lax.axis_size(axis))
    arrived = lax.all_to_all(tiles, axis, split_axis=0, concat_axis=0, tiled=True)
    return arrived.astype(jnp.float32).sum(axis=0)


def products_kernel(
    flipped,
    pack,
    coords_ref,
    count_ref,
    tiles_hbm,
    gathered_ref,
    out_ref,
    order_ref,
    bounds_ref,
    cursor_ref,
    tiles_ref,
    load_sem,
):
    chunks = load_sem.shape[0]
    size = tiles_ref.shape[0] // chunks
    loads = [
        pltpu.make_async_copy(
            tiles_hbm.at[pl.ds(c * size, size)], tiles_ref.at[pl.ds(c * size, size)], load_sem.at[c]
        )
        for c in range(chunks)
    ]
    for load in loads:
        load.start()
    blocks = out_ref.shape[0]
    sources_count = gathered_ref.shape[0]
    live = count_ref[0]
    for target in range(blocks + 1):
        bounds_ref[target] = 0

    def count(slot, carry):
        target = coords_ref[slot] // sources_count
        bounds_ref[target + 1] = bounds_ref[target + 1] + 1
        return carry

    lax.fori_loop(0, live, count, 0)
    for target in range(blocks):
        bounds_ref[target + 1] = bounds_ref[target + 1] + bounds_ref[target]
        cursor_ref[target] = bounds_ref[target]

    def place(slot, carry):
        target = coords_ref[slot] // sources_count
        position = cursor_ref[target]
        order_ref[position] = slot
        cursor_ref[target] = position + 1
        return carry

    lax.fori_loop(0, live, place, 0)
    for load in loads:
        load.wait()

    def product(first, end, total):
        tiles, sources = [], []
        for offset in range(pack):
            slot = order_ref[jnp.minimum(first + offset, end - 1)]
            tile = tiles_ref[slot]
            tiles.append(jnp.where(first + offset < end, tile, jnp.zeros_like(tile)))
            sources.append(gathered_ref[coords_ref[slot] % sources_count])
        if flipped:
            return total + lax.dot_general(
                jnp.concatenate(sources, axis=1),
                jnp.concatenate(tiles, axis=1),
                (((1,), (1,)), ((), ())),
                preferred_element_type=jnp.float32,
            )
        return total + jnp.dot(
            jnp.concatenate(tiles, axis=1),
            jnp.concatenate(sources, axis=0),
            preferred_element_type=jnp.float32,
        )

    for target in range(blocks):
        first, end = bounds_ref[target], bounds_ref[target + 1]
        total = lax.fori_loop(
            0,
            (end - first + pack - 1) // pack,
            lambda step, total: product(first + step * pack, end, total),
            jnp.zeros(out_ref.shape[1:], jnp.float32),
        )
        out_ref[target] = total.astype(out_ref.dtype)


def tile_products(gathered, tiles, coords, live_total, flipped=False, pack=8):
    row_blocks = lax.axis_size("col")
    slots = tiles.shape[0]
    block_shape = gathered.shape[1:]
    vmem = pl.BlockSpec(memory_space=pltpu.VMEM)
    smem = pl.BlockSpec(memory_space=pltpu.SMEM)
    return pl.pallas_call(
        functools.partial(products_kernel, flipped, pack),
        in_specs=[smem, smem, pl.BlockSpec(memory_space=pl.ANY), vmem],
        out_specs=vmem,
        out_shape=jax.ShapeDtypeStruct((row_blocks, *block_shape), jnp.bfloat16),
        scratch_shapes=[
            pltpu.SMEM((slots,), jnp.int32),
            pltpu.SMEM((row_blocks + 1,), jnp.int32),
            pltpu.SMEM((row_blocks,), jnp.int32),
            pltpu.VMEM(tiles.shape, tiles.dtype),
            pltpu.SemaphoreType.DMA((8,)),
        ],
    )(coords, live_total.reshape(1), tiles, gathered)


def on_device(
    features,
    tiles,
    tile_coords,
    tile_count,
    batch_mask,
    history,
    weight_one,
    bias_one,
    weight_two,
    bias_two,
):
    tile_set = tiles[0, 0]
    coord_set = tile_coords[0, 0, :, 0] * lax.axis_size("row") + tile_coords[0, 0, :, 1]
    live_total = tile_count[0, 0]
    gathered_input = gather(features[0, 0], 0)
    summed_one = tile_products(gathered_input, tile_set, coord_set, live_total)
    pushed, gathered_proj = middle(
        summed_one,
        features[0, 0],
        weight_one,
        bias_one,
        batch_mask[0, 0],
        history[0, 0],
        weight_two,
        1,
    )
    summed_two = tile_products(gathered_proj, tile_set, coord_set, live_total, True)
    owned_two = exchange(summed_two, "col", True, 3).astype(jnp.float32).sum(axis=0)
    own_block = gathered_proj[lax.axis_index("row")].astype(jnp.float32)
    scores = (own_block + owned_two).T + bias_two
    return (pushed[None, None], scores[None, None])


def solution(mesh):
    return jax.shard_map(
        on_device,
        mesh=mesh,
        in_specs=(
            P("row", "col", None, None),
            P("row", "col", None, None, None),
            P("row", "col", None, None),
            P("row", "col"),
            P("row", "col", None),
            P("row", "col", None, None),
            P(),
            P(),
            P(),
            P(),
        ),
        out_specs=(P("row", "col", None, None), P("row", "col", None, None)),
        check_vma=False,
    )
```

```python
import functools

import jax
import jax.numpy as jnp
from jax import lax
from jax.experimental import pallas as pl
from jax.experimental.pallas import tpu as pltpu
from jax.sharding import PartitionSpec as P

MESH_ID = pl.DeviceIdType.MESH


def exchange_kernel(axis, other_axis, n, spread, src_ref, out_ref, send_sem, recv_sem):
    me = lax.axis_index(axis)
    other = lax.axis_index(other_axis)

    def device(k):
        return (k, other) if axis == "row" else (other, k)

    def outgoing(k):
        source = src_ref.at[k] if spread else src_ref
        return pltpu.make_async_remote_copy(
            src_ref=source,
            dst_ref=out_ref.at[me],
            send_sem=send_sem.at[k],
            recv_sem=recv_sem.at[me],
            device_id=device(k),
            device_id_type=MESH_ID,
        )

    def incoming(k):
        source = src_ref.at[k] if spread else src_ref
        return pltpu.make_async_remote_copy(
            src_ref=source,
            dst_ref=out_ref.at[k],
            send_sem=send_sem.at[k],
            recv_sem=recv_sem.at[k],
            device_id=device(k),
            device_id_type=MESH_ID,
        )

    barrier = pltpu.get_barrier_semaphore()

    def greet(step, carry):
        k = lax.rem(me + step, n)
        pl.semaphore_signal(barrier, 1, device_id=device(k), device_id_type=MESH_ID)
        return carry

    lax.fori_loop(1, n, greet, 0)
    pl.semaphore_wait(barrier, n - 1)

    def send(step, carry):
        outgoing(lax.rem(me + step, n)).start()
        return carry

    lax.fori_loop(1, n, send, 0)
    out_ref[me] = src_ref[me] if spread else src_ref[...]

    def finish(step, carry):
        k = lax.rem(me + step, n)
        outgoing(k).wait_send()
        incoming(lax.rem(me + n - step, n)).wait_recv()
        return carry

    lax.fori_loop(1, n, finish, 0)


def row_partners():
    me = lax.axis_index("row")
    return me, lax.axis_index("col"), me + 1 - 2 * lax.rem(me, 2)


def row_greet(barrier, n):
    me, other, twin = row_partners()
    pl.semaphore_signal(barrier, 1, device_id=(twin, other), device_id_type=MESH_ID)

    def greet(step, carry):
        peer = lax.rem(me + 2 * step, n)
        pl.semaphore_signal(barrier, 1, device_id=(peer, other), device_id_type=MESH_ID)
        return carry

    lax.fori_loop(1, n // 2, greet, 0)
    return n // 2


def row_transfer(n, src_ref, out_ref, send_sem, pass_sem, recv_sem):
    me, other, twin = row_partners()
    half = n // 2

    def copy(source, slot, sems, k):
        return pltpu.make_async_remote_copy(
            src_ref=source,
            dst_ref=out_ref.at[slot],
            send_sem=sems.at[k],
            recv_sem=recv_sem.at[slot],
            device_id=(k, other),
            device_id_type=MESH_ID,
        )

    def peer(step):
        return lax.rem(me + 2 * step, n)

    def far(step):
        return lax.rem(twin + 2 * step, n)

    def send(step, carry):
        copy(src_ref, me, send_sem, peer(step)).start()
        return carry

    lax.fori_loop(1, half, send, 0)
    copy(src_ref, me, send_sem, twin).start()

    def relay(step, carry):
        k = peer(step)
        copy(src_ref, k, send_sem, k).wait_recv()
        copy(out_ref.at[k], k, pass_sem, twin).start()
        return carry

    lax.fori_loop(1, half, relay, 0)

    def finish(step, carry):
        k = peer(step)
        copy(src_ref, me, send_sem, k).wait_send()
        copy(out_ref.at[k], k, pass_sem, twin).wait_send()
        copy(src_ref, far(step), send_sem, twin).wait_recv()
        return carry

    lax.fori_loop(1, half, finish, 0)
    copy(src_ref, me, send_sem, twin).wait_send()
    copy(src_ref, twin, send_sem, twin).wait_recv()


def gather_kernel(n, src_ref, out_ref, send_sem, pass_sem, recv_sem):
    barrier = pltpu.get_barrier_semaphore()
    pl.semaphore_wait(barrier, row_greet(barrier, n))
    out_ref[lax.axis_index("row")] = src_ref[...]
    row_transfer(n, src_ref, out_ref, send_sem, pass_sem, recv_sem)


def gather(block, tag):
    n = lax.axis_size("row")
    vmem = pl.BlockSpec(memory_space=pltpu.VMEM)
    return pl.pallas_call(
        functools.partial(gather_kernel, n),
        out_shape=jax.ShapeDtypeStruct((n, *block.shape), block.dtype),
        in_specs=[vmem],
        out_specs=vmem,
        scratch_shapes=[pltpu.SemaphoreType.DMA((n,))] * 3,
        compiler_params=pltpu.CompilerParams(collective_id=tag, has_side_effects=True),
    )(block)


def middle_kernel(
    n_row,
    n_col,
    parts_ref,
    features_ref,
    weight_one_ref,
    bias_one_ref,
    mask_ref,
    history_ref,
    weight_two_ref,
    pushed_ref,
    out_ref,
    landing_ref,
    col_send,
    col_recv,
    send_sem,
    pass_sem,
    recv_sem,
):
    row = lax.axis_index("row")
    me = lax.axis_index("col")

    def col_copy(k, slot):
        return pltpu.make_async_remote_copy(
            src_ref=parts_ref.at[k],
            dst_ref=landing_ref.at[slot],
            send_sem=col_send.at[k],
            recv_sem=col_recv.at[slot],
            device_id=(row, k),
            device_id_type=MESH_ID,
        )

    barrier = pltpu.get_barrier_semaphore()

    def greet(step, carry):
        k = lax.rem(me + step, n_col)
        pl.semaphore_signal(barrier, 1, device_id=(row, k), device_id_type=MESH_ID)
        return carry

    lax.fori_loop(1, n_col, greet, 0)
    expected = row_greet(barrier, n_row)
    pl.semaphore_wait(barrier, n_col - 1 + expected)

    def send(step, carry):
        col_copy(lax.rem(me + step, n_col), me).start()
        return carry

    lax.fori_loop(1, n_col, send, 0)
    landing_ref[me] = parts_ref[me]

    def finish(step, carry):
        col_copy(lax.rem(me + step, n_col), me).wait_send()
        col_copy(me, lax.rem(me + n_col - step, n_col)).wait_recv()
        return carry

    lax.fori_loop(1, n_col, finish, 0)
    total = features_ref[...].astype(jnp.float32)
    for k in range(n_col):
        total = total + landing_ref[k].astype(jnp.float32)
    agg = total.astype(jnp.bfloat16)
    pre = jnp.dot(agg, weight_one_ref[...], preferred_element_type=jnp.float32)
    hidden = jnp.maximum(pre + bias_one_ref[...], 0.0).astype(jnp.bfloat16)
    pushed = jnp.where(mask_ref[...] == 1, hidden, history_ref[...])
    pushed_ref[...] = pushed
    projected = lax.dot_general(
        weight_two_ref[...], pushed, (((1,), (1,)), ((), ())), preferred_element_type=jnp.float32
    )
    out_ref[row] = projected.astype(out_ref.dtype)
    row_transfer(n_row, out_ref.at[row], out_ref, send_sem, pass_sem, recv_sem)


def middle(parts, features, weight_one, bias_one, mask, history, weight_two, tag):
    n_row = lax.axis_size("row")
    n_col = lax.axis_size("col")
    classes = weight_two.shape[1]
    nodes = features.shape[0]
    vmem = pl.BlockSpec(memory_space=pltpu.VMEM)
    return pl.pallas_call(
        functools.partial(middle_kernel, n_row, n_col),
        out_shape=(
            jax.ShapeDtypeStruct(history.shape, history.dtype),
            jax.ShapeDtypeStruct((n_row, classes, nodes), jnp.bfloat16),
        ),
        in_specs=[vmem] * 7,
        out_specs=(vmem, vmem),
        scratch_shapes=[
            pltpu.VMEM(parts.shape, parts.dtype),
            pltpu.SemaphoreType.DMA((n_col,)),
            pltpu.SemaphoreType.DMA((n_col,)),
        ]
        + [pltpu.SemaphoreType.DMA((n_row,))] * 3,
        compiler_params=pltpu.CompilerParams(collective_id=tag, has_side_effects=True),
    )(
        parts,
        features,
        weight_one,
        bias_one.reshape(1, -1),
        mask.reshape(-1, 1),
        history,
        weight_two.T,
    )


def exchange(block, axis, spread, tag):
    other_axis = "col" if axis == "row" else "row"
    n = lax.axis_size(axis)
    shape = block.shape[1:] if spread else block.shape
    vmem = pl.BlockSpec(memory_space=pltpu.VMEM)
    return pl.pallas_call(
        functools.partial(exchange_kernel, axis, other_axis, n, spread),
        out_shape=jax.ShapeDtypeStruct((n, *shape), block.dtype),
        in_specs=[vmem],
        out_specs=vmem,
        scratch_shapes=[pltpu.SemaphoreType.DMA((n,)), pltpu.SemaphoreType.DMA((n,))],
        compiler_params=pltpu.CompilerParams(collective_id=tag, has_side_effects=True),
    )(block)


def joined_along(tiles, dim):
    tiles = jnp.moveaxis(tiles, 0, dim)
    lengths = tiles.shape
    return tiles.reshape(*lengths[:dim], lengths[dim] * lengths[dim + 1], *lengths[dim + 2 :])


def copy_for_each(shard, axis):
    copies = jnp.broadcast_to(shard, (lax.axis_size(axis), *shard.shape))
    return lax.all_to_all(copies, axis, split_axis=0, concat_axis=0, tiled=True)


def collect(shard, axis, dim):
    return joined_along(copy_for_each(shard, axis), dim)


def in_blocks(shard, dim, size):
    lengths = shard.shape
    tiles = shard.reshape(*lengths[:dim], size, lengths[dim] // size, *lengths[dim + 1 :])
    return jnp.moveaxis(tiles, dim, 0)


def sent_and_summed(shard, axis, dim):
    tiles = in_blocks(shard, dim, lax.axis_size(axis))
    arrived = lax.all_to_all(tiles, axis, split_axis=0, concat_axis=0, tiled=True)
    return arrived.astype(jnp.float32).sum(axis=0)


def products_kernel(
    flipped,
    pack,
    coords_ref,
    count_ref,
    tiles_hbm,
    gathered_ref,
    out_ref,
    order_ref,
    bounds_ref,
    cursor_ref,
    tiles_ref,
    load_sem,
):
    chunks = load_sem.shape[0]
    size = (tiles_ref.shape[0] - 1) // chunks
    loads = [
        pltpu.make_async_copy(
            tiles_hbm.at[pl.ds(c * size, size)], tiles_ref.at[pl.ds(c * size, size)], load_sem.at[c]
        )
        for c in range(chunks)
    ]
    blank = chunks * size
    tiles_ref[blank] = jnp.zeros(tiles_ref.shape[1:], tiles_ref.dtype)
    for load in loads:
        load.start()
    blocks = out_ref.shape[0]
    live = count_ref[0]
    for target in range(blocks + 1):
        bounds_ref[target] = 0

    def count(slot, carry):
        target = coords_ref[2 * slot]
        bounds_ref[target + 1] = bounds_ref[target + 1] + 1
        return carry

    lax.fori_loop(0, live, count, 0)
    for target in range(blocks):
        bounds_ref[target + 1] = bounds_ref[target + 1] + bounds_ref[target]
        cursor_ref[target] = bounds_ref[target]

    def place(slot, carry):
        target = coords_ref[2 * slot]
        position = cursor_ref[target]
        order_ref[position] = slot
        cursor_ref[target] = position + 1
        return carry

    lax.fori_loop(0, live, place, 0)
    for load in loads:
        load.wait()

    def product(first, end, total):
        tiles, sources = [], []
        for offset in range(pack):
            slot = order_ref[jnp.minimum(first + offset, end - 1)]
            tiles.append(tiles_ref[jnp.where(first + offset < end, slot, blank)])
            sources.append(gathered_ref[coords_ref[2 * slot + 1]])
        if flipped:
            return total + lax.dot_general(
                jnp.concatenate(sources, axis=1),
                jnp.concatenate(tiles, axis=1),
                (((1,), (1,)), ((), ())),
                preferred_element_type=jnp.float32,
            )
        return total + jnp.dot(
            jnp.concatenate(tiles, axis=1),
            jnp.concatenate(sources, axis=0),
            preferred_element_type=jnp.float32,
        )

    for target in range(blocks):
        first, end = bounds_ref[target], bounds_ref[target + 1]
        total = lax.fori_loop(
            0,
            (end - first + pack - 1) // pack,
            lambda step, total: product(first + step * pack, end, total),
            jnp.zeros(out_ref.shape[1:], jnp.float32),
        )
        out_ref[target] = total.astype(out_ref.dtype)


def tile_products(gathered, tiles, coords, live_total, flipped=False, pack=8):
    row_blocks = lax.axis_size("col")
    slots = tiles.shape[0]
    block_shape = gathered.shape[1:]
    vmem = pl.BlockSpec(memory_space=pltpu.VMEM)
    smem = pl.BlockSpec(memory_space=pltpu.SMEM)
    return pl.pallas_call(
        functools.partial(products_kernel, flipped, pack),
        in_specs=[smem, smem, pl.BlockSpec(memory_space=pl.ANY), vmem],
        out_specs=vmem,
        out_shape=jax.ShapeDtypeStruct((row_blocks, *block_shape), jnp.bfloat16),
        scratch_shapes=[
            pltpu.SMEM((slots,), jnp.int32),
            pltpu.SMEM((row_blocks + 1,), jnp.int32),
            pltpu.SMEM((row_blocks,), jnp.int32),
            pltpu.VMEM((slots + 1, *tiles.shape[1:]), tiles.dtype),
            pltpu.SemaphoreType.DMA((8,)),
        ],
    )(coords.reshape(-1), live_total.reshape(1), tiles, gathered)


def on_device(
    features,
    tiles,
    tile_coords,
    tile_count,
    batch_mask,
    history,
    weight_one,
    bias_one,
    weight_two,
    bias_two,
):
    tile_set = tiles[0, 0]
    coord_set = tile_coords[0, 0]
    live_total = tile_count[0, 0]
    gathered_input = gather(features[0, 0], 0)
    summed_one = tile_products(gathered_input, tile_set, coord_set, live_total)
    pushed, gathered_proj = middle(
        summed_one,
        features[0, 0],
        weight_one,
        bias_one,
        batch_mask[0, 0],
        history[0, 0],
        weight_two,
        1,
    )
    summed_two = tile_products(gathered_proj, tile_set, coord_set, live_total, True)
    owned_two = exchange(summed_two, "col", True, 3).astype(jnp.float32).sum(axis=0)
    own_block = gathered_proj[lax.axis_index("row")].astype(jnp.float32)
    scores = (own_block + owned_two).T + bias_two
    return (pushed[None, None], scores[None, None])


def solution(mesh):
    return jax.shard_map(
        on_device,
        mesh=mesh,
        in_specs=(
            P("row", "col", None, None),
            P("row", "col", None, None, None),
            P("row", "col", None, None),
            P("row", "col"),
            P("row", "col", None),
            P("row", "col", None, None),
            P(),
            P(),
            P(),
            P(),
        ),
        out_specs=(P("row", "col", None, None), P("row", "col", None, None)),
        check_vma=False,
    )
```

```python
import functools

import jax
import jax.numpy as jnp
from jax import lax
from jax.experimental import pallas as pl
from jax.experimental.pallas import tpu as pltpu
from jax.sharding import PartitionSpec as P

MESH_ID = pl.DeviceIdType.MESH


def exchange_kernel(axis, other_axis, n, spread, src_ref, out_ref, send_sem, recv_sem):
    me = lax.axis_index(axis)
    other = lax.axis_index(other_axis)

    def device(k):
        return (k, other) if axis == "row" else (other, k)

    def outgoing(k):
        source = src_ref.at[k] if spread else src_ref
        return pltpu.make_async_remote_copy(
            src_ref=source,
            dst_ref=out_ref.at[me],
            send_sem=send_sem.at[k],
            recv_sem=recv_sem.at[me],
            device_id=device(k),
            device_id_type=MESH_ID,
        )

    def incoming(k):
        source = src_ref.at[k] if spread else src_ref
        return pltpu.make_async_remote_copy(
            src_ref=source,
            dst_ref=out_ref.at[k],
            send_sem=send_sem.at[k],
            recv_sem=recv_sem.at[k],
            device_id=device(k),
            device_id_type=MESH_ID,
        )

    barrier = pltpu.get_barrier_semaphore()

    def greet(step, carry):
        k = lax.rem(me + step, n)
        pl.semaphore_signal(barrier, 1, device_id=device(k), device_id_type=MESH_ID)
        return carry

    lax.fori_loop(1, n, greet, 0)
    pl.semaphore_wait(barrier, n - 1)

    def send(step, carry):
        outgoing(lax.rem(me + step, n)).start()
        return carry

    lax.fori_loop(1, n, send, 0)
    out_ref[me] = src_ref[me] if spread else src_ref[...]

    def finish(step, carry):
        k = lax.rem(me + step, n)
        outgoing(k).wait_send()
        incoming(lax.rem(me + n - step, n)).wait_recv()
        return carry

    lax.fori_loop(1, n, finish, 0)


def row_partners():
    me = lax.axis_index("row")
    return me, lax.axis_index("col"), me + 1 - 2 * lax.rem(me, 2)


def row_greet(barrier, n):
    me, other, twin = row_partners()
    pl.semaphore_signal(barrier, 1, device_id=(twin, other), device_id_type=MESH_ID)

    def greet(step, carry):
        peer = lax.rem(me + 2 * step, n)
        pl.semaphore_signal(barrier, 1, device_id=(peer, other), device_id_type=MESH_ID)
        return carry

    lax.fori_loop(1, n // 2, greet, 0)
    return n // 2


def row_transfer(n, src_ref, out_ref, send_sem, pass_sem, recv_sem):
    me, other, twin = row_partners()
    half = n // 2

    def copy(source, slot, sems, k):
        return pltpu.make_async_remote_copy(
            src_ref=source,
            dst_ref=out_ref.at[slot],
            send_sem=sems.at[k],
            recv_sem=recv_sem.at[slot],
            device_id=(k, other),
            device_id_type=MESH_ID,
        )

    def peer(step):
        return lax.rem(me + 2 * step, n)

    def far(step):
        return lax.rem(twin + 2 * step, n)

    def send(step, carry):
        copy(src_ref, me, send_sem, peer(step)).start()
        return carry

    lax.fori_loop(1, half, send, 0)
    copy(src_ref, me, send_sem, twin).start()

    def relay(step, carry):
        k = peer(step)
        copy(src_ref, k, send_sem, k).wait_recv()
        copy(out_ref.at[k], k, pass_sem, twin).start()
        return carry

    lax.fori_loop(1, half, relay, 0)

    def finish(step, carry):
        k = peer(step)
        copy(src_ref, me, send_sem, k).wait_send()
        copy(out_ref.at[k], k, pass_sem, twin).wait_send()
        copy(src_ref, far(step), send_sem, twin).wait_recv()
        return carry

    lax.fori_loop(1, half, finish, 0)
    copy(src_ref, me, send_sem, twin).wait_send()
    copy(src_ref, twin, send_sem, twin).wait_recv()


def gather_kernel(n, src_ref, out_ref, send_sem, pass_sem, recv_sem):
    barrier = pltpu.get_barrier_semaphore()
    pl.semaphore_wait(barrier, row_greet(barrier, n))
    out_ref[lax.axis_index("row")] = src_ref[...]
    row_transfer(n, src_ref, out_ref, send_sem, pass_sem, recv_sem)


def gather(block, tag):
    n = lax.axis_size("row")
    vmem = pl.BlockSpec(memory_space=pltpu.VMEM)
    return pl.pallas_call(
        functools.partial(gather_kernel, n),
        out_shape=jax.ShapeDtypeStruct((n, *block.shape), block.dtype),
        in_specs=[vmem],
        out_specs=vmem,
        scratch_shapes=[pltpu.SemaphoreType.DMA((n,))] * 3,
        compiler_params=pltpu.CompilerParams(collective_id=tag, has_side_effects=True),
    )(block)


def middle_kernel(
    n_row,
    n_col,
    parts_ref,
    features_ref,
    weight_one_ref,
    bias_one_ref,
    mask_ref,
    history_ref,
    weight_two_ref,
    pushed_ref,
    out_ref,
    landing_ref,
    col_send,
    col_recv,
    send_sem,
    pass_sem,
    recv_sem,
):
    row = lax.axis_index("row")
    me = lax.axis_index("col")

    def col_copy(k, slot):
        return pltpu.make_async_remote_copy(
            src_ref=parts_ref.at[k],
            dst_ref=landing_ref.at[slot],
            send_sem=col_send.at[k],
            recv_sem=col_recv.at[slot],
            device_id=(row, k),
            device_id_type=MESH_ID,
        )

    barrier = pltpu.get_barrier_semaphore()

    def greet(step, carry):
        k = lax.rem(me + step, n_col)
        pl.semaphore_signal(barrier, 1, device_id=(row, k), device_id_type=MESH_ID)
        return carry

    lax.fori_loop(1, n_col, greet, 0)
    expected = row_greet(barrier, n_row)
    pl.semaphore_wait(barrier, n_col - 1 + expected)

    def send(step, carry):
        col_copy(lax.rem(me + step, n_col), me).start()
        return carry

    lax.fori_loop(1, n_col, send, 0)
    landing_ref[me] = parts_ref[me]

    def finish(step, carry):
        col_copy(lax.rem(me + step, n_col), me).wait_send()
        col_copy(me, lax.rem(me + n_col - step, n_col)).wait_recv()
        return carry

    lax.fori_loop(1, n_col, finish, 0)
    total = features_ref[...].astype(jnp.float32)
    for k in range(n_col):
        total = total + landing_ref[k].astype(jnp.float32)
    agg = total.astype(jnp.bfloat16)
    pre = jnp.dot(agg, weight_one_ref[...], preferred_element_type=jnp.float32)
    hidden = jnp.maximum(pre + bias_one_ref[...], 0.0).astype(jnp.bfloat16)
    pushed = jnp.where(mask_ref[...] == 1, hidden, history_ref[...])
    pushed_ref[...] = pushed
    projected = lax.dot_general(
        weight_two_ref[...], pushed, (((1,), (1,)), ((), ())), preferred_element_type=jnp.float32
    )
    out_ref[row] = projected.astype(out_ref.dtype)
    row_transfer(n_row, out_ref.at[row], out_ref, send_sem, pass_sem, recv_sem)


def middle(parts, features, weight_one, bias_one, mask, history, weight_two, tag):
    n_row = lax.axis_size("row")
    n_col = lax.axis_size("col")
    classes = weight_two.shape[1]
    nodes = features.shape[0]
    vmem = pl.BlockSpec(memory_space=pltpu.VMEM)
    return pl.pallas_call(
        functools.partial(middle_kernel, n_row, n_col),
        out_shape=(
            jax.ShapeDtypeStruct(history.shape, history.dtype),
            jax.ShapeDtypeStruct((n_row, classes, nodes), jnp.bfloat16),
        ),
        in_specs=[vmem] * 7,
        out_specs=(vmem, vmem),
        scratch_shapes=[
            pltpu.VMEM(parts.shape, parts.dtype),
            pltpu.SemaphoreType.DMA((n_col,)),
            pltpu.SemaphoreType.DMA((n_col,)),
        ]
        + [pltpu.SemaphoreType.DMA((n_row,))] * 3,
        compiler_params=pltpu.CompilerParams(collective_id=tag, has_side_effects=True),
    )(
        parts,
        features,
        weight_one,
        bias_one.reshape(1, -1),
        mask.reshape(-1, 1),
        history,
        weight_two.T,
    )


def exchange(block, axis, spread, tag):
    other_axis = "col" if axis == "row" else "row"
    n = lax.axis_size(axis)
    shape = block.shape[1:] if spread else block.shape
    vmem = pl.BlockSpec(memory_space=pltpu.VMEM)
    return pl.pallas_call(
        functools.partial(exchange_kernel, axis, other_axis, n, spread),
        out_shape=jax.ShapeDtypeStruct((n, *shape), block.dtype),
        in_specs=[vmem],
        out_specs=vmem,
        scratch_shapes=[pltpu.SemaphoreType.DMA((n,)), pltpu.SemaphoreType.DMA((n,))],
        compiler_params=pltpu.CompilerParams(collective_id=tag, has_side_effects=True),
    )(block)


def joined_along(tiles, dim):
    tiles = jnp.moveaxis(tiles, 0, dim)
    lengths = tiles.shape
    return tiles.reshape(*lengths[:dim], lengths[dim] * lengths[dim + 1], *lengths[dim + 2 :])


def copy_for_each(shard, axis):
    copies = jnp.broadcast_to(shard, (lax.axis_size(axis), *shard.shape))
    return lax.all_to_all(copies, axis, split_axis=0, concat_axis=0, tiled=True)


def collect(shard, axis, dim):
    return joined_along(copy_for_each(shard, axis), dim)


def in_blocks(shard, dim, size):
    lengths = shard.shape
    tiles = shard.reshape(*lengths[:dim], size, lengths[dim] // size, *lengths[dim + 1 :])
    return jnp.moveaxis(tiles, dim, 0)


def sent_and_summed(shard, axis, dim):
    tiles = in_blocks(shard, dim, lax.axis_size(axis))
    arrived = lax.all_to_all(tiles, axis, split_axis=0, concat_axis=0, tiled=True)
    return arrived.astype(jnp.float32).sum(axis=0)


def products_kernel(
    flipped,
    pack,
    coords_ref,
    count_ref,
    tiles_hbm,
    gathered_hbm,
    out_ref,
    order_ref,
    bounds_ref,
    cursor_ref,
    tiles_ref,
    load_sem,
    gathered_ref,
    gathered_sem,
):
    chunks = load_sem.shape[0]
    size = tiles_ref.shape[0] // chunks
    loads = [
        pltpu.make_async_copy(
            tiles_hbm.at[pl.ds(c * size, size)], tiles_ref.at[pl.ds(c * size, size)], load_sem.at[c]
        )
        for c in range(chunks)
    ]
    loads.append(pltpu.make_async_copy(gathered_hbm, gathered_ref, gathered_sem.at[0]))
    for load in loads:
        load.start()
    blocks = out_ref.shape[0]
    live = count_ref[0]
    for target in range(blocks + 1):
        bounds_ref[target] = 0

    def count(slot, carry):
        target = coords_ref[2 * slot]
        bounds_ref[target + 1] = bounds_ref[target + 1] + 1
        return carry

    lax.fori_loop(0, live, count, 0)
    for target in range(blocks):
        bounds_ref[target + 1] = bounds_ref[target + 1] + bounds_ref[target]
        cursor_ref[target] = bounds_ref[target]

    def place(slot, carry):
        target = coords_ref[2 * slot]
        position = cursor_ref[target]
        order_ref[position] = slot
        cursor_ref[target] = position + 1
        return carry

    lax.fori_loop(0, live, place, 0)
    for load in loads:
        load.wait()

    def product(first, end, total):
        tiles, sources = [], []
        for offset in range(pack):
            slot = order_ref[jnp.minimum(first + offset, end - 1)]
            tile = tiles_ref[slot]
            tiles.append(jnp.where(first + offset < end, tile, jnp.zeros_like(tile)))
            sources.append(gathered_ref[coords_ref[2 * slot + 1]])
        if flipped:
            return total + lax.dot_general(
                jnp.concatenate(sources, axis=1),
                jnp.concatenate(tiles, axis=1),
                (((1,), (1,)), ((), ())),
                preferred_element_type=jnp.float32,
            )
        return total + jnp.dot(
            jnp.concatenate(tiles, axis=1),
            jnp.concatenate(sources, axis=0),
            preferred_element_type=jnp.float32,
        )

    for target in range(blocks):
        first, end = bounds_ref[target], bounds_ref[target + 1]
        total = lax.fori_loop(
            0,
            (end - first + pack - 1) // pack,
            lambda step, total: product(first + step * pack, end, total),
            jnp.zeros(out_ref.shape[1:], jnp.float32),
        )
        out_ref[target] = total.astype(out_ref.dtype)


def tile_products(gathered, tiles, coords, live_total, flipped=False, pack=8):
    row_blocks = lax.axis_size("col")
    slots = tiles.shape[0]
    block_shape = gathered.shape[1:]
    vmem = pl.BlockSpec(memory_space=pltpu.VMEM)
    smem = pl.BlockSpec(memory_space=pltpu.SMEM)
    return pl.pallas_call(
        functools.partial(products_kernel, flipped, pack),
        in_specs=[smem, smem, pl.BlockSpec(memory_space=pl.ANY), pl.BlockSpec(memory_space=pl.ANY)],
        out_specs=vmem,
        out_shape=jax.ShapeDtypeStruct((row_blocks, *block_shape), jnp.bfloat16),
        scratch_shapes=[
            pltpu.SMEM((slots,), jnp.int32),
            pltpu.SMEM((row_blocks + 1,), jnp.int32),
            pltpu.SMEM((row_blocks,), jnp.int32),
            pltpu.VMEM(tiles.shape, tiles.dtype),
            pltpu.SemaphoreType.DMA((8,)),
            pltpu.VMEM(gathered.shape, gathered.dtype),
            pltpu.SemaphoreType.DMA((1,)),
        ],
    )(coords.reshape(-1), live_total.reshape(1), tiles, gathered)


def on_device(
    features,
    tiles,
    tile_coords,
    tile_count,
    batch_mask,
    history,
    weight_one,
    bias_one,
    weight_two,
    bias_two,
):
    tile_set = tiles[0, 0]
    coord_set = tile_coords[0, 0]
    live_total = tile_count[0, 0]
    gathered_input = gather(features[0, 0], 0)
    summed_one = tile_products(gathered_input, tile_set, coord_set, live_total)
    pushed, gathered_proj = middle(
        summed_one,
        features[0, 0],
        weight_one,
        bias_one,
        batch_mask[0, 0],
        history[0, 0],
        weight_two,
        1,
    )
    summed_two = tile_products(gathered_proj, tile_set, coord_set, live_total, True)
    owned_two = exchange(summed_two, "col", True, 3).astype(jnp.float32).sum(axis=0)
    own_block = gathered_proj[lax.axis_index("row")].astype(jnp.float32)
    scores = (own_block + owned_two).T + bias_two
    return (pushed[None, None], scores[None, None])


def solution(mesh):
    return jax.shard_map(
        on_device,
        mesh=mesh,
        in_specs=(
            P("row", "col", None, None),
            P("row", "col", None, None, None),
            P("row", "col", None, None),
            P("row", "col"),
            P("row", "col", None),
            P("row", "col", None, None),
            P(),
            P(),
            P(),
            P(),
        ),
        out_specs=(P("row", "col", None, None), P("row", "col", None, None)),
        check_vma=False,
    )
```

```python
import functools

import jax
import jax.numpy as jnp
from jax import lax
from jax.experimental import pallas as pl
from jax.experimental.pallas import tpu as pltpu
from jax.sharding import PartitionSpec as P

MESH_ID = pl.DeviceIdType.MESH


def exchange_kernel(axis, other_axis, n, spread, src_ref, out_ref, send_sem, recv_sem):
    me = lax.axis_index(axis)
    other = lax.axis_index(other_axis)

    def device(k):
        return (k, other) if axis == "row" else (other, k)

    def outgoing(k):
        source = src_ref.at[k] if spread else src_ref
        return pltpu.make_async_remote_copy(
            src_ref=source,
            dst_ref=out_ref.at[me],
            send_sem=send_sem.at[k],
            recv_sem=recv_sem.at[me],
            device_id=device(k),
            device_id_type=MESH_ID,
        )

    def incoming(k):
        source = src_ref.at[k] if spread else src_ref
        return pltpu.make_async_remote_copy(
            src_ref=source,
            dst_ref=out_ref.at[k],
            send_sem=send_sem.at[k],
            recv_sem=recv_sem.at[k],
            device_id=device(k),
            device_id_type=MESH_ID,
        )

    barrier = pltpu.get_barrier_semaphore()

    def greet(step, carry):
        k = lax.rem(me + step, n)
        pl.semaphore_signal(barrier, 1, device_id=device(k), device_id_type=MESH_ID)
        return carry

    lax.fori_loop(1, n, greet, 0)
    pl.semaphore_wait(barrier, n - 1)

    def send(step, carry):
        outgoing(lax.rem(me + step, n)).start()
        return carry

    lax.fori_loop(1, n, send, 0)
    out_ref[me] = src_ref[me] if spread else src_ref[...]

    def finish(step, carry):
        k = lax.rem(me + step, n)
        outgoing(k).wait_send()
        incoming(lax.rem(me + n - step, n)).wait_recv()
        return carry

    lax.fori_loop(1, n, finish, 0)


def row_partners():
    me = lax.axis_index("row")
    return me, lax.axis_index("col"), me + 1 - 2 * lax.rem(me, 2)


def row_greet(barrier, n):
    me, other, twin = row_partners()
    pl.semaphore_signal(barrier, 1, device_id=(twin, other), device_id_type=MESH_ID)

    def greet(step, carry):
        peer = lax.rem(me + 2 * step, n)
        pl.semaphore_signal(barrier, 1, device_id=(peer, other), device_id_type=MESH_ID)
        return carry

    lax.fori_loop(1, n // 2, greet, 0)
    return n // 2


def row_transfer(n, src_ref, out_ref, send_sem, pass_sem, recv_sem):
    me, other, twin = row_partners()
    half = n // 2

    def copy(source, slot, sems, k):
        return pltpu.make_async_remote_copy(
            src_ref=source,
            dst_ref=out_ref.at[slot],
            send_sem=sems.at[k],
            recv_sem=recv_sem.at[slot],
            device_id=(k, other),
            device_id_type=MESH_ID,
        )

    def peer(step):
        return lax.rem(me + 2 * step, n)

    def far(step):
        return lax.rem(twin + 2 * step, n)

    def send(step, carry):
        copy(src_ref, me, send_sem, peer(step)).start()
        return carry

    lax.fori_loop(1, half, send, 0)
    copy(src_ref, me, send_sem, twin).start()

    def relay(step, carry):
        k = peer(step)
        copy(src_ref, k, send_sem, k).wait_recv()
        copy(out_ref.at[k], k, pass_sem, twin).start()
        return carry

    lax.fori_loop(1, half, relay, 0)

    def finish(step, carry):
        k = peer(step)
        copy(src_ref, me, send_sem, k).wait_send()
        copy(out_ref.at[k], k, pass_sem, twin).wait_send()
        copy(src_ref, far(step), send_sem, twin).wait_recv()
        return carry

    lax.fori_loop(1, half, finish, 0)
    copy(src_ref, me, send_sem, twin).wait_send()
    copy(src_ref, twin, send_sem, twin).wait_recv()


def gather_kernel(n, src_ref, out_ref, send_sem, pass_sem, recv_sem):
    barrier = pltpu.get_barrier_semaphore()
    pl.semaphore_wait(barrier, row_greet(barrier, n))
    out_ref[lax.axis_index("row")] = src_ref[...]
    row_transfer(n, src_ref, out_ref, send_sem, pass_sem, recv_sem)


def gather(block, tag):
    n = lax.axis_size("row")
    vmem = pl.BlockSpec(memory_space=pltpu.VMEM)
    return pl.pallas_call(
        functools.partial(gather_kernel, n),
        out_shape=jax.ShapeDtypeStruct((n, *block.shape), block.dtype),
        in_specs=[vmem],
        out_specs=vmem,
        scratch_shapes=[pltpu.SemaphoreType.DMA((n,))] * 3,
        compiler_params=pltpu.CompilerParams(collective_id=tag, has_side_effects=True),
    )(block)


def middle_kernel(
    n_row,
    n_col,
    parts_ref,
    features_ref,
    weight_one_ref,
    bias_one_ref,
    mask_ref,
    history_ref,
    weight_two_ref,
    pushed_ref,
    out_ref,
    landing_ref,
    col_send,
    col_recv,
    send_sem,
    pass_sem,
    recv_sem,
    local_sem,
):
    row = lax.axis_index("row")
    me = lax.axis_index("col")

    def col_copy(k, slot):
        return pltpu.make_async_remote_copy(
            src_ref=parts_ref.at[k],
            dst_ref=landing_ref.at[slot],
            send_sem=col_send.at[k],
            recv_sem=col_recv.at[slot],
            device_id=(row, k),
            device_id_type=MESH_ID,
        )

    barrier = pltpu.get_barrier_semaphore()

    def greet(step, carry):
        k = lax.rem(me + step, n_col)
        pl.semaphore_signal(barrier, 1, device_id=(row, k), device_id_type=MESH_ID)
        return carry

    lax.fori_loop(1, n_col, greet, 0)
    expected = row_greet(barrier, n_row)
    pl.semaphore_wait(barrier, n_col - 1 + expected)

    def send(step, carry):
        col_copy(lax.rem(me + step, n_col), me).start()
        return carry

    lax.fori_loop(1, n_col, send, 0)
    own_copy = pltpu.make_async_copy(parts_ref.at[me], landing_ref.at[me], local_sem.at[0])
    own_copy.start()
    own_copy.wait()

    def finish(step, carry):
        col_copy(lax.rem(me + step, n_col), me).wait_send()
        col_copy(me, lax.rem(me + n_col - step, n_col)).wait_recv()
        return carry

    lax.fori_loop(1, n_col, finish, 0)
    total = features_ref[...].astype(jnp.float32)
    for k in range(n_col):
        total = total + landing_ref[k].astype(jnp.float32)
    agg = total.astype(jnp.bfloat16)
    pre = jnp.dot(agg, weight_one_ref[...], preferred_element_type=jnp.float32)
    hidden = jnp.maximum(pre + bias_one_ref[...], 0.0).astype(jnp.bfloat16)
    pushed = jnp.where(mask_ref[...] == 1, hidden, history_ref[...])
    pushed_ref[...] = pushed
    projected = lax.dot_general(
        weight_two_ref[...], pushed, (((1,), (1,)), ((), ())), preferred_element_type=jnp.float32
    )
    out_ref[row] = projected.astype(out_ref.dtype)
    row_transfer(n_row, out_ref.at[row], out_ref, send_sem, pass_sem, recv_sem)


def middle(parts, features, weight_one, bias_one, mask, history, weight_two, tag):
    n_row = lax.axis_size("row")
    n_col = lax.axis_size("col")
    classes = weight_two.shape[1]
    nodes = features.shape[0]
    vmem = pl.BlockSpec(memory_space=pltpu.VMEM)
    return pl.pallas_call(
        functools.partial(middle_kernel, n_row, n_col),
        out_shape=(
            jax.ShapeDtypeStruct(history.shape, history.dtype),
            jax.ShapeDtypeStruct((n_row, classes, nodes), jnp.bfloat16),
        ),
        in_specs=[pl.BlockSpec(memory_space=pl.ANY)] + [vmem] * 6,
        out_specs=(vmem, vmem),
        scratch_shapes=[
            pltpu.VMEM(parts.shape, parts.dtype),
            pltpu.SemaphoreType.DMA((n_col,)),
            pltpu.SemaphoreType.DMA((n_col,)),
        ]
        + [pltpu.SemaphoreType.DMA((n_row,))] * 3
        + [pltpu.SemaphoreType.DMA((1,))],
        compiler_params=pltpu.CompilerParams(collective_id=tag, has_side_effects=True),
    )(
        parts,
        features,
        weight_one,
        bias_one.reshape(1, -1),
        mask.reshape(-1, 1),
        history,
        weight_two.T,
    )


def exchange(block, axis, spread, tag):
    other_axis = "col" if axis == "row" else "row"
    n = lax.axis_size(axis)
    shape = block.shape[1:] if spread else block.shape
    vmem = pl.BlockSpec(memory_space=pltpu.VMEM)
    return pl.pallas_call(
        functools.partial(exchange_kernel, axis, other_axis, n, spread),
        out_shape=jax.ShapeDtypeStruct((n, *shape), block.dtype),
        in_specs=[vmem],
        out_specs=vmem,
        scratch_shapes=[pltpu.SemaphoreType.DMA((n,)), pltpu.SemaphoreType.DMA((n,))],
        compiler_params=pltpu.CompilerParams(collective_id=tag, has_side_effects=True),
    )(block)


def joined_along(tiles, dim):
    tiles = jnp.moveaxis(tiles, 0, dim)
    lengths = tiles.shape
    return tiles.reshape(*lengths[:dim], lengths[dim] * lengths[dim + 1], *lengths[dim + 2 :])


def copy_for_each(shard, axis):
    copies = jnp.broadcast_to(shard, (lax.axis_size(axis), *shard.shape))
    return lax.all_to_all(copies, axis, split_axis=0, concat_axis=0, tiled=True)


def collect(shard, axis, dim):
    return joined_along(copy_for_each(shard, axis), dim)


def in_blocks(shard, dim, size):
    lengths = shard.shape
    tiles = shard.reshape(*lengths[:dim], size, lengths[dim] // size, *lengths[dim + 1 :])
    return jnp.moveaxis(tiles, dim, 0)


def sent_and_summed(shard, axis, dim):
    tiles = in_blocks(shard, dim, lax.axis_size(axis))
    arrived = lax.all_to_all(tiles, axis, split_axis=0, concat_axis=0, tiled=True)
    return arrived.astype(jnp.float32).sum(axis=0)


def products_kernel(
    flipped,
    pack,
    coords_ref,
    count_ref,
    tiles_hbm,
    gathered_ref,
    out_ref,
    order_ref,
    bounds_ref,
    cursor_ref,
    tiles_ref,
    load_sem,
):
    chunks = load_sem.shape[0]
    size = tiles_ref.shape[0] // chunks
    loads = [
        pltpu.make_async_copy(
            tiles_hbm.at[pl.ds(c * size, size)], tiles_ref.at[pl.ds(c * size, size)], load_sem.at[c]
        )
        for c in range(chunks)
    ]
    for load in loads:
        load.start()
    blocks = out_ref.shape[0]
    live = count_ref[0]
    for target in range(blocks + 1):
        bounds_ref[target] = 0

    def count(slot, carry):
        target = coords_ref[2 * slot]
        bounds_ref[target + 1] = bounds_ref[target + 1] + 1
        return carry

    lax.fori_loop(0, live, count, 0)
    for target in range(blocks):
        bounds_ref[target + 1] = bounds_ref[target + 1] + bounds_ref[target]
        cursor_ref[target] = bounds_ref[target]

    def place(slot, carry):
        target = coords_ref[2 * slot]
        position = cursor_ref[target]
        order_ref[position] = slot
        cursor_ref[target] = position + 1
        return carry

    lax.fori_loop(0, live, place, 0)
    for load in loads:
        load.wait()

    def product(first, end, total):
        tiles, sources = [], []
        for offset in range(pack):
            slot = order_ref[jnp.minimum(first + offset, end - 1)]
            tile = tiles_ref[slot]
            tiles.append(jnp.where(first + offset < end, tile, jnp.zeros_like(tile)))
            sources.append(gathered_ref[coords_ref[2 * slot + 1]])
        if flipped:
            return total + lax.dot_general(
                jnp.concatenate(sources, axis=1),
                jnp.concatenate(tiles, axis=1),
                (((1,), (1,)), ((), ())),
                preferred_element_type=jnp.float32,
            )
        return total + jnp.dot(
            jnp.concatenate(tiles, axis=1),
            jnp.concatenate(sources, axis=0),
            preferred_element_type=jnp.float32,
        )

    for target in range(blocks):
        first, end = bounds_ref[target], bounds_ref[target + 1]
        total = lax.fori_loop(
            0,
            (end - first + pack - 1) // pack,
            lambda step, total: product(first + step * pack, end, total),
            jnp.zeros(out_ref.shape[1:], jnp.float32),
        )
        out_ref[target] = total.astype(out_ref.dtype)


def tile_products(gathered, tiles, coords, live_total, flipped=False, pack=8):
    row_blocks = lax.axis_size("col")
    slots = tiles.shape[0]
    block_shape = gathered.shape[1:]
    vmem = pl.BlockSpec(memory_space=pltpu.VMEM)
    smem = pl.BlockSpec(memory_space=pltpu.SMEM)
    return pl.pallas_call(
        functools.partial(products_kernel, flipped, pack),
        in_specs=[smem, smem, pl.BlockSpec(memory_space=pl.ANY), vmem],
        out_specs=vmem,
        out_shape=jax.ShapeDtypeStruct((row_blocks, *block_shape), jnp.bfloat16),
        scratch_shapes=[
            pltpu.SMEM((slots,), jnp.int32),
            pltpu.SMEM((row_blocks + 1,), jnp.int32),
            pltpu.SMEM((row_blocks,), jnp.int32),
            pltpu.VMEM(tiles.shape, tiles.dtype),
            pltpu.SemaphoreType.DMA((8,)),
        ],
    )(coords.reshape(-1), live_total.reshape(1), tiles, gathered)


def on_device(
    features,
    tiles,
    tile_coords,
    tile_count,
    batch_mask,
    history,
    weight_one,
    bias_one,
    weight_two,
    bias_two,
):
    tile_set = tiles[0, 0]
    coord_set = tile_coords[0, 0]
    live_total = tile_count[0, 0]
    gathered_input = gather(features[0, 0], 0)
    summed_one = tile_products(gathered_input, tile_set, coord_set, live_total)
    pushed, gathered_proj = middle(
        summed_one,
        features[0, 0],
        weight_one,
        bias_one,
        batch_mask[0, 0],
        history[0, 0],
        weight_two,
        1,
    )
    summed_two = tile_products(gathered_proj, tile_set, coord_set, live_total, True)
    owned_two = exchange(summed_two, "col", True, 3).astype(jnp.float32).sum(axis=0)
    own_block = gathered_proj[lax.axis_index("row")].astype(jnp.float32)
    scores = (own_block + owned_two).T + bias_two
    return (pushed[None, None], scores[None, None])


def solution(mesh):
    return jax.shard_map(
        on_device,
        mesh=mesh,
        in_specs=(
            P("row", "col", None, None),
            P("row", "col", None, None, None),
            P("row", "col", None, None),
            P("row", "col"),
            P("row", "col", None),
            P("row", "col", None, None),
            P(),
            P(),
            P(),
            P(),
        ),
        out_specs=(P("row", "col", None, None), P("row", "col", None, None)),
        check_vma=False,
    )
```
